128 devices in a mesh: gx: 16 (over y_lo, x, core), gy: 8 (over z, y_hi).
Axes of the slice: x: 4, y: 4 (y_hi: 2, y_lo: 2; y = y_hi * 2 + y_lo), z: 4, core: 2. Of those that a mesh axis runs over, the one named last changes fastest.
Arguments:
- previous: float32 [256, 256, 2048], P('gx', 'gy'), may hold values from -1.8 to 1.8
- source: float32 [256, 256, 2048], P('gx', 'gy'), may hold values from -5 to 5
- conductivity: float32 [256, 256, 2048], P('gx', 'gy'), may hold values from 0.24 to 8.1
Outputs:
- correction: float32 [256, 256, 2048], P('gx', 'gy')
The draws below stay inside these ranges and needn't reach their ends.
All inputs are finite; a program needn't handle non-finite values.
Results may differ from the reference program's by a relative error of at most 0.000068.
Values sent between devices are 32-bit elements; how exact they have to be, the bound alone decides.
No kernel may reach another device: no remote copies, remote signals or barrier semaphores. Data moves between devices by JAX's collectives and lax.ppermute only.
A program may use at most 320 MiB of HBM per device.

```python
import math
import jax
import jax.numpy as jnp
from jax import lax

F = 16
CSWEEPS = 32
NX = 256
NY = 256
NZ = 2048


def draw_source(key, part):
    rough_key = jax.random.fold_in(key, 11)
    wave_key = jax.random.fold_in(key, 12)
    phase_key = jax.random.fold_in(key, 13)
    block_key = jax.random.fold_in(key, 14)
    rough_part = jnp.clip(jax.random.normal(rough_key, (NX, NY, NZ), jnp.float32), -3.0, 3.0)
    block_values = jax.random.uniform(block_key, (NX // F, NY // F, NZ // F), jnp.float32, -1.2, 1.2)
    block_part = jnp.broadcast_to(block_values[:, None, :, None, :, None], (NX // F, F, NY // F, F, NZ // F, F)).reshape(NX, NY, NZ)
    waves = jax.random.randint(wave_key, (3,), 1, 3).astype(jnp.float32)
    phase_value = jax.random.uniform(phase_key, (), jnp.float32, -math.pi, math.pi)
    plane_pos = jnp.arange(NX, dtype=jnp.float32)[:, None, None] / NX
    row_pos = jnp.arange(NY, dtype=jnp.float32)[None, :, None] / NY
    col_pos = jnp.arange(NZ, dtype=jnp.float32)[None, None, :] / NZ
    angle_value = 2.0 * math.pi * (waves[0] * plane_pos + waves[1] * row_pos + waves[2] * col_pos) + phase_value
    smooth_part = 0.6 * jnp.cos(angle_value)
    return (rough_part + block_part + smooth_part).astype(jnp.float32)


def draw_conductivity(key, part):
    cell_key = jax.random.fold_in(key, 21)
    phase_key = jax.random.fold_in(key, 22)
    cell_part = jnp.exp(jax.random.uniform(cell_key, (NX, NY, NZ), jnp.float32, math.log(0.5), math.log(4.0)))
    phase_value = jax.random.uniform(phase_key, (), jnp.float32, -math.pi, math.pi)
    plane_pos = jnp.arange(NX, dtype=jnp.float32)[:, None, None] / NX
    row_pos = jnp.arange(NY, dtype=jnp.float32)[None, :, None] / NY
    smooth_part = jnp.exp(0.7 * jnp.cos(2.0 * math.pi * (plane_pos + row_pos) + phase_value))
    return (cell_part * smooth_part).astype(jnp.float32)


def levels(rng, shape, cuts, low, top_value):
    def one(dim, blocks):
        heights = jax.random.uniform(jax.random.fold_in(jax.random.fold_in(rng, 6), dim), (blocks,), jnp.float32, low / len(cuts), top_value / len(cuts))
        return jnp.repeat(jnp.exp(heights), shape[dim] // blocks).reshape((-1,) + (1,) * (len(shape) - dim - 1))

    level = one(*cuts[0])
    for cut in cuts[1:]:
        level = level * one(*cut)
    return level


def noise(key, shape, scale, bound, shards=(), kind=jnp.bfloat16):
    array = jax.random.normal(key, shape, jnp.float32) * scale
    if len(shards) > 0:
        array = levels(key, shape, shards, -0.22, 0.18) * array
    return jnp.clip(array, min=-bound, max=bound).astype(kind)


def setup_inputs(seed: int = 0) -> dict:
    arg_keys = jax.random.split(jax.random.key(seed), 4)
    return {
        "previous": noise(arg_keys[0], (NX, NY, NZ), 0.3, 1.8, ((0, 16), (1, 8)), jnp.float32),
        "source": draw_source(jax.random.fold_in(arg_keys[3], 71), 0),
        "conductivity": draw_conductivity(jax.random.fold_in(arg_keys[3], 71), 0),
    }


reaction = 0.2
damping = 0.8
coarse_factor = 0.25


def beside_all(values):
    return [jnp.roll(values, -1, 0), jnp.roll(values, 1, 0), jnp.roll(values, -1, 1), jnp.roll(values, 1, 1), jnp.roll(values, 1, 2), jnp.roll(values, -1, 2)]


def diagonal(conduct, factor):
    summed = jnp.full_like(conduct, reaction)
    for beside in beside_all(conduct):
        summed = summed + (0.5 * factor) * (conduct + beside)
    return summed


def operate(field, conduct, factor):
    result = reaction * field
    for near_field, near_cond in zip(beside_all(field), beside_all(conduct)):
        result = result + ((0.5 * factor) * (conduct + near_cond)) * (field - near_field)
    return result


def restrict(values):
    planes, rows_count, cols_count = values.shape
    return values.reshape(planes // F, F, rows_count // F, F, cols_count // F, F).mean(axis=(1, 3, 5))


def interp_matrix(coarse_count):
    fine_index = jnp.arange(coarse_count * F, dtype=jnp.int32)
    base_index = fine_index // F + 1
    offset = ((fine_index % F).astype(jnp.float32) + 0.5) / F - 0.5
    side_index = jnp.where(offset > 0, base_index + 1, base_index - 1)
    row_index = jnp.arange(coarse_count + 2, dtype=jnp.int32)[:, None]
    weight = jnp.abs(offset)
    first_part = jnp.where(row_index == base_index[None, :], 1.0 - weight, 0.0 * weight)
    return first_part + jnp.where(row_index == side_index[None, :], weight, 0.0 * weight)


def reference(previous, source, conductivity):
    diag_fine = diagonal(conductivity, 1.0)
    residual = source - operate(previous, conductivity, 1.0)
    fine_corr = damping * residual / diag_fine
    for repeat in range(2):
        fine_corr = fine_corr + damping * (residual - operate(fine_corr, conductivity, 1.0)) / diag_fine
    coarse_resid = restrict(residual)
    coarse_cond = restrict(conductivity)
    factor = coarse_factor
    diag_coarse = diagonal(coarse_cond, factor)
    coarse_corr = damping * coarse_resid / diag_coarse
    for repeat in range(CSWEEPS - 1):
        coarse_corr = coarse_corr + damping * (coarse_resid - operate(coarse_corr, coarse_cond, factor)) / diag_coarse
    padded = jnp.pad(coarse_corr, 1, mode="wrap")
    along_cols = jnp.einsum("abc,cz->abz", padded, interp_matrix(coarse_corr.shape[2]), precision=lax.Precision.HIGHEST)
    along_rows = jnp.einsum("abz,by->ayz", along_cols, interp_matrix(coarse_corr.shape[1]), precision=lax.Precision.HIGHEST)
    interpolated = jnp.einsum("ayz,ax->xyz", along_rows, interp_matrix(coarse_corr.shape[0]), precision=lax.Precision.HIGHEST)
    return fine_corr + interpolated
```

```python
import functools
import jax
import jax.numpy as jnp
from jax import lax
from jax.experimental import pallas as pl
from jax.experimental.pallas import tpu as pltpu
from jax.sharding import PartitionSpec as P

F = 16
CSWEEPS = 32
REACTION = 0.2
DAMPING = 0.8
COARSE_FACTOR = 0.25
F32 = jnp.float32
BF16 = jnp.bfloat16
STRIP = 8

VM = pl.BlockSpec(memory_space=pltpu.VMEM)
SM = pl.BlockSpec(memory_space=pltpu.SMEM)
ANY = pl.BlockSpec(memory_space=pl.ANY)


def params(mib):
    return pltpu.CompilerParams(vmem_limit_bytes=mib * 1024 * 1024)


def cost(flops, nbytes):
    return pl.CostEstimate(flops=int(flops), bytes_accessed=int(nbytes), transcendentals=0)


def sds(*shape):
    return jax.ShapeDtypeStruct(shape, F32)


def zp(a):
    return pltpu.roll(a, a.shape[-1] - 1, a.ndim - 1)


def zm(a):
    return pltpu.roll(a, 1, a.ndim - 1)


def beside_rows(ref, x, r, rows, value):
    low, high = r * STRIP, (r + 1) * STRIP
    up = ref[x, low + 1 : high + 1, :] if high < rows else pltpu.roll(value, STRIP - 1, 0)
    down = ref[x, low - 1 : high - 1, :] if low > 0 else pltpu.roll(value, 1, 0)
    return up, down


def row_halves(r, rows, cols):
    sub = lax.broadcasted_iota(jnp.int32, (STRIP, cols), 0)
    up = jnp.where(sub == STRIP - 1, 0.0, 0.5).astype(F32) if (r + 1) * STRIP == rows else 0.5
    down = jnp.where(sub == 0, 0.0, 0.5).astype(F32) if r == 0 else 0.5
    return up, down


def couplings(k, x, planes, r, rows):
    k0 = k[x, r * STRIP : (r + 1) * STRIP, :]
    up, down = beside_rows(k, x, r, rows, k0)
    h_up, h_down = row_halves(r, rows, k0.shape[-1])
    h_next = jnp.where(x < planes - 1, 0.5, 0.0).astype(F32)
    h_prev = jnp.where(x > 0, 0.5, 0.0).astype(F32)
    xn, xp = jnp.minimum(x + 1, planes - 1), jnp.maximum(x - 1, 0)
    c_next = h_next * (k0 + k[xn, r * STRIP : (r + 1) * STRIP, :])
    c_prev = h_prev * (k0 + k[xp, r * STRIP : (r + 1) * STRIP, :])
    c_up = h_up * (k0 + up)
    c_down = h_down * (k0 + down)
    c_z = 0.5 * (k0 + zp(k0))
    return k0, xn, xp, c_next, c_prev, c_up, c_down, c_z


def inner_kernel(v, s, k, w_ref, f_ref, dpl, rpl, drow, rrow, sums):
    planes, rows, cols = v.shape
    sums[...] = jnp.zeros_like(sums)

    def plane(x, carry):
        for r in range(rows // STRIP):
            sl = slice(r * STRIP, (r + 1) * STRIP)
            k0, xn, xp, c_next, c_prev, c_up, c_down, c_z = couplings(k, x, planes, r, rows)
            v0 = v[x, sl, :]
            v_up, v_down = beside_rows(v, x, r, rows, v0)
            f_z = c_z * (v0 - zp(v0))
            diag = REACTION + c_next + c_prev + c_up + c_down + c_z + zm(c_z)
            res = (
                s[x, sl, :]
                - REACTION * v0
                - c_next * (v0 - v[xn, sl, :])
                - c_prev * (v0 - v[xp, sl, :])
                - c_up * (v0 - v_up)
                - c_down * (v0 - v_down)
                - f_z
                + zm(f_z)
            )
            w = DAMPING / diag
            w_ref[x, sl, :] = w
            f_ref[x, sl, :] = w * res
            half = r * STRIP // F
            sums[half * STRIP : (half + 1) * STRIP, :] += res
            sums[(2 + half) * STRIP : (3 + half) * STRIP, :] += k0
            if r == 0:
                drow[0, pl.ds(x, 1), :] = diag[0:1]
                rrow[0, pl.ds(x, 1), :] = res[0:1]
            if (r + 1) * STRIP == rows:
                drow[1, pl.ds(x, 1), :] = diag[STRIP - 1 :]
                rrow[1, pl.ds(x, 1), :] = res[STRIP - 1 :]

            @pl.when((x == 0) | (x == planes - 1))
            def _():
                side = jnp.where(x == 0, 0, 1)
                dpl[side, sl, :] = diag
                rpl[side, sl, :] = res

        return carry

    lax.fori_loop(0, planes, plane, 0)


def cross(gpl, grow, pl_ref, row_ref, sign):
    rows, planes = gpl.shape[1], grow.shape[1]
    pl_ref[...] = pl_ref[...] + sign * gpl[...]
    row_ref[...] = row_ref[...] + sign * grow[...]
    for a, x in ((0, 0), (1, planes - 1)):
        for b, y in ((0, 0), (1, rows - 1)):
            pl_ref[a, y : y + 1, :] = pl_ref[a, y : y + 1, :] + sign * grow[b, x : x + 1, :]
            row_ref[b, x : x + 1, :] = row_ref[b, x : x + 1, :] + sign * gpl[a, y : y + 1, :]


def split3(a):
    one = a.astype(BF16)
    rest = a - one.astype(F32)
    two = rest.astype(BF16)
    three = (rest - two.astype(F32)).astype(BF16)
    return jnp.concatenate([one, two, three], 0)


def joined3(a):
    n = a.shape[0] // 3
    return a[:n] + a[n : 2 * n] + a[2 * n :]


def edge_kernel(
    dpl, rpl, drow, rrow, pl_lo, pl_hi, rw_lo, rw_hi, xl, xh, yl, yh, sums,
    f_pl, f_row, w_pl, w_row, wc_pl, wc_row, payload,
    c_pl, c_row, q_pl, q_row,
):
    cols = dpl.shape[2]
    rows = dpl.shape[1]
    for side, mine, other in ((0, pl_lo, xl), (1, pl_hi, xh)):
        c_pl[side] = 0.5 * (mine[1] + other[1])
        q_pl[side] = c_pl[side] * (mine[0] - other[0])
    for side, mine, other in ((0, rw_lo, yl), (1, rw_hi, yh)):
        c_row[side] = 0.5 * (mine[1] + other[1])
        q_row[side] = c_row[side] * (mine[0] - other[0])
    w_pl[...] = dpl[...]
    w_row[...] = drow[...]
    cross(c_pl, c_row, w_pl, w_row, 1.0)
    f_pl[...] = rpl[...]
    f_row[...] = rrow[...]
    cross(q_pl, q_row, f_pl, f_row, -1.0)
    w_pl[...] = DAMPING / w_pl[...]
    w_row[...] = DAMPING / w_row[...]
    f_pl[...] = f_pl[...] * w_pl[...]
    f_row[...] = f_row[...] * w_row[...]
    wc_pl[...] = w_pl[...] * c_pl[...]
    wc_row[...] = w_row[...] * c_row[...]
    parts = []
    for half in range(rows // F):
        total = sums[half * STRIP : (half + 1) * STRIP, :]
        for side in range(2):
            for r in range(half * F // STRIP, (half + 1) * F // STRIP):
                total = total - q_pl[side, r * STRIP : (r + 1) * STRIP, :]
        if half == 0:
            for r in range(q_row.shape[1] // STRIP):
                total = total - q_row[0, r * STRIP : (r + 1) * STRIP, :]
        if half == rows // F - 1:
            for r in range(q_row.shape[1] // STRIP):
                total = total - q_row[1, r * STRIP : (r + 1) * STRIP, :]
        parts.append(total)
    parts.append(sums[2 * STRIP :, :])
    col = lax.broadcasted_iota(jnp.int32, (cols, cols // F), 0)
    cell = lax.broadcasted_iota(jnp.int32, (cols, cols // F), 1)
    gather = jnp.where(col // F == cell, 1.0, 0.0).astype(BF16)
    reduced = joined3(
        jnp.dot(split3(jnp.concatenate(parts, 0)), gather, preferred_element_type=F32)
    )
    means = [
        jnp.sum(reduced[i * STRIP : (i + 1) * STRIP], axis=0, keepdims=True) * (1.0 / F**3)
        for i in range(4)
    ]
    tile = jnp.concatenate(means + means, 0)
    for i in range(payload.shape[0] // STRIP):
        payload[i * STRIP : (i + 1) * STRIP, :] = tile


def put_edges(ref, e_pl, e_row):
    planes, rows, _ = ref.shape
    for x in range(planes):
        ref[x, 0:1, :] = e_row[0, x : x + 1, :]
        ref[x, rows - 1 : rows, :] = e_row[1, x : x + 1, :]
    ref[0] = e_pl[0]
    ref[planes - 1] = e_pl[1]


def neighbour_sum(k, u, x, planes, r, rows):
    sl = slice(r * STRIP, (r + 1) * STRIP)
    k0, xn, xp, c_next, c_prev, c_up, c_down, c_z = couplings(k, x, planes, r, rows)
    u0 = u[x, sl, :]
    u_up, u_down = beside_rows(u, x, r, rows, u0)
    total = (
        c_next * u[xn, sl, :]
        + c_prev * u[xp, sl, :]
        + c_up * u_up
        + c_down * u_down
        + c_z * zp(u0)
        + zm(c_z * u0)
    )
    return u0, total


def sweep_kernel(k, w, f, w_pl, w_row, f_pl, f_row, g_ref, g_pl, g_row):
    planes, rows, cols = k.shape
    put_edges(w, w_pl, w_row)
    put_edges(f, f_pl, f_row)

    def plane(x, carry):
        for r in range(rows // STRIP):
            sl = slice(r * STRIP, (r + 1) * STRIP)
            u0, total = neighbour_sum(k, f, x, planes, r, rows)
            new = (2.0 - DAMPING) * u0 + w[x, sl, :] * total
            g_ref[x, sl, :] = new
            if r == 0:
                g_row[0, pl.ds(x, 1), :] = new[0:1]
            if (r + 1) * STRIP == rows:
                g_row[1, pl.ds(x, 1), :] = new[STRIP - 1 :]
        return carry

    lax.fori_loop(0, planes, plane, 0)
    g_pl[0] = g_ref[0]
    g_pl[1] = g_ref[planes - 1]


def mid_kernel(g_pl, g_row, wc_pl, wc_row, xl, xh, yl, yh, o_pl, o_row, q_pl, q_row):
    for side, other in ((0, xl), (1, xh)):
        q_pl[side] = wc_pl[side] * other[...]
    for side, other in ((0, yl), (1, yh)):
        q_row[side] = wc_row[side] * other[...]
    o_pl[...] = g_pl[...]
    o_row[...] = g_row[...]
    cross(q_pl, q_row, o_pl, o_row, 1.0)


def last_kernel(k, w, f, g, interp, w_pl, w_row, f_pl, f_row, g_pl, g_row, out):
    planes, rows, cols = k.shape
    put_edges(w, w_pl, w_row)
    put_edges(f, f_pl, f_row)
    put_edges(g, g_pl, g_row)

    def plane(x, carry):
        offset = ((x % F).astype(F32) + 0.5) / F - 0.5
        weight = jnp.abs(offset)
        side = jnp.where(offset > 0, 2, 0)
        for r in range(rows // STRIP):
            sl = slice(r * STRIP, (r + 1) * STRIP)
            u0, total = neighbour_sum(k, g, x, planes, r, rows)
            coarse = (1.0 - weight) * interp[1, sl, :] + weight * interp[side, sl, :]
            new = f[x, sl, :] + (1.0 - DAMPING) * u0 + w[x, sl, :] * total
            out[x, sl, :] = new + coarse
        return carry

    lax.fori_loop(0, planes, plane, 0)


def finish_kernel(src, wc_pl, wc_row, xl, xh, yl, yh, out, b_pl, b_lo, b_hi, sems):
    planes, rows, _ = out.shape
    spots = (
        (out.at[0], b_pl.at[0]),
        (out.at[planes - 1], b_pl.at[1]),
        (out.at[1 : planes - 1, 0:STRIP, :], b_lo),
        (out.at[1 : planes - 1, rows - STRIP : rows, :], b_hi),
    )
    reads = [pltpu.make_async_copy(o, b, sems.at[i]) for i, (o, b) in enumerate(spots)]
    for c in reads:
        c.start()
    for c in reads:
        c.wait()
    for side, other in ((0, xl), (1, xh)):
        x = side * (planes - 1)
        b_pl[side] = b_pl[side] + wc_pl[side] * other[...]
        b_pl[side, 0:1, :] = b_pl[side, 0:1, :] + wc_row[0, x : x + 1, :] * yl[x : x + 1, :]
        b_pl[side, rows - 1 : rows, :] = (
            b_pl[side, rows - 1 : rows, :] + wc_row[1, x : x + 1, :] * yh[x : x + 1, :]
        )
    for x in range(1, planes - 1):
        b_lo[x - 1, 0:1, :] = b_lo[x - 1, 0:1, :] + wc_row[0, x : x + 1, :] * yl[x : x + 1, :]
        b_hi[x - 1, STRIP - 1 :, :] = (
            b_hi[x - 1, STRIP - 1 :, :] + wc_row[1, x : x + 1, :] * yh[x : x + 1, :]
        )
    writes = [pltpu.make_async_copy(b, o, sems.at[i]) for i, (o, b) in enumerate(spots)]
    for c in writes:
        c.start()
    for c in writes:
        c.wait()


def coarse_kernel(place, got, interp, coef, b_ref, u_ref, *, nx, ny, rows):
    nz = got.shape[1]
    per = 2 * 2

    def field(start):
        return [
            jnp.stack([got[pl.ds(p * ny * per + start + t, ny, stride=per), :] for p in range(nx)], 0)
            for t in range(2)
        ]

    resid, cond = field(0), field(2)

    def beside(a, t):
        mine = a[t]
        nxt = jnp.concatenate([mine[1:], mine[:1]], 0)
        prv = jnp.concatenate([mine[-1:], mine[:-1]], 0)
        up = a[1] if t == 0 else pltpu.roll(a[0], ny - 1, 1)
        down = a[0] if t == 1 else pltpu.roll(a[1], 1, 1)
        return nxt, prv, up, down, pltpu.roll(mine, 1, 2), pltpu.roll(mine, nz - 1, 2)

    for t in range(2):
        cs = [(0.5 * COARSE_FACTOR) * (cond[t] + other) for other in beside(cond, t)]
        diag = REACTION
        for c in cs:
            diag = diag + c
        inv = DAMPING / diag
        for i, c in enumerate(cs):
            coef[i, t] = inv * c
        b_ref[t] = inv * resid[t]
        u_ref[0, t] = b_ref[t]

    def sweep(src, dst):
        for p in range(nx):
            pn, pp = (p + 1) % nx, (p - 1) % nx
            u = [u_ref[src, t, p] for t in range(2)]
            for t in range(2):
                up = u[1] if t == 0 else pltpu.roll(u[0], ny - 1, 0)
                down = u[0] if t == 1 else pltpu.roll(u[1], 1, 0)
                a = b_ref[t, p] + (1.0 - DAMPING) * u[t]
                a = a + coef[0, t, p] * u_ref[src, t, pn]
                a = a + coef[1, t, p] * u_ref[src, t, pp]
                c = coef[2, t, p] * up + coef[3, t, p] * down
                c = c + coef[4, t, p] * pltpu.roll(u[t], 1, 1)
                c = c + coef[5, t, p] * pltpu.roll(u[t], nz - 1, 1)
                u_ref[dst, t, p] = a + c

    def pair(i, carry):
        sweep(0, 1)
        sweep(1, 0)
        return carry

    steps = CSWEEPS - 1
    lax.fori_loop(0, steps // 2, pair, 0)
    last = 0
    if steps % 2:
        sweep(0, 1)
        last = 1

    gx, gy = place[0], place[1]
    lines = []
    for d in (-1, 0, 1):
        p = lax.rem(gx + d + nx, nx)
        prev_s, next_s = lax.rem(gy + ny - 1, ny), lax.rem(gy + 1, ny)
        for t, s in ((1, prev_s), (0, gy), (1, gy), (0, next_s)):
            lines.append(u_ref[last, t, p, pl.ds(s, 1), :])
    lines = jnp.concatenate(lines + lines[:4], 0)
    cols = nz * F
    cell = lax.broadcasted_iota(jnp.int32, (nz, cols), 0)
    col = lax.broadcasted_iota(jnp.int32, (nz, cols), 1)
    base = col // F
    offset = ((col % F).astype(F32) + 0.5) / F - 0.5
    side = jnp.where(offset > 0, base + 1, base - 1)
    side = jnp.where(side < 0, side + nz, jnp.where(side >= nz, side - nz, side))
    weight = jnp.abs(offset)
    matrix = jnp.where(cell == base, 1.0 - weight, 0.0) + jnp.where(cell == side, weight, 0.0)
    wide = joined3(jnp.dot(split3(lines), matrix.astype(BF16), preferred_element_type=F32))
    sub = lax.broadcasted_iota(jnp.int32, (STRIP, cols), 0)
    for plane in range(3):
        for r in range(rows // STRIP):
            row = r * STRIP + sub
            off = ((row % F).astype(F32) + 0.5) / F - 0.5
            wt = jnp.abs(off)
            block = r * STRIP // F
            near = block + 1
            far = near + (1 if (r * STRIP) % F >= F // 2 else -1)
            a = wide[plane * 4 + near : plane * 4 + near + 1]
            c = wide[plane * 4 + far : plane * 4 + far + 1]
            interp[plane, r * STRIP : (r + 1) * STRIP, :] = (1.0 - wt) * a + wt * c


def swap(axis, low, high):
    count = lax.axis_size(axis)
    forward = [(i, (i + 1) % count) for i in range(count)]
    backward = [(i, (i - 1) % count) for i in range(count)]
    return lax.ppermute(high, axis, forward), lax.ppermute(low, axis, backward)


def per_device(nx, ny, v, s, k):
    planes, rows, cols = v.shape
    n = planes * rows * cols
    vm = pltpu.VMEM
    rw_lo = jnp.stack([v[:, 0], k[:, 0]])
    rw_hi = jnp.stack([v[:, rows - 1], k[:, rows - 1]])
    yl, yh = swap("gy", rw_lo, rw_hi)
    pl_lo = jnp.stack([v[0], k[0]])
    pl_hi = jnp.stack([v[planes - 1], k[planes - 1]])
    xl, xh = swap("gx", pl_lo, pl_hi)

    full, e_pl, e_row = sds(planes, rows, cols), sds(2, rows, cols), sds(2, planes, cols)
    w, f, dpl, rpl, drow, rrow, sums = pl.pallas_call(
        inner_kernel,
        out_shape=(full, full, e_pl, e_pl, e_row, e_row, sds(4 * STRIP, cols)),
        in_specs=[VM] * 3,
        out_specs=(VM,) * 7,
        compiler_params=params(40),
        cost_estimate=cost(50 * n, 20 * n),
        name="inner",
    )(v, s, k)

    devices = nx * ny
    f_pl, f_row, w_pl, w_row, wc_pl, wc_row, payload = pl.pallas_call(
        edge_kernel,
        out_shape=(e_pl, e_row, e_pl, e_row, e_pl, e_row, sds(devices * 4, cols // F)),
        in_specs=[VM] * 13,
        out_specs=(VM,) * 7,
        scratch_shapes=[vm(e.shape, F32) for e in (e_pl, e_row, e_pl, e_row)],
        compiler_params=params(32),
        cost_estimate=cost(10 * n // 8, n),
        name="edge",
    )(dpl, rpl, drow, rrow, pl_lo, pl_hi, rw_lo, rw_hi, xl, xh, yl, yh, sums)

    fyl, fyh = swap("gy", f_row[0], f_row[1])
    fxl, fxh = swap("gx", f_pl[0], f_pl[1])
    got = lax.all_to_all(payload, ("gx", "gy"), 0, 0, tiled=True)

    g, g_pl, g_row = pl.pallas_call(
        sweep_kernel,
        out_shape=(full, e_pl, e_row),
        in_specs=[VM] * 7,
        out_specs=(VM,) * 3,
        compiler_params=params(40),
        cost_estimate=cost(40 * n, 16 * n),
        name="sweep",
    )(k, w, f, w_pl, w_row, f_pl, f_row)

    h_pl, h_row = pl.pallas_call(
        mid_kernel,
        out_shape=(e_pl, e_row),
        in_specs=[VM] * 8,
        out_specs=(VM,) * 2,
        scratch_shapes=[vm(e_pl.shape, F32), vm(e_row.shape, F32)],
        compiler_params=params(24),
        cost_estimate=cost(n // 8, n // 2),
        name="mid",
    )(g_pl, g_row, wc_pl, wc_row, fxl, fxh, fyl, fyh)

    gyl, gyh = swap("gy", h_row[0], h_row[1])
    gxl, gxh = swap("gx", h_pl[0], h_pl[1])

    place = jnp.stack([lax.axis_index("gx"), lax.axis_index("gy")]).astype(jnp.int32)
    cells = (nx, ny, cols // F)
    interp = pl.pallas_call(
        functools.partial(coarse_kernel, nx=nx, ny=ny, rows=rows),
        out_shape=sds(3, rows, cols),
        in_specs=[SM, VM],
        out_specs=VM,
        scratch_shapes=[
            vm((6, 2) + cells, F32),
            vm((2,) + cells, F32),
            vm((2, 2) + cells, F32),
        ],
        compiler_params=params(24),
        cost_estimate=cost(20 * n, n),
        name="coarse",
    )(place, got)

    out = pl.pallas_call(
        last_kernel,
        out_shape=full,
        in_specs=[VM] * 11,
        out_specs=VM,
        compiler_params=params(44),
        cost_estimate=cost(40 * n, 20 * n),
        name="last",
    )(k, w, f, g, interp, w_pl, w_row, f_pl, f_row, h_pl, h_row)

    return pl.pallas_call(
        finish_kernel,
        out_shape=full,
        in_specs=[ANY] + [VM] * 6,
        out_specs=ANY,
        scratch_shapes=[
            vm((2, rows, cols), F32),
            vm((planes - 2, STRIP, cols), F32),
            vm((planes - 2, STRIP, cols), F32),
            pltpu.SemaphoreType.DMA((4,)),
        ],
        input_output_aliases={0: 0},
        compiler_params=params(24),
        cost_estimate=cost(n // 4, 6 * n),
        name="finish",
    )(out, wc_pl, wc_row, gxl, gxh, gyl, gyh)


def solution(mesh):
    placed = P("gx", "gy", None)
    body = functools.partial(per_device, mesh.shape["gx"], mesh.shape["gy"])
    return jax.shard_map(
        body, mesh=mesh, in_specs=(placed,) * 3, out_specs=placed, check_vma=False
    )
```

```python
import functools
import jax
import jax.numpy as jnp
from jax import lax
from jax.experimental import pallas as pl
from jax.experimental.pallas import tpu as pltpu
from jax.sharding import PartitionSpec as P

F = 16
CSWEEPS = 32
REACTION = 0.2
DAMPING = 0.8
COARSE_FACTOR = 0.25
F32 = jnp.float32
BF16 = jnp.bfloat16
STRIP = 8

VM = pl.BlockSpec(memory_space=pltpu.VMEM)
SM = pl.BlockSpec(memory_space=pltpu.SMEM)
ANY = pl.BlockSpec(memory_space=pl.ANY)


def params(mib):
    return pltpu.CompilerParams(vmem_limit_bytes=mib * 1024 * 1024)


def cost(flops, nbytes):
    return pl.CostEstimate(flops=int(flops), bytes_accessed=int(nbytes), transcendentals=0)


def sds(*shape):
    return jax.ShapeDtypeStruct(shape, F32)


def zp(a):
    return pltpu.roll(a, a.shape[-1] - 1, a.ndim - 1)


def zm(a):
    return pltpu.roll(a, 1, a.ndim - 1)


def shifted_up(rolled, r):
    nxt = rolled[min(r + 1, len(rolled) - 1)]
    sub = lax.broadcasted_iota(jnp.int32, nxt.shape, 0)
    return jnp.where(sub == STRIP - 1, nxt, rolled[r])


def shifted_down(rolled, r):
    prv = rolled[r - 1]
    sub = lax.broadcasted_iota(jnp.int32, prv.shape, 0)
    return jnp.where(sub == 0, prv, rolled[r])


def strips(rows):
    return [slice(r * STRIP, (r + 1) * STRIP) for r in range(rows // STRIP)]


def ends_kernel(v, k, rw_lo, rw_hi, pl_lo, pl_hi, sems):
    planes, rows, _ = v.shape
    copies = []
    for i, a in enumerate((v, k)):
        for j, (src, dst) in enumerate(
            (
                (a.at[:, 0, :], rw_lo.at[i]),
                (a.at[:, rows - 1, :], rw_hi.at[i]),
                (a.at[0], pl_lo.at[i]),
                (a.at[planes - 1], pl_hi.at[i]),
            )
        ):
            copies.append(pltpu.make_async_copy(src, dst, sems.at[i, j]))
    for c in copies:
        c.start()
    for c in copies:
        c.wait()


def inner_kernel(
    v_hbm, s_hbm, k_hbm,
    w_ref, f_ref, cx, cy, cz, d_lo, d_hi, r_lo, r_hi, drow, rrow, sums,
    v, s, k, fx, sems,
):
    planes, rows, cols = v.shape
    sl = strips(rows)
    n = len(sl)

    def copy(i, x):
        src, dst = ((k_hbm, k), (v_hbm, v), (s_hbm, s))[i]
        return pltpu.make_async_copy(src.at[x], dst.at[x], sems.at[i, x])

    for x in range(planes):
        for i in range(3):
            copy(i, x).start()
    sums[...] = jnp.zeros_like(sums)
    fx[...] = jnp.zeros_like(fx)
    cx[0] = jnp.zeros_like(fx)
    copy(0, 0).wait()
    copy(1, 0).wait()

    def plane(x, carry):
        @pl.when(x < planes - 1)
        def _():
            copy(0, x + 1).wait()
            copy(1, x + 1).wait()

        copy(2, x).wait()
        xn = jnp.minimum(x + 1, planes - 1)
        h_next = jnp.where(x < planes - 1, 0.5, 0.0).astype(F32)
        k0 = [k[x, a, :] for a in sl]
        v0 = [v[x, a, :] for a in sl]
        k_up = [pltpu.roll(a, STRIP - 1, 0) for a in k0]
        v_up = [pltpu.roll(a, STRIP - 1, 0) for a in v0]
        c_y, f_y = [], []
        for r in range(n):
            c = 0.5 * (k0[r] + shifted_up(k_up, r))
            if r == n - 1:
                sub = lax.broadcasted_iota(jnp.int32, c.shape, 0)
                c = jnp.where(sub == STRIP - 1, 0.0, c)
            cy[x, sl[r], :] = c
            c_y.append(c)
            f_y.append(c * (v0[r] - shifted_up(v_up, r)))
        c_dn = [pltpu.roll(a, 1, 0) for a in c_y]
        f_dn = [pltpu.roll(a, 1, 0) for a in f_y]
        for r in range(n):
            a = sl[r]
            c_next = h_next * (k0[r] + k[xn, a, :])
            f_next = c_next * (v0[r] - v[xn, a, :])
            c_prev = cx[x, a, :]
            f_prev = fx[a, :]
            cx[x + 1, a, :] = c_next
            fx[a, :] = f_next
            c_z = 0.5 * (k0[r] + zp(k0[r]))
            f_z = c_z * (v0[r] - zp(v0[r]))
            cz[x, a, :] = c_z
            diag = ((REACTION + c_next) + (c_prev + c_y[r])) + (
                (shifted_down(c_dn, r) + c_z) + zm(c_z)
            )
            res = ((s[x, a, :] - REACTION * v0[r]) + (f_prev - f_next)) + (
                (shifted_down(f_dn, r) - f_y[r]) + (zm(f_z) - f_z)
            )
            w = DAMPING / diag
            w_ref[x, a, :] = w
            f_ref[x, a, :] = w * res
            half = r * STRIP // F
            sums[half * STRIP : (half + 1) * STRIP, :] += res
            sums[(2 + half) * STRIP : (3 + half) * STRIP, :] += k0[r]
            if r == 0:
                drow[0, pl.ds(x, 1), :] = diag[0:1]
                rrow[0, pl.ds(x, 1), :] = res[0:1]
            if r == n - 1:
                drow[1, pl.ds(x, 1), :] = diag[STRIP - 1 :]
                rrow[1, pl.ds(x, 1), :] = res[STRIP - 1 :]

            @pl.when(x == 0)
            def _():
                d_lo[a, :] = diag
                r_lo[a, :] = res

            @pl.when(x == planes - 1)
            def _():
                d_hi[a, :] = diag
                r_hi[a, :] = res

        return carry

    lax.fori_loop(0, planes, plane, 0)


def cross(q_pl, q_row, pls, rws, sign):
    rows, planes = q_pl.shape[1], q_row.shape[1]
    for a in range(2):
        pls[a][...] = pls[a][...] + sign * q_pl[a]
        rws[a][...] = rws[a][...] + sign * q_row[a]
    for a, x in ((0, 0), (1, planes - 1)):
        for b, y in ((0, 0), (1, rows - 1)):
            pls[a][y : y + 1, :] = pls[a][y : y + 1, :] + sign * q_row[b, x : x + 1, :]
            rws[b][x : x + 1, :] = rws[b][x : x + 1, :] + sign * q_pl[a, y : y + 1, :]


def split3(a):
    one = a.astype(BF16)
    rest = a - one.astype(F32)
    two = rest.astype(BF16)
    three = (rest - two.astype(F32)).astype(BF16)
    return jnp.concatenate([one, two, three], 0)


def joined3(a):
    n = a.shape[0] // 3
    return a[:n] + a[n : 2 * n] + a[2 * n :]


def edge_kernel(
    d_lo, d_hi, r_lo, r_hi, drow, rrow, pl_lo, pl_hi, rw_lo, rw_hi, xl, xh, yl, yh, sums,
    f_pl0, f_pl1, f_row0, f_row1, w_pl0, w_pl1, w_row0, w_row1, wc_pl, wc_row, payload,
    q_pl, q_row,
):
    rows, cols = d_lo.shape
    f_pl, f_row, w_pl, w_row = (f_pl0, f_pl1), (f_row0, f_row1), (w_pl0, w_pl1), (w_row0, w_row1)
    for side, mine, other in ((0, pl_lo, xl), (1, pl_hi, xh)):
        c = 0.5 * (mine[1] + other[1])
        wc_pl[side] = c
        q_pl[side] = c * (mine[0] - other[0])
    for side, mine, other in ((0, rw_lo, yl), (1, rw_hi, yh)):
        c = 0.5 * (mine[1] + other[1])
        wc_row[side] = c
        q_row[side] = c * (mine[0] - other[0])
    for side, d, r in ((0, d_lo, r_lo), (1, d_hi, r_hi)):
        w_pl[side][...] = d[...]
        f_pl[side][...] = r[...]
        w_row[side][...] = drow[side]
        f_row[side][...] = rrow[side]
    cross(wc_pl, wc_row, w_pl, w_row, 1.0)
    cross(q_pl, q_row, f_pl, f_row, -1.0)
    for w, f, wc in ((w_pl, f_pl, wc_pl), (w_row, f_row, wc_row)):
        for side in range(2):
            inv = DAMPING / w[side][...]
            w[side][...] = inv
            f[side][...] = f[side][...] * inv
            wc[side] = wc[side] * inv
    parts = []
    for half in range(rows // F):
        total = sums[half * STRIP : (half + 1) * STRIP, :]
        for side in range(2):
            for r in range(half * F // STRIP, (half + 1) * F // STRIP):
                total = total - q_pl[side, r * STRIP : (r + 1) * STRIP, :]
        if half == 0:
            for r in range(q_row.shape[1] // STRIP):
                total = total - q_row[0, r * STRIP : (r + 1) * STRIP, :]
        if half == rows // F - 1:
            for r in range(q_row.shape[1] // STRIP):
                total = total - q_row[1, r * STRIP : (r + 1) * STRIP, :]
        parts.append(total)
    parts.append(sums[2 * STRIP :, :])
    col = lax.broadcasted_iota(jnp.int32, (cols, cols // F), 0)
    cell = lax.broadcasted_iota(jnp.int32, (cols, cols // F), 1)
    gather = jnp.where(col // F == cell, 1.0, 0.0).astype(BF16)
    reduced = joined3(
        jnp.dot(split3(jnp.concatenate(parts, 0)), gather, preferred_element_type=F32)
    )
    means = [
        jnp.sum(reduced[i * STRIP : (i + 1) * STRIP], axis=0, keepdims=True) * (1.0 / F**3)
        for i in range(4)
    ]
    tile = jnp.concatenate(means + means, 0)
    for i in range(payload.shape[0] // STRIP):
        payload[i * STRIP : (i + 1) * STRIP, :] = tile


def put_edges(ref, e_pl0, e_pl1, e_row0, e_row1):
    planes, rows, _ = ref.shape
    for x in range(1, planes - 1):
        ref[x, 0:1, :] = e_row0[x : x + 1, :]
        ref[x, rows - 1 : rows, :] = e_row1[x : x + 1, :]
    ref[0] = e_pl0[...]
    ref[planes - 1] = e_pl1[...]


def neighbour_sums(x, u, cx, cy, cz):
    planes, rows, _ = u.shape
    sl = strips(rows)
    xn, xp = jnp.minimum(x + 1, planes - 1), jnp.maximum(x - 1, 0)
    u0 = [u[x, a, :] for a in sl]
    u_up = [pltpu.roll(a, STRIP - 1, 0) for a in u0]
    c_y = [cy[x, a, :] for a in sl]
    q_dn = [pltpu.roll(c * a, 1, 0) for c, a in zip(c_y, u0)]
    for r, a in enumerate(sl):
        c_z = cz[x, a, :]
        total = (
            (cx[x + 1, a, :] * u[xn, a, :] + cx[x, a, :] * u[xp, a, :])
            + (c_y[r] * shifted_up(u_up, r) + shifted_down(q_dn, r))
            + (c_z * zp(u0[r]) + zm(c_z * u0[r]))
        )
        yield r, a, u0[r], total


def sweep_kernel(
    w, f, cx, cy, cz, w_pl0, w_pl1, w_row0, w_row1, f_pl0, f_pl1, f_row0, f_row1,
    g_ref, g_pl, g_row,
):
    planes, rows, cols = w.shape
    put_edges(w, w_pl0, w_pl1, w_row0, w_row1)
    put_edges(f, f_pl0, f_pl1, f_row0, f_row1)

    def plane(x, carry):
        for r, a, u0, total in neighbour_sums(x, f, cx, cy, cz):
            new = (2.0 - DAMPING) * u0 + w[x, a, :] * total
            g_ref[x, a, :] = new
            if r == 0:
                g_row[0, pl.ds(x, 1), :] = new[0:1]
            if (r + 1) * STRIP == rows:
                g_row[1, pl.ds(x, 1), :] = new[STRIP - 1 :]
        return carry

    lax.fori_loop(0, planes, plane, 0)
    g_pl[0] = g_ref[0]
    g_pl[1] = g_ref[planes - 1]


def mid_kernel(
    g_pl, g_row, wc_pl, wc_row, xl, xh, yl, yh, o_pl0, o_pl1, o_row0, o_row1, q_pl, q_row
):
    for side, x, y in ((0, xl, yl), (1, xh, yh)):
        q_pl[side] = wc_pl[side] * x[...]
        q_row[side] = wc_row[side] * y[...]
    for side, p, r in ((0, o_pl0, o_row0), (1, o_pl1, o_row1)):
        p[...] = g_pl[side]
        r[...] = g_row[side]
    cross(q_pl, q_row, (o_pl0, o_pl1), (o_row0, o_row1), 1.0)


def last_kernel(
    w, f, cx, cy, cz, g, interp, w_pl0, w_pl1, w_row0, w_row1, f_pl0, f_pl1, f_row0, f_row1,
    g_pl0, g_pl1, g_row0, g_row1, out, b_pl, b_lo, b_hi, body, sems,
):
    planes, rows, cols = w.shape
    n = rows // STRIP
    put_edges(w, w_pl0, w_pl1, w_row0, w_row1)
    put_edges(f, f_pl0, f_pl1, f_row0, f_row1)
    put_edges(g, g_pl0, g_pl1, g_row0, g_row1)

    def copy(x):
        return pltpu.make_async_copy(
            body.at[x], out.at[x, STRIP : rows - STRIP, :], sems.at[x]
        )

    def plane(x, carry):
        offset = ((x % F).astype(F32) + 0.5) / F - 0.5
        weight = jnp.abs(offset)
        side = jnp.where(offset > 0, 2, 0)
        inside = (x > 0) & (x < planes - 1)
        slot = jnp.clip(x - 1, 0, planes - 3)
        end = jnp.where(x == 0, 0, 1)
        for r, a, u0, total in neighbour_sums(x, g, cx, cy, cz):
            coarse = (1.0 - weight) * interp[1, a, :] + weight * interp[side, a, :]
            new = (f[x, a, :] + (1.0 - DAMPING) * u0) + (w[x, a, :] * total + coarse)

            @pl.when(inside)
            def _():
                if r == 0:
                    b_lo[slot] = new
                elif r == n - 1:
                    b_hi[slot] = new
                else:
                    body[x, (r - 1) * STRIP : r * STRIP, :] = new

            @pl.when(jnp.logical_not(inside))
            def _():
                b_pl[end, a, :] = new

        @pl.when(inside)
        def _():
            copy(x).start()

        return carry

    lax.fori_loop(0, planes, plane, 0)
    for x in range(1, planes - 1):
        copy(x).wait()


def finish_kernel(
    src, b_pl, b_lo, b_hi, wc_pl, wc_row, xl, xh, yl, yh, out, s_pl, s_lo, s_hi, sems
):
    del src
    planes, rows, cols = out.shape
    spots = (
        (s_lo, out.at[1 : planes - 1, 0:STRIP, :]),
        (s_hi, out.at[1 : planes - 1, rows - STRIP : rows, :]),
        (s_pl.at[0], out.at[0]),
        (s_pl.at[1], out.at[planes - 1]),
    )
    copies = [pltpu.make_async_copy(a, b, sems.at[i]) for i, (a, b) in enumerate(spots)]
    sub = lax.broadcasted_iota(jnp.int32, (STRIP, cols), 0)
    for x in range(1, planes - 1):
        q = wc_row[0, x : x + 1, :] * yl[x : x + 1, :]
        s_lo[x - 1] = b_lo[x - 1] + jnp.where(sub == 0, q, 0.0)
    copies[0].start()
    for x in range(1, planes - 1):
        q = wc_row[1, x : x + 1, :] * yh[x : x + 1, :]
        s_hi[x - 1] = b_hi[x - 1] + jnp.where(sub == STRIP - 1, q, 0.0)
    copies[1].start()
    for side, other in ((0, xl), (1, xh)):
        x = side * (planes - 1)
        s_pl[side] = b_pl[side] + wc_pl[side] * other[...]
        for y, b, halo in ((0, 0, yl), (rows - 1, 1, yh)):
            s_pl[side, y : y + 1, :] = (
                s_pl[side, y : y + 1, :] + wc_row[b, x : x + 1, :] * halo[x : x + 1, :]
            )
        copies[2 + side].start()
    for c in copies:
        c.wait()


def coarse_kernel(place, got, interp, coef, b_ref, u_ref, *, nx, ny, rows):
    nz = got.shape[1]
    per = 2 * 2

    def field(start):
        return [
            jnp.stack([got[pl.ds(p * ny * per + start + t, ny, stride=per), :] for p in range(nx)], 0)
            for t in range(2)
        ]

    resid, cond = field(0), field(2)

    def beside(a, t):
        mine = a[t]
        nxt = jnp.concatenate([mine[1:], mine[:1]], 0)
        prv = jnp.concatenate([mine[-1:], mine[:-1]], 0)
        up = a[1] if t == 0 else pltpu.roll(a[0], ny - 1, 1)
        down = a[0] if t == 1 else pltpu.roll(a[1], 1, 1)
        return nxt, prv, up, down, pltpu.roll(mine, 1, 2), pltpu.roll(mine, nz - 1, 2)

    for t in range(2):
        cs = [(0.5 * COARSE_FACTOR) * (cond[t] + other) for other in beside(cond, t)]
        diag = REACTION
        for c in cs:
            diag = diag + c
        inv = DAMPING / diag
        for i, c in enumerate(cs):
            coef[i, t] = inv * c
        b_ref[t] = inv * resid[t]
        u_ref[0, t] = b_ref[t]

    def sweep(src, dst):
        for p in range(nx):
            pn, pp = (p + 1) % nx, (p - 1) % nx
            u = [u_ref[src, t, p] for t in range(2)]
            for t in range(2):
                up = u[1] if t == 0 else pltpu.roll(u[0], ny - 1, 0)
                down = u[0] if t == 1 else pltpu.roll(u[1], 1, 0)
                a = b_ref[t, p] + (1.0 - DAMPING) * u[t]
                a = a + coef[0, t, p] * u_ref[src, t, pn]
                a = a + coef[1, t, p] * u_ref[src, t, pp]
                c = coef[2, t, p] * up + coef[3, t, p] * down
                c = c + coef[4, t, p] * pltpu.roll(u[t], 1, 1)
                c = c + coef[5, t, p] * pltpu.roll(u[t], nz - 1, 1)
                u_ref[dst, t, p] = a + c

    def pair(i, carry):
        sweep(0, 1)
        sweep(1, 0)
        return carry

    steps = CSWEEPS - 1
    lax.fori_loop(0, steps // 2, pair, 0)
    last = 0
    if steps % 2:
        sweep(0, 1)
        last = 1

    gx, gy = place[0], place[1]
    lines = []
    for d in (-1, 0, 1):
        p = lax.rem(gx + d + nx, nx)
        prev_s, next_s = lax.rem(gy + ny - 1, ny), lax.rem(gy + 1, ny)
        for t, s in ((1, prev_s), (0, gy), (1, gy), (0, next_s)):
            lines.append(u_ref[last, t, p, pl.ds(s, 1), :])
    lines = jnp.concatenate(lines + lines[:4], 0)
    cols = nz * F
    cell = lax.broadcasted_iota(jnp.int32, (nz, cols), 0)
    col = lax.broadcasted_iota(jnp.int32, (nz, cols), 1)
    base = col // F
    offset = ((col % F).astype(F32) + 0.5) / F - 0.5
    side = jnp.where(offset > 0, base + 1, base - 1)
    side = jnp.where(side < 0, side + nz, jnp.where(side >= nz, side - nz, side))
    weight = jnp.abs(offset)
    matrix = jnp.where(cell == base, 1.0 - weight, 0.0) + jnp.where(cell == side, weight, 0.0)
    wide = joined3(jnp.dot(split3(lines), matrix.astype(BF16), preferred_element_type=F32))
    sub = lax.broadcasted_iota(jnp.int32, (STRIP, cols), 0)
    for plane in range(3):
        for r in range(rows // STRIP):
            row = r * STRIP + sub
            off = ((row % F).astype(F32) + 0.5) / F - 0.5
            wt = jnp.abs(off)
            block = r * STRIP // F
            near = block + 1
            far = near + (1 if (r * STRIP) % F >= F // 2 else -1)
            a = wide[plane * 4 + near : plane * 4 + near + 1]
            c = wide[plane * 4 + far : plane * 4 + far + 1]
            interp[plane, r * STRIP : (r + 1) * STRIP, :] = (1.0 - wt) * a + wt * c


def swap(axis, low, high):
    count = lax.axis_size(axis)
    forward = [(i, (i + 1) % count) for i in range(count)]
    backward = [(i, (i - 1) % count) for i in range(count)]
    return lax.ppermute(high, axis, forward), lax.ppermute(low, axis, backward)


def per_device(nx, ny, v, s, k):
    planes, rows, cols = v.shape
    n = planes * rows * cols
    vm = pltpu.VMEM
    dma = pltpu.SemaphoreType.DMA
    full, edge, line = sds(planes, rows, cols), sds(rows, cols), sds(planes, cols)
    edges, lines = sds(2, rows, cols), sds(2, planes, cols)

    rw_lo, rw_hi, pl_lo, pl_hi = pl.pallas_call(
        ends_kernel,
        out_shape=(lines, lines, edges, edges),
        in_specs=[ANY] * 2,
        out_specs=(VM,) * 4,
        scratch_shapes=[dma((2, 4))],
        compiler_params=params(4),
        cost_estimate=cost(0, n // 2),
        name="ends",
    )(v, k)
    yl, yh = swap("gy", rw_lo, rw_hi)
    xl, xh = swap("gx", pl_lo, pl_hi)

    w, f, cx, cy, cz, d_lo, d_hi, r_lo, r_hi, drow, rrow, sums = pl.pallas_call(
        inner_kernel,
        out_shape=(full, full, sds(planes + 1, rows, cols), full, full)
        + (edge,) * 4
        + (lines, lines, sds(4 * STRIP, cols)),
        in_specs=[ANY] * 3,
        out_specs=(VM,) * 12,
        scratch_shapes=[vm(full.shape, F32)] * 3 + [vm(edge.shape, F32), dma((3, planes))],
        compiler_params=params(18),
        cost_estimate=cost(50 * n, 32 * n),
        name="inner",
    )(v, s, k)

    devices = nx * ny
    out = pl.pallas_call(
        edge_kernel,
        out_shape=(edge, edge, line, line) * 2 + (edges, lines, sds(devices * 4, cols // F)),
        in_specs=[VM] * 15,
        out_specs=(VM,) * 11,
        scratch_shapes=[vm(edges.shape, F32), vm(lines.shape, F32)],
        compiler_params=params(6),
        cost_estimate=cost(10 * n // 8, n),
        name="edge",
    )(d_lo, d_hi, r_lo, r_hi, drow, rrow, pl_lo, pl_hi, rw_lo, rw_hi, xl, xh, yl, yh, sums)
    f_edges, w_edges, (wc_pl, wc_row, payload) = out[:4], out[4:8], out[8:]

    fyl, fyh = swap("gy", f_edges[2], f_edges[3])
    fxl, fxh = swap("gx", f_edges[0], f_edges[1])
    got = lax.all_to_all(payload, ("gx", "gy"), 0, 0, tiled=True)

    g, g_pl, g_row = pl.pallas_call(
        sweep_kernel,
        out_shape=(full, edges, lines),
        in_specs=[VM] * 13,
        out_specs=(VM,) * 3,
        compiler_params=params(4),
        cost_estimate=cost(40 * n, 16 * n),
        name="sweep",
    )(w, f, cx, cy, cz, *w_edges, *f_edges)

    g_edges = pl.pallas_call(
        mid_kernel,
        out_shape=(edge, edge, line, line),
        in_specs=[VM] * 8,
        out_specs=(VM,) * 4,
        scratch_shapes=[vm(edges.shape, F32), vm(lines.shape, F32)],
        compiler_params=params(4),
        cost_estimate=cost(n // 8, n // 2),
        name="mid",
    )(g_pl, g_row, wc_pl, wc_row, fxl, fxh, fyl, fyh)

    gyl, gyh = swap("gy", g_edges[2], g_edges[3])
    gxl, gxh = swap("gx", g_edges[0], g_edges[1])

    place = jnp.stack([lax.axis_index("gx"), lax.axis_index("gy")]).astype(jnp.int32)
    cells = (nx, ny, cols // F)
    interp = pl.pallas_call(
        functools.partial(coarse_kernel, nx=nx, ny=ny, rows=rows),
        out_shape=sds(3, rows, cols),
        in_specs=[SM, VM],
        out_specs=VM,
        scratch_shapes=[
            vm((6, 2) + cells, F32),
            vm((2,) + cells, F32),
            vm((2, 2) + cells, F32),
        ],
        compiler_params=params(8),
        cost_estimate=cost(20 * n, n),
        name="coarse",
    )(place, got)

    b_side = sds(planes - 2, STRIP, cols)
    out, b_pl, b_lo, b_hi = pl.pallas_call(
        last_kernel,
        out_shape=(full, edges, b_side, b_side),
        in_specs=[VM] * 19,
        out_specs=(ANY, VM, VM, VM),
        scratch_shapes=[vm((planes, rows - 2 * STRIP, cols), F32), dma((planes,))],
        compiler_params=params(8),
        cost_estimate=cost(40 * n, 20 * n),
        name="last",
    )(w, f, cx, cy, cz, g, interp, *w_edges, *f_edges, *g_edges)

    return pl.pallas_call(
        finish_kernel,
        out_shape=full,
        in_specs=[ANY] + [VM] * 9,
        out_specs=ANY,
        scratch_shapes=[
            vm(edges.shape, F32), vm(b_side.shape, F32), vm(b_side.shape, F32), dma((4,)),
        ],
        input_output_aliases={0: 0},
        compiler_params=params(6),
        cost_estimate=cost(n // 4, 3 * n),
        name="finish",
    )(out, b_pl, b_lo, b_hi, wc_pl, wc_row, gxl, gxh, gyl, gyh)


def solution(mesh):
    placed = P("gx", "gy", None)
    body = functools.partial(per_device, mesh.shape["gx"], mesh.shape["gy"])
    return jax.shard_map(
        body, mesh=mesh, in_specs=(placed,) * 3, out_specs=placed, check_vma=False
    )
```

```python
import functools
import jax
import jax.numpy as jnp
from jax import lax
from jax.experimental import pallas as pl
from jax.experimental.pallas import tpu as pltpu
from jax.sharding import PartitionSpec as P

F = 16
CSWEEPS = 32
REACTION = 0.2
DAMPING = 0.8
COARSE_FACTOR = 0.25
F32 = jnp.float32
BF16 = jnp.bfloat16
STRIP = 8

VM = pl.BlockSpec(memory_space=pltpu.VMEM)
ANY = pl.BlockSpec(memory_space=pl.ANY)
HBM = pl.BlockSpec(memory_space=pltpu.HBM)


def params(mib):
    return pltpu.CompilerParams(vmem_limit_bytes=mib * 1024 * 1024)


def cost(flops, nbytes):
    return pl.CostEstimate(flops=int(flops), bytes_accessed=int(nbytes), transcendentals=0)


def sds(*shape):
    return jax.ShapeDtypeStruct(shape, F32)


def zp(a):
    return pltpu.roll(a, a.shape[-1] - 1, a.ndim - 1)


def zm(a):
    return pltpu.roll(a, 1, a.ndim - 1)


def shifted_up(rolled, r):
    nxt = rolled[min(r + 1, len(rolled) - 1)]
    sub = lax.broadcasted_iota(jnp.int32, nxt.shape, 0)
    return jnp.where(sub == STRIP - 1, nxt, rolled[r])


def shifted_down(rolled, r):
    prv = rolled[r - 1]
    sub = lax.broadcasted_iota(jnp.int32, prv.shape, 0)
    return jnp.where(sub == 0, prv, rolled[r])


def up_coupling(k0, k_up, r):
    c = 0.5 * (k0[r] + shifted_up(k_up, r))
    if r == len(k0) - 1:
        sub = lax.broadcasted_iota(jnp.int32, c.shape, 0)
        c = jnp.where(sub == STRIP - 1, 0.0, c)
    return c


def strips(rows):
    return [slice(r * STRIP, (r + 1) * STRIP) for r in range(rows // STRIP)]


def ends_kernel(v, k, rw_lo, rw_hi, pl_lo, pl_hi, sems):
    planes, rows, _ = v.shape
    copies = []
    for i, a in enumerate((v, k)):
        for j, (src, dst) in enumerate(
            (
                (a.at[:, 0, :], rw_lo.at[i]),
                (a.at[:, rows - 1, :], rw_hi.at[i]),
                (a.at[0], pl_lo.at[i]),
                (a.at[planes - 1], pl_hi.at[i]),
            )
        ):
            copies.append(pltpu.make_async_copy(src, dst, sems.at[i, j]))
    for c in copies:
        c.start()
    for c in copies:
        c.wait()


def inner_kernel(
    v_hbm, s_hbm, k_hbm,
    w_hbm, f_hbm, d_lo, d_hi, r_lo, r_hi, drow, rrow, sums,
    v, s, k, w_ref, f_ref, cx, fx, sems, out_sems,
):
    planes, rows, cols = v.shape
    sl = strips(rows)
    n = len(sl)

    def copy(i, x):
        src, dst = ((k_hbm, k), (v_hbm, v), (s_hbm, s))[i]
        return pltpu.make_async_copy(src.at[x], dst.at[x], sems.at[i, x])

    def out_copy(i, x):
        src, dst = ((w_ref, w_hbm), (f_ref, f_hbm))[i]
        return pltpu.make_async_copy(src.at[x], dst.at[x], out_sems.at[i, x])

    for x in range(planes):
        for i in range(3):
            copy(i, x).start()
    sums[...] = jnp.zeros_like(sums)
    fx[...] = jnp.zeros_like(fx)
    cx[...] = jnp.zeros_like(cx)
    copy(0, 0).wait()
    copy(1, 0).wait()

    def plane(x, carry):
        @pl.when(x < planes - 1)
        def _():
            copy(0, x + 1).wait()
            copy(1, x + 1).wait()

        copy(2, x).wait()
        xn = jnp.minimum(x + 1, planes - 1)
        h_next = jnp.where(x < planes - 1, 0.5, 0.0).astype(F32)
        k0 = [k[x, a, :] for a in sl]
        v0 = [v[x, a, :] for a in sl]
        k_up = [pltpu.roll(a, STRIP - 1, 0) for a in k0]
        v_up = [pltpu.roll(a, STRIP - 1, 0) for a in v0]
        c_y, f_y = [], []
        for r in range(n):
            c = up_coupling(k0, k_up, r)
            c_y.append(c)
            f_y.append(c * (v0[r] - shifted_up(v_up, r)))
        c_dn = [pltpu.roll(a, 1, 0) for a in c_y]
        f_dn = [pltpu.roll(a, 1, 0) for a in f_y]
        for r in range(n):
            a = sl[r]
            c_next = h_next * (k0[r] + k[xn, a, :])
            f_next = c_next * (v0[r] - v[xn, a, :])
            c_prev = cx[a, :]
            f_prev = fx[a, :]
            cx[a, :] = c_next
            fx[a, :] = f_next
            c_z = 0.5 * (k0[r] + zp(k0[r]))
            f_z = c_z * (v0[r] - zp(v0[r]))
            diag = ((REACTION + c_next) + (c_prev + c_y[r])) + (
                (shifted_down(c_dn, r) + c_z) + zm(c_z)
            )
            res = ((s[x, a, :] - REACTION * v0[r]) + (f_prev - f_next)) + (
                (shifted_down(f_dn, r) - f_y[r]) + (zm(f_z) - f_z)
            )
            w = DAMPING / diag
            w_ref[x, a, :] = w
            f_ref[x, a, :] = w * res
            half = r * STRIP // F
            sums[half * STRIP : (half + 1) * STRIP, :] += res
            sums[(2 + half) * STRIP : (3 + half) * STRIP, :] += k0[r]
            if r == 0:
                drow[0, pl.ds(x, 1), :] = diag[0:1]
                rrow[0, pl.ds(x, 1), :] = res[0:1]
            if r == n - 1:
                drow[1, pl.ds(x, 1), :] = diag[STRIP - 1 :]
                rrow[1, pl.ds(x, 1), :] = res[STRIP - 1 :]

            @pl.when(x == 0)
            def _():
                d_lo[a, :] = diag
                r_lo[a, :] = res

            @pl.when(x == planes - 1)
            def _():
                d_hi[a, :] = diag
                r_hi[a, :] = res

        out_copy(0, x).start()
        out_copy(1, x).start()
        return carry

    lax.fori_loop(0, planes, plane, 0)
    for x in range(planes):
        for i in range(2):
            out_copy(i, x).wait()


def cross(q_pl, q_row, pls, rws, sign):
    rows, planes = q_pl.shape[1], q_row.shape[1]
    for a in range(2):
        pls[a][...] = pls[a][...] + sign * q_pl[a]
        rws[a][...] = rws[a][...] + sign * q_row[a]
    for a, x in ((0, 0), (1, planes - 1)):
        for b, y in ((0, 0), (1, rows - 1)):
            pls[a][y : y + 1, :] = pls[a][y : y + 1, :] + sign * q_row[b, x : x + 1, :]
            rws[b][x : x + 1, :] = rws[b][x : x + 1, :] + sign * q_pl[a, y : y + 1, :]


def split3(a):
    one = a.astype(BF16)
    rest = a - one.astype(F32)
    two = rest.astype(BF16)
    three = (rest - two.astype(F32)).astype(BF16)
    return jnp.concatenate([one, two, three], 0)


def joined3(a):
    n = a.shape[0] // 3
    return a[:n] + a[n : 2 * n] + a[2 * n :]


def edge_kernel(
    d_lo, d_hi, r_lo, r_hi, drow, rrow, pl_lo, pl_hi, rw_lo, rw_hi, xl, xh, yl, yh, sums,
    f_pl0, f_pl1, f_row0, f_row1, w_pl0, w_pl1, w_row0, w_row1, wc_pl, wc_row, payload,
    q_pl, q_row,
):
    rows, cols = d_lo.shape
    f_pl, f_row, w_pl, w_row = (f_pl0, f_pl1), (f_row0, f_row1), (w_pl0, w_pl1), (w_row0, w_row1)
    for side, mine, other in ((0, pl_lo, xl), (1, pl_hi, xh)):
        c = 0.5 * (mine[1] + other[1])
        wc_pl[side] = c
        q_pl[side] = c * (mine[0] - other[0])
    for side, mine, other in ((0, rw_lo, yl), (1, rw_hi, yh)):
        c = 0.5 * (mine[1] + other[1])
        wc_row[side] = c
        q_row[side] = c * (mine[0] - other[0])
    for side, d, r in ((0, d_lo, r_lo), (1, d_hi, r_hi)):
        w_pl[side][...] = d[...]
        f_pl[side][...] = r[...]
        w_row[side][...] = drow[side]
        f_row[side][...] = rrow[side]
    cross(wc_pl, wc_row, w_pl, w_row, 1.0)
    cross(q_pl, q_row, f_pl, f_row, -1.0)
    for w, f, wc in ((w_pl, f_pl, wc_pl), (w_row, f_row, wc_row)):
        for side in range(2):
            inv = DAMPING / w[side][...]
            w[side][...] = inv
            f[side][...] = f[side][...] * inv
            wc[side] = wc[side] * inv
    parts = []
    for half in range(rows // F):
        total = sums[half * STRIP : (half + 1) * STRIP, :]
        for side in range(2):
            for r in range(half * F // STRIP, (half + 1) * F // STRIP):
                total = total - q_pl[side, r * STRIP : (r + 1) * STRIP, :]
        if half == 0:
            for r in range(q_row.shape[1] // STRIP):
                total = total - q_row[0, r * STRIP : (r + 1) * STRIP, :]
        if half == rows // F - 1:
            for r in range(q_row.shape[1] // STRIP):
                total = total - q_row[1, r * STRIP : (r + 1) * STRIP, :]
        parts.append(total)
    parts.append(sums[2 * STRIP :, :])
    col = lax.broadcasted_iota(jnp.int32, (cols, cols // F), 0)
    cell = lax.broadcasted_iota(jnp.int32, (cols, cols // F), 1)
    gather = jnp.where(col // F == cell, 1.0, 0.0).astype(BF16)
    reduced = joined3(
        jnp.dot(split3(jnp.concatenate(parts, 0)), gather, preferred_element_type=F32)
    )
    means = [
        jnp.sum(reduced[i * STRIP : (i + 1) * STRIP], axis=0, keepdims=True) * (1.0 / F**3)
        for i in range(4)
    ]
    tile = jnp.concatenate(means + means, 0)
    for i in range(payload.shape[0] // STRIP):
        payload[i * STRIP : (i + 1) * STRIP, :] = tile


def put_edges(ref, x, e_pl0, e_pl1, e_row0, e_row1):
    planes, rows, _ = ref.shape
    ref[x, 0:1, :] = e_row0[pl.ds(x, 1), :]
    ref[x, rows - 1 : rows, :] = e_row1[pl.ds(x, 1), :]

    @pl.when(x == 0)
    def _():
        ref[x] = e_pl0[...]

    @pl.when(x == planes - 1)
    def _():
        ref[x] = e_pl1[...]


def neighbour_sums(x, u, cx, cy, cz):
    planes, rows, _ = u.shape
    sl = strips(rows)
    xn, xp = jnp.minimum(x + 1, planes - 1), jnp.maximum(x - 1, 0)
    u0 = [u[x, a, :] for a in sl]
    u_up = [pltpu.roll(a, STRIP - 1, 0) for a in u0]
    c_y = [cy[x, a, :] for a in sl]
    q_dn = [pltpu.roll(c * a, 1, 0) for c, a in zip(c_y, u0)]
    for r, a in enumerate(sl):
        c_z = cz[x, a, :]
        total = (
            (cx[x + 1, a, :] * u[xn, a, :] + cx[x, a, :] * u[xp, a, :])
            + (c_y[r] * shifted_up(u_up, r) + shifted_down(q_dn, r))
            + (c_z * zp(u0[r]) + zm(c_z * u0[r]))
        )
        yield r, a, u0[r], total


def sweep_kernel(
    k_hbm, w_hbm, f_hbm, w_pl0, w_pl1, w_row0, w_row1, f_pl0, f_pl1, f_row0, f_row1,
    w, f, cx_hbm, cy, cz, g_ref, g_pl, g_row, k, cx, sems, out_sems,
):
    planes, rows, cols = w.shape
    sl = strips(rows)

    def out_copy(x):
        return pltpu.make_async_copy(cx.at[x], cx_hbm.at[x], out_sems.at[x])

    def copy(i, x):
        src, dst = ((k_hbm, k), (f_hbm, f), (w_hbm, w))[i]
        return pltpu.make_async_copy(src.at[x], dst.at[x], sems.at[i, x])

    def arrive(x):
        for i in range(3):
            copy(i, x).wait()
        put_edges(f, x, f_pl0, f_pl1, f_row0, f_row1)
        put_edges(w, x, w_pl0, w_pl1, w_row0, w_row1)

    for x in range(planes):
        for i in range(3):
            copy(i, x).start()
    cx[0] = jnp.zeros_like(k[0])
    out_copy(0).start()
    arrive(0)

    def plane(x, carry):
        @pl.when(x < planes - 1)
        def _():
            arrive(x + 1)

        xn = jnp.minimum(x + 1, planes - 1)
        h_next = jnp.where(x < planes - 1, 0.5, 0.0).astype(F32)
        k0 = [k[x, a, :] for a in sl]
        k_up = [pltpu.roll(a, STRIP - 1, 0) for a in k0]
        for r, a in enumerate(sl):
            cx[x + 1, a, :] = h_next * (k0[r] + k[xn, a, :])
            cy[x, a, :] = up_coupling(k0, k_up, r)
            cz[x, a, :] = 0.5 * (k0[r] + zp(k0[r]))
        for r, a, u0, total in neighbour_sums(x, f, cx, cy, cz):
            new = (2.0 - DAMPING) * u0 + w[x, a, :] * total
            g_ref[x, a, :] = new
            if r == 0:
                g_row[0, pl.ds(x, 1), :] = new[0:1]
            if (r + 1) * STRIP == rows:
                g_row[1, pl.ds(x, 1), :] = new[STRIP - 1 :]
        out_copy(x + 1).start()
        return carry

    lax.fori_loop(0, planes, plane, 0)
    g_pl[0] = g_ref[0]
    g_pl[1] = g_ref[planes - 1]
    for x in range(planes + 1):
        out_copy(x).wait()


def mid_kernel(
    g_pl, g_row, wc_pl, wc_row, xl, xh, yl, yh, o_pl0, o_pl1, o_row0, o_row1, q_pl, q_row
):
    for side, x, y in ((0, xl, yl), (1, xh, yh)):
        q_pl[side] = wc_pl[side] * x[...]
        q_row[side] = wc_row[side] * y[...]
    for side, p, r in ((0, o_pl0, o_row0), (1, o_pl1, o_row1)):
        p[...] = g_pl[side]
        r[...] = g_row[side]
    cross(q_pl, q_row, (o_pl0, o_pl1), (o_row0, o_row1), 1.0)


def last_kernel(
    w, f, cx_hbm, cy, cz, g_any, interp, g_pl0, g_pl1, g_row0, g_row1,
    out, b_pl, b_lo, b_hi, g, cx, body, in_sems, cx_sems, sems,
):
    planes, rows, cols = w.shape
    n = rows // STRIP

    def in_copy(x):
        return pltpu.make_async_copy(g_any.at[x], g.at[x], in_sems.at[x])

    def copy(x):
        return pltpu.make_async_copy(
            body.at[x], out.at[x, STRIP : rows - STRIP, :], sems.at[x]
        )

    def cx_copy(x):
        return pltpu.make_async_copy(cx_hbm.at[x], cx.at[x], cx_sems.at[x])

    def arrive(x):
        cx_copy(x + 1).wait()
        in_copy(x).wait()
        put_edges(g, x, g_pl0, g_pl1, g_row0, g_row1)

    cx_copy(0).start()
    for x in range(planes):
        in_copy(x).start()
        cx_copy(x + 1).start()
    cx_copy(0).wait()
    arrive(0)

    def plane(x, carry):
        @pl.when(x < planes - 1)
        def _():
            arrive(x + 1)

        offset = ((x % F).astype(F32) + 0.5) / F - 0.5
        weight = jnp.abs(offset)
        side = jnp.where(offset > 0, 2, 0)
        inside = (x > 0) & (x < planes - 1)
        slot = jnp.clip(x - 1, 0, planes - 3)
        end = jnp.where(x == 0, 0, 1)
        for r, a, u0, total in neighbour_sums(x, g, cx, cy, cz):
            coarse = (1.0 - weight) * interp[1, a, :] + weight * interp[side, a, :]
            new = (f[x, a, :] + (1.0 - DAMPING) * u0) + (w[x, a, :] * total + coarse)

            @pl.when(inside)
            def _():
                if r == 0:
                    b_lo[slot] = new
                elif r == n - 1:
                    b_hi[slot] = new
                else:
                    body[x, (r - 1) * STRIP : r * STRIP, :] = new

            @pl.when(jnp.logical_not(inside))
            def _():
                b_pl[end, a, :] = new

        @pl.when(inside)
        def _():
            copy(x).start()

        return carry

    lax.fori_loop(0, planes, plane, 0)
    for x in range(1, planes - 1):
        copy(x).wait()


def finish_kernel(
    src, b_pl, b_lo, b_hi, wc_pl, wc_row, xl, xh, yl, yh, out, s_pl, s_lo, s_hi, sems
):
    del src
    planes, rows, cols = out.shape
    spots = (
        (s_lo, out.at[1 : planes - 1, 0:STRIP, :]),
        (s_hi, out.at[1 : planes - 1, rows - STRIP : rows, :]),
        (s_pl.at[0], out.at[0]),
        (s_pl.at[1], out.at[planes - 1]),
    )
    copies = [pltpu.make_async_copy(a, b, sems.at[i]) for i, (a, b) in enumerate(spots)]
    sub = lax.broadcasted_iota(jnp.int32, (STRIP, cols), 0)
    for x in range(1, planes - 1):
        q = wc_row[0, x : x + 1, :] * yl[x : x + 1, :]
        s_lo[x - 1] = b_lo[x - 1] + jnp.where(sub == 0, q, 0.0)
    copies[0].start()
    for x in range(1, planes - 1):
        q = wc_row[1, x : x + 1, :] * yh[x : x + 1, :]
        s_hi[x - 1] = b_hi[x - 1] + jnp.where(sub == STRIP - 1, q, 0.0)
    copies[1].start()
    for side, other in ((0, xl), (1, xh)):
        x = side * (planes - 1)
        s_pl[side] = b_pl[side] + wc_pl[side] * other[...]
        for y, b, halo in ((0, 0, yl), (rows - 1, 1, yh)):
            s_pl[side, y : y + 1, :] = (
                s_pl[side, y : y + 1, :] + wc_row[b, x : x + 1, :] * halo[x : x + 1, :]
            )
        copies[2 + side].start()
    for c in copies:
        c.wait()


def coarse_kernel(got, interp, coef, b_ref, u_ref, *, nx, ny, rows):
    nz = got.shape[1]
    per = 2 * 2

    def field(start):
        return [
            jnp.stack([got[pl.ds(p * ny * per + start + t, ny, stride=per), :] for p in range(nx)], 0)
            for t in range(2)
        ]

    resid, cond = field(0), field(2)

    def beside(a, t):
        mine = a[t]
        nxt = jnp.concatenate([mine[1:], mine[:1]], 0)
        prv = jnp.concatenate([mine[-1:], mine[:-1]], 0)
        up = a[1] if t == 0 else pltpu.roll(a[0], ny - 1, 1)
        down = a[0] if t == 1 else pltpu.roll(a[1], 1, 1)
        return nxt, prv, up, down, pltpu.roll(mine, 1, 2), pltpu.roll(mine, nz - 1, 2)

    for t in range(2):
        cs = [(0.5 * COARSE_FACTOR) * (cond[t] + other) for other in beside(cond, t)]
        diag = REACTION
        for c in cs:
            diag = diag + c
        inv = DAMPING / diag
        for i, c in enumerate(cs):
            coef[i, t] = inv * c
        b_ref[t] = inv * resid[t]
        u_ref[0, t] = b_ref[t]

    def sweep(src, dst):
        for p in range(nx):
            pn, pp = (p + 1) % nx, (p - 1) % nx
            u = [u_ref[src, t, p] for t in range(2)]
            for t in range(2):
                up = u[1] if t == 0 else pltpu.roll(u[0], ny - 1, 0)
                down = u[0] if t == 1 else pltpu.roll(u[1], 1, 0)
                a = b_ref[t, p] + (1.0 - DAMPING) * u[t]
                a = a + coef[0, t, p] * u_ref[src, t, pn]
                a = a + coef[1, t, p] * u_ref[src, t, pp]
                c = coef[2, t, p] * up + coef[3, t, p] * down
                c = c + coef[4, t, p] * pltpu.roll(u[t], 1, 1)
                c = c + coef[5, t, p] * pltpu.roll(u[t], nz - 1, 1)
                u_ref[dst, t, p] = a + c

    def pair(i, carry):
        sweep(0, 1)
        sweep(1, 0)
        return carry

    steps = CSWEEPS - 1
    lax.fori_loop(0, steps // 2, pair, 0)
    last = 0
    if steps % 2:
        sweep(0, 1)
        last = 1

    gx, gy = lax.axis_index("gx"), lax.axis_index("gy")
    lines = []
    for d in (-1, 0, 1):
        p = lax.rem(gx + d + nx, nx)
        prev_s, next_s = lax.rem(gy + ny - 1, ny), lax.rem(gy + 1, ny)
        for t, s in ((1, prev_s), (0, gy), (1, gy), (0, next_s)):
            lines.append(u_ref[last, t, p, pl.ds(s, 1), :])
    lines = jnp.concatenate(lines + lines[:4], 0)
    cols = nz * F
    cell = lax.broadcasted_iota(jnp.int32, (nz, cols), 0)
    col = lax.broadcasted_iota(jnp.int32, (nz, cols), 1)
    base = col // F
    offset = ((col % F).astype(F32) + 0.5) / F - 0.5
    side = jnp.where(offset > 0, base + 1, base - 1)
    side = jnp.where(side < 0, side + nz, jnp.where(side >= nz, side - nz, side))
    weight = jnp.abs(offset)
    matrix = jnp.where(cell == base, 1.0 - weight, 0.0) + jnp.where(cell == side, weight, 0.0)
    wide = joined3(jnp.dot(split3(lines), matrix.astype(BF16), preferred_element_type=F32))
    sub = lax.broadcasted_iota(jnp.int32, (STRIP, cols), 0)
    for plane in range(3):
        for r in range(rows // STRIP):
            row = r * STRIP + sub
            off = ((row % F).astype(F32) + 0.5) / F - 0.5
            wt = jnp.abs(off)
            block = r * STRIP // F
            near = block + 1
            far = near + (1 if (r * STRIP) % F >= F // 2 else -1)
            a = wide[plane * 4 + near : plane * 4 + near + 1]
            c = wide[plane * 4 + far : plane * 4 + far + 1]
            interp[plane, r * STRIP : (r + 1) * STRIP, :] = (1.0 - wt) * a + wt * c


def swap(axis, low, high):
    count = lax.axis_size(axis)
    forward = [(i, (i + 1) % count) for i in range(count)]
    backward = [(i, (i - 1) % count) for i in range(count)]
    return lax.ppermute(high, axis, forward), lax.ppermute(low, axis, backward)


def per_device(nx, ny, v, s, k):
    planes, rows, cols = v.shape
    n = planes * rows * cols
    vm = pltpu.VMEM
    dma = pltpu.SemaphoreType.DMA
    full, edge, line = sds(planes, rows, cols), sds(rows, cols), sds(planes, cols)
    edges, lines = sds(2, rows, cols), sds(2, planes, cols)

    rw_lo, rw_hi, pl_lo, pl_hi = pl.pallas_call(
        ends_kernel,
        out_shape=(lines, lines, edges, edges),
        in_specs=[HBM] * 2,
        out_specs=(VM,) * 4,
        scratch_shapes=[dma((2, 4))],
        compiler_params=params(58),
        cost_estimate=cost(0, n // 2),
        name="ends",
    )(v, k)
    yl, yh = swap("gy", rw_lo, rw_hi)
    xl, xh = swap("gx", pl_lo, pl_hi)

    w, f, d_lo, d_hi, r_lo, r_hi, drow, rrow, sums = pl.pallas_call(
        inner_kernel,
        out_shape=(full, full) + (edge,) * 4 + (lines, lines, sds(4 * STRIP, cols)),
        in_specs=[HBM] * 3,
        out_specs=(HBM,) * 2 + (VM,) * 7,
        scratch_shapes=[vm(full.shape, F32)] * 5
        + [vm(edge.shape, F32)] * 2
        + [dma((3, planes)), dma((2, planes))],
        compiler_params=params(52),
        cost_estimate=cost(50 * n, 20 * n),
        name="inner",
    )(v, s, k)

    devices = nx * ny
    out = pl.pallas_call(
        edge_kernel,
        out_shape=(edge, edge, line, line) * 2 + (edges, lines, sds(devices * 4, cols // F)),
        in_specs=[VM] * 15,
        out_specs=(VM,) * 11,
        scratch_shapes=[vm(edges.shape, F32), vm(lines.shape, F32)],
        compiler_params=params(6),
        cost_estimate=cost(10 * n // 8, n),
        name="edge",
    )(d_lo, d_hi, r_lo, r_hi, drow, rrow, pl_lo, pl_hi, rw_lo, rw_hi, xl, xh, yl, yh, sums)
    f_edges, w_edges, (wc_pl, wc_row, payload) = out[:4], out[4:8], out[8:]

    fyl, fyh = swap("gy", f_edges[2], f_edges[3])
    fxl, fxh = swap("gx", f_edges[0], f_edges[1])
    got = lax.all_to_all(payload, ("gx", "gy"), 0, 0, tiled=True)

    got, w, f, k = lax.optimization_barrier((got, w, f, k))

    w, f, cx, cy, cz, g, g_pl, g_row = pl.pallas_call(
        sweep_kernel,
        out_shape=(full, full, sds(planes + 1, rows, cols), full, full, full, edges, lines),
        in_specs=[HBM] * 3 + [VM] * 8,
        out_specs=(VM, VM, HBM) + (VM,) * 5,
        scratch_shapes=[
            vm(full.shape, F32),
            vm((planes + 1, rows, cols), F32),
            dma((3, planes)),
            dma((planes + 1,)),
        ],
        compiler_params=params(31),
        cost_estimate=cost(40 * n, 12 * n),
        name="sweep",
    )(k, w, f, *w_edges, *f_edges)

    g_edges = pl.pallas_call(
        mid_kernel,
        out_shape=(edge, edge, line, line),
        in_specs=[VM] * 8,
        out_specs=(VM,) * 4,
        scratch_shapes=[vm(edges.shape, F32), vm(lines.shape, F32)],
        compiler_params=params(4),
        cost_estimate=cost(n // 8, n // 2),
        name="mid",
    )(g_pl, g_row, wc_pl, wc_row, fxl, fxh, fyl, fyh)

    gyl, gyh = swap("gy", g_edges[2], g_edges[3])
    gxl, gxh = swap("gx", g_edges[0], g_edges[1])

    cells = (nx, ny, cols // F)
    interp = pl.pallas_call(
        functools.partial(coarse_kernel, nx=nx, ny=ny, rows=rows),
        out_shape=sds(3, rows, cols),
        in_specs=[VM],
        out_specs=VM,
        scratch_shapes=[
            vm((6, 2) + cells, F32),
            vm((2,) + cells, F32),
            vm((2, 2) + cells, F32),
        ],
        compiler_params=params(8),
        cost_estimate=cost(20 * n, n),
        name="coarse",
    )(got)

    b_side = sds(planes - 2, STRIP, cols)
    out, b_pl, b_lo, b_hi = pl.pallas_call(
        last_kernel,
        out_shape=(full, edges, b_side, b_side),
        in_specs=[VM] * 2 + [HBM] + [VM] * 2 + [ANY] + [VM] * 5,
        out_specs=(HBM, VM, VM, VM),
        scratch_shapes=[
            vm(full.shape, F32),
            vm((planes + 1, rows, cols), F32),
            vm((planes, rows - 2 * STRIP, cols), F32),
            dma((planes,)),
            dma((planes + 1,)),
            dma((planes,)),
        ],
        compiler_params=params(30),
        cost_estimate=cost(40 * n, 20 * n),
        name="last",
    )(w, f, cx, cy, cz, g, interp, *g_edges)

    return pl.pallas_call(
        finish_kernel,
        out_shape=full,
        in_specs=[HBM] + [VM] * 9,
        out_specs=HBM,
        scratch_shapes=[
            vm(edges.shape, F32), vm(b_side.shape, F32), vm(b_side.shape, F32), dma((4,)),
        ],
        input_output_aliases={0: 0},
        compiler_params=params(6),
        cost_estimate=cost(n // 4, 3 * n),
        name="finish",
    )(out, b_pl, b_lo, b_hi, wc_pl, wc_row, gxl, gxh, gyl, gyh)


def solution(mesh):
    placed = P("gx", "gy", None)
    body = functools.partial(per_device, mesh.shape["gx"], mesh.shape["gy"])
    return jax.shard_map(
        body, mesh=mesh, in_specs=(placed,) * 3, out_specs=placed, check_vma=False
    )
```

```python
import functools
import jax
import jax.numpy as jnp
from jax import lax
from jax.experimental import pallas as pl
from jax.experimental.pallas import tpu as pltpu
from jax.sharding import PartitionSpec as P

F = 16
CSWEEPS = 32
REACTION = 0.2
DAMPING = 0.8
COARSE_FACTOR = 0.25
F32 = jnp.float32
BF16 = jnp.bfloat16
STRIP = 8
LANES = 128

VM = pl.BlockSpec(memory_space=pltpu.VMEM)
ANY = pl.BlockSpec(memory_space=pl.ANY)
HBM = pl.BlockSpec(memory_space=pltpu.HBM)


def params(mib):
    return pltpu.CompilerParams(vmem_limit_bytes=mib * 1024 * 1024)


def cost(flops, nbytes):
    return pl.CostEstimate(flops=int(flops), bytes_accessed=int(nbytes), transcendentals=0)


def sds(*shape):
    return jax.ShapeDtypeStruct(shape, F32)


def left(a):
    return pltpu.roll(a, LANES - 1, 1)


def right(a):
    return pltpu.roll(a, 1, 1)


def upward(a):
    return pltpu.roll(a, STRIP - 1, 0)


def downward(a):
    return pltpu.roll(a, 1, 0)


def masks():
    lane = lax.broadcasted_iota(jnp.int32, (STRIP, LANES), 1)
    sub = lax.broadcasted_iota(jnp.int32, (STRIP, LANES), 0)
    return lane == 0, lane == LANES - 1, sub == 0, sub == STRIP - 1


def tiles(cols):
    return [slice(j * LANES, (j + 1) * LANES) for j in range(cols // LANES)]


def strips(rows):
    return [slice(r * STRIP, (r + 1) * STRIP) for r in range(rows // STRIP)]


def ends_kernel(v, k, rw_lo, rw_hi, pl_lo, pl_hi, sems):
    planes, rows, _ = v.shape
    copies = []
    for i, a in enumerate((v, k)):
        for j, (src, dst) in enumerate(
            (
                (a.at[:, 0, :], rw_lo.at[i]),
                (a.at[:, rows - 1, :], rw_hi.at[i]),
                (a.at[0], pl_lo.at[i]),
                (a.at[planes - 1], pl_hi.at[i]),
            )
        ):
            copies.append(pltpu.make_async_copy(src, dst, sems.at[i, j]))
    for c in copies:
        c.start()
    for c in copies:
        c.wait()


def inner_kernel(
    v_hbm, s_hbm, k_hbm,
    w_hbm, f_hbm, d_lo, d_hi, r_lo, r_hi, drow, rrow, sums,
    v, s, k, w_ref, f_ref, cx, fx, ends, sems, out_sems,
):
    planes, rows, cols = v.shape
    sl = strips(rows)
    n = len(sl)

    def copy(i, x):
        src, dst = ((k_hbm, k), (v_hbm, v), (s_hbm, s))[i]
        return pltpu.make_async_copy(src.at[x], dst.at[x], sems.at[i, x])

    def out_copy(i, x):
        src, dst = ((w_ref, w_hbm), (f_ref, f_hbm))[i]
        return pltpu.make_async_copy(src.at[x], dst.at[x], out_sems.at[i, x])

    for x in range(planes):
        for i in range(3):
            copy(i, x).start()
    sums[...] = jnp.zeros_like(sums)
    fx[...] = jnp.zeros_like(fx)
    cx[...] = jnp.zeros_like(cx)
    copy(0, 0).wait()
    copy(1, 0).wait()
    tl = tiles(cols)
    m = len(tl)
    lane0, lane1, sub0, sub1 = masks()

    def plane(x, first=False, last=False):
        xn = x if last else x + 1
        if not last:
            copy(0, x + 1).wait()
            copy(1, x + 1).wait()
        copy(2, x).wait()
        rk = [left(k[x, a, tl[0]]) for a in sl]
        rv = [left(v[x, a, tl[0]]) for a in sl]
        pc, pf = [], []
        for r, a in enumerate(sl):
            k0, v0 = k[x, a, tl[-1]], v[x, a, tl[-1]]
            c = 0.5 * (k0 + jnp.where(lane1, rk[r], left(k0)))
            pc.append(right(c))
            pf.append(right(c * (v0 - jnp.where(lane1, rv[r], left(v0)))))
        for j in range(m):
            t, tn = tl[j], tl[(j + 1) % m]
            ks = [k[x, a, t] for a in sl]
            vs = [v[x, a, t] for a in sl]
            ku = [upward(a) for a in ks]
            vu = [upward(a) for a in vs]
            dc = df = 0.0
            res_sum = k_sum = None
            for r, a in enumerate(sl):
                k0, v0 = ks[r], vs[r]
                nk, nv = left(k[x, a, tn]), left(v[x, a, tn])
                c_z = 0.5 * (k0 + jnp.where(lane1, nk, rk[r]))
                f_z = c_z * (v0 - jnp.where(lane1, nv, rv[r]))
                rk[r], rv[r] = nk, nv
                mc, mf = right(c_z), right(f_z)
                diag = c_z + jnp.where(lane0, pc[r], mc)
                res = jnp.where(lane0, pf[r], mf) - f_z
                pc[r], pf[r] = mc, mf
                if r < n - 1:
                    c_y = 0.5 * (k0 + jnp.where(sub1, ku[r + 1], ku[r]))
                    f_y = c_y * (v0 - jnp.where(sub1, vu[r + 1], vu[r]))
                else:
                    c_y = jnp.where(sub1, 0.0, 0.5 * (k0 + ku[r]))
                    f_y = c_y * (v0 - vu[r])
                nc, nf = downward(c_y), downward(f_y)
                diag = diag + (c_y + jnp.where(sub0, dc, nc))
                res = res + (jnp.where(sub0, df, nf) - f_y)
                dc, df = nc, nf
                if not first:
                    diag = diag + cx[a, t]
                    res = res + fx[a, t]
                if not last:
                    c_x = 0.5 * (k0 + k[xn, a, t])
                    f_x = c_x * (v0 - v[xn, a, t])
                    cx[a, t] = c_x
                    fx[a, t] = f_x
                    diag = diag + c_x
                    res = res - f_x
                diag = diag + REACTION
                res = res + (s[x, a, t] - REACTION * v0)
                w = DAMPING / diag
                w_ref[x, a, t] = w
                f_ref[x, a, t] = w * res
                half = r * STRIP // F
                res_sum = res if r * STRIP % F == 0 else res_sum + res
                k_sum = k0 if r * STRIP % F == 0 else k_sum + k0
                if (r + 1) * STRIP % F == 0:
                    sums[half * STRIP : (half + 1) * STRIP, t] += res_sum
                    sums[(2 + half) * STRIP : (3 + half) * STRIP, t] += k_sum
                if r in (0, n - 1):
                    ends[min(r, 1), 0, :, t] = diag
                    ends[min(r, 1), 1, :, t] = res
                if first:
                    d_lo[a, t] = diag
                    r_lo[a, t] = res
                if last:
                    d_hi[a, t] = diag
                    r_hi[a, t] = res
        for b, y in ((0, 0), (1, STRIP - 1)):
            drow[b, pl.ds(x, 1), :] = ends[b, 0, y : y + 1, :]
            rrow[b, pl.ds(x, 1), :] = ends[b, 1, y : y + 1, :]
        out_copy(0, x).start()
        out_copy(1, x).start()

    def body(x, carry):
        plane(x)
        return carry

    plane(0, first=True)
    lax.fori_loop(1, planes - 1, body, 0)
    plane(planes - 1, last=True)
    for x in range(planes):
        for i in range(2):
            out_copy(i, x).wait()


def cross(q_pl, q_row, pls, rws, sign):
    rows, planes = q_pl.shape[1], q_row.shape[1]
    for a in range(2):
        pls[a][...] = pls[a][...] + sign * q_pl[a]
        rws[a][...] = rws[a][...] + sign * q_row[a]
    for a, x in ((0, 0), (1, planes - 1)):
        for b, y in ((0, 0), (1, rows - 1)):
            pls[a][y : y + 1, :] = pls[a][y : y + 1, :] + sign * q_row[b, x : x + 1, :]
            rws[b][x : x + 1, :] = rws[b][x : x + 1, :] + sign * q_pl[a, y : y + 1, :]


def split3(a):
    one = a.astype(BF16)
    rest = a - one.astype(F32)
    two = rest.astype(BF16)
    three = (rest - two.astype(F32)).astype(BF16)
    return jnp.concatenate([one, two, three], 0)


def joined3(a):
    n = a.shape[0] // 3
    return a[:n] + a[n : 2 * n] + a[2 * n :]


def edge_kernel(
    d_lo, d_hi, r_lo, r_hi, drow, rrow, pl_lo, pl_hi, rw_lo, rw_hi, xl, xh, yl, yh, sums,
    f_pl0, f_pl1, f_row0, f_row1, w_pl0, w_pl1, w_row0, w_row1, wc_pl, wc_row, payload,
    q_pl, q_row,
):
    rows, cols = d_lo.shape
    f_pl, f_row, w_pl, w_row = (f_pl0, f_pl1), (f_row0, f_row1), (w_pl0, w_pl1), (w_row0, w_row1)
    for side, mine, other in ((0, pl_lo, xl), (1, pl_hi, xh)):
        c = 0.5 * (mine[1] + other[1])
        wc_pl[side] = c
        q_pl[side] = c * (mine[0] - other[0])
    for side, mine, other in ((0, rw_lo, yl), (1, rw_hi, yh)):
        c = 0.5 * (mine[1] + other[1])
        wc_row[side] = c
        q_row[side] = c * (mine[0] - other[0])
    for side, d, r in ((0, d_lo, r_lo), (1, d_hi, r_hi)):
        w_pl[side][...] = d[...]
        f_pl[side][...] = r[...]
        w_row[side][...] = drow[side]
        f_row[side][...] = rrow[side]
    cross(wc_pl, wc_row, w_pl, w_row, 1.0)
    cross(q_pl, q_row, f_pl, f_row, -1.0)
    for w, f, wc in ((w_pl, f_pl, wc_pl), (w_row, f_row, wc_row)):
        for side in range(2):
            inv = DAMPING / w[side][...]
            w[side][...] = inv
            f[side][...] = f[side][...] * inv
            wc[side] = wc[side] * inv
    parts = []
    for half in range(rows // F):
        total = sums[half * STRIP : (half + 1) * STRIP, :]
        for side in range(2):
            for r in range(half * F // STRIP, (half + 1) * F // STRIP):
                total = total - q_pl[side, r * STRIP : (r + 1) * STRIP, :]
        if half == 0:
            for r in range(q_row.shape[1] // STRIP):
                total = total - q_row[0, r * STRIP : (r + 1) * STRIP, :]
        if half == rows // F - 1:
            for r in range(q_row.shape[1] // STRIP):
                total = total - q_row[1, r * STRIP : (r + 1) * STRIP, :]
        parts.append(total)
    parts.append(sums[2 * STRIP :, :])
    col = lax.broadcasted_iota(jnp.int32, (cols, cols // F), 0)
    cell = lax.broadcasted_iota(jnp.int32, (cols, cols // F), 1)
    gather = jnp.where(col // F == cell, 1.0, 0.0).astype(BF16)
    reduced = joined3(
        jnp.dot(split3(jnp.concatenate(parts, 0)), gather, preferred_element_type=F32)
    )
    means = [
        jnp.sum(reduced[i * STRIP : (i + 1) * STRIP], axis=0, keepdims=True) * (1.0 / F**3)
        for i in range(4)
    ]
    tile = jnp.concatenate(means + means, 0)
    for i in range(payload.shape[0] // STRIP):
        payload[i * STRIP : (i + 1) * STRIP, :] = tile


def put_edges(ref, x, e_pl0, e_pl1, e_row0, e_row1):
    planes, rows, _ = ref.shape
    ref[x, 0:1, :] = e_row0[pl.ds(x, 1), :]
    ref[x, rows - 1 : rows, :] = e_row1[pl.ds(x, 1), :]

    @pl.when(x == 0)
    def _():
        ref[x] = e_pl0[...]

    @pl.when(x == planes - 1)
    def _():
        ref[x] = e_pl1[...]


def tile_sums(x, u, coupling, side_coupling):
    planes, rows, cols = u.shape
    sl, tl = strips(rows), tiles(cols)
    m = len(tl)
    lane0, lane1, sub0, sub1 = masks()
    xn, xp = jnp.minimum(x + 1, planes - 1), jnp.maximum(x - 1, 0)
    ru = [left(u[x, a, tl[0]]) for a in sl]
    pm = [right(side_coupling(r) * u[x, a, tl[-1]]) for r, a in enumerate(sl)]
    for j in range(m):
        t, tn = tl[j], tl[(j + 1) % m]
        us = [u[x, a, t] for a in sl]
        uu = [upward(a) for a in us]
        dn = 0.0
        for r, a in enumerate(sl):
            c_next, c_prev, c_up, c_z = coupling(r, a, j, t, tn)
            u0 = us[r]
            nu = left(u[x, a, tn])
            total = c_next * u[xn, a, t] + c_prev * u[xp, a, t]
            total = total + c_z * jnp.where(lane1, nu, ru[r])
            ru[r] = nu
            mu = right(c_z * u0)
            total = total + jnp.where(lane0, pm[r], mu)
            pm[r] = mu
            above = jnp.where(sub1, uu[r + 1], uu[r]) if r + 1 < len(sl) else uu[r]
            nd = downward(c_up * u0)
            total = total + (c_up * above + jnp.where(sub0, dn, nd))
            dn = nd
            yield r, a, t, u0, total


def sweep_kernel(
    k_hbm, w_hbm, f_hbm, w_pl0, w_pl1, w_row0, w_row1, f_pl0, f_pl1, f_row0, f_row1,
    w, f, cx_hbm, cy, cz, g_ref, g_pl, g_row, k, cx, sems, out_sems,
):
    planes, rows, cols = w.shape
    sl, tl = strips(rows), tiles(cols)

    def out_copy(x):
        return pltpu.make_async_copy(cx.at[x], cx_hbm.at[x], out_sems.at[x])

    def copy(i, x):
        src, dst = ((k_hbm, k), (f_hbm, f), (w_hbm, w))[i]
        return pltpu.make_async_copy(src.at[x], dst.at[x], sems.at[i, x])

    def arrive(x):
        for i in range(3):
            copy(i, x).wait()
        put_edges(f, x, f_pl0, f_pl1, f_row0, f_row1)
        put_edges(w, x, w_pl0, w_pl1, w_row0, w_row1)

    for x in range(planes):
        for i in range(3):
            copy(i, x).start()
    cx[0] = jnp.zeros_like(k[0])
    out_copy(0).start()
    arrive(0)

    def plane(x, carry):
        @pl.when(x < planes - 1)
        def _():
            arrive(x + 1)

        xn = jnp.minimum(x + 1, planes - 1)
        h_next = jnp.where(x < planes - 1, 0.5, 0.0).astype(F32)
        rk = [left(k[x, a, tl[0]]) for a in sl]
        lane0, lane1, sub0, sub1 = masks()

        def side_coupling(r):
            k0 = k[x, sl[r], tl[-1]]
            return 0.5 * (k0 + jnp.where(lane1, rk[r], left(k0)))

        def coupling(r, a, j, t, tn):
            k0 = k[x, a, t]
            up = upward(k0)
            if r + 1 < len(sl):
                c_up = 0.5 * (k0 + jnp.where(sub1, upward(k[x, sl[r + 1], t]), up))
            else:
                c_up = jnp.where(sub1, 0.0, 0.5 * (k0 + up))
            nk = left(k[x, a, tn])
            c_z = 0.5 * (k0 + jnp.where(lane1, nk, rk[r]))
            rk[r] = nk
            c_next = h_next * (k0 + k[xn, a, t])
            cx[x + 1, a, t] = c_next
            cy[x, a, t] = c_up
            cz[x, a, t] = c_z
            return c_next, cx[x, a, t], c_up, c_z

        for r, a, t, u0, total in tile_sums(x, f, coupling, side_coupling):
            new = (2.0 - DAMPING) * u0 + w[x, a, t] * total
            g_ref[x, a, t] = new
        g_row[0, pl.ds(x, 1), :] = g_ref[x, 0:1, :]
        g_row[1, pl.ds(x, 1), :] = g_ref[x, rows - 1 : rows, :]
        out_copy(x + 1).start()
        return carry

    lax.fori_loop(0, planes, plane, 0)
    g_pl[0] = g_ref[0]
    g_pl[1] = g_ref[planes - 1]
    for x in range(planes + 1):
        out_copy(x).wait()


def mid_kernel(
    g_pl, g_row, wc_pl, wc_row, xl, xh, yl, yh, o_pl0, o_pl1, o_row0, o_row1, q_pl, q_row
):
    for side, x, y in ((0, xl, yl), (1, xh, yh)):
        q_pl[side] = wc_pl[side] * x[...]
        q_row[side] = wc_row[side] * y[...]
    for side, p, r in ((0, o_pl0, o_row0), (1, o_pl1, o_row1)):
        p[...] = g_pl[side]
        r[...] = g_row[side]
    cross(q_pl, q_row, (o_pl0, o_pl1), (o_row0, o_row1), 1.0)


def last_kernel(
    w, f, cx_hbm, cy, cz, g_any, interp, g_pl0, g_pl1, g_row0, g_row1,
    out, body, g, cx, in_sems, cx_sems, sems,
):
    planes, rows, cols = w.shape

    def in_copy(x):
        return pltpu.make_async_copy(g_any.at[x], g.at[x], in_sems.at[x])

    def copy(x):
        return pltpu.make_async_copy(
            body.at[x, STRIP : rows - STRIP, :], out.at[x, STRIP : rows - STRIP, :], sems.at[x]
        )

    def cx_copy(x):
        return pltpu.make_async_copy(cx_hbm.at[x], cx.at[x], cx_sems.at[x])

    def arrive(x):
        cx_copy(x + 1).wait()
        in_copy(x).wait()
        put_edges(g, x, g_pl0, g_pl1, g_row0, g_row1)

    cx_copy(0).start()
    for x in range(planes):
        in_copy(x).start()
        cx_copy(x + 1).start()
    cx_copy(0).wait()
    arrive(0)

    def plane(x, carry):
        @pl.when(x < planes - 1)
        def _():
            arrive(x + 1)

        offset = ((x % F).astype(F32) + 0.5) / F - 0.5
        weight = jnp.abs(offset)
        side = jnp.where(offset > 0, 2, 0)

        def coupling(r, a, j, t, tn):
            return cx[x + 1, a, t], cx[x, a, t], cy[x, a, t], cz[x, a, t]

        def side_coupling(r):
            return cz[x, strips(rows)[r], tiles(cols)[-1]]

        for r, a, t, u0, total in tile_sums(x, g, coupling, side_coupling):
            coarse = (1.0 - weight) * interp[1, a, t] + weight * interp[side, a, t]
            new = f[x, a, t] + (1.0 - DAMPING) * u0 + coarse
            body[x, a, t] = new + w[x, a, t] * total

        @pl.when((x > 0) & (x < planes - 1))
        def _():
            copy(x).start()

        return carry

    lax.fori_loop(0, planes, plane, 0)
    for x in range(1, planes - 1):
        copy(x).wait()


def finish_kernel(
    src, body, wc_pl, wc_row, xl, xh, yl, yh, out, s_pl, s_lo, s_hi, sems
):
    del src
    planes, rows, cols = out.shape
    spots = (
        (s_lo, out.at[1 : planes - 1, 0:STRIP, :]),
        (s_hi, out.at[1 : planes - 1, rows - STRIP : rows, :]),
        (s_pl.at[0], out.at[0]),
        (s_pl.at[1], out.at[planes - 1]),
    )
    copies = [pltpu.make_async_copy(a, b, sems.at[i]) for i, (a, b) in enumerate(spots)]
    sub = lax.broadcasted_iota(jnp.int32, (STRIP, cols), 0)
    for x in range(1, planes - 1):
        q = wc_row[0, x : x + 1, :] * yl[x : x + 1, :]
        s_lo[x - 1] = body[x, :STRIP, :] + jnp.where(sub == 0, q, 0.0)
    copies[0].start()
    for x in range(1, planes - 1):
        q = wc_row[1, x : x + 1, :] * yh[x : x + 1, :]
        s_hi[x - 1] = body[x, rows - STRIP :, :] + jnp.where(sub == STRIP - 1, q, 0.0)
    copies[1].start()
    for side, other in ((0, xl), (1, xh)):
        x = side * (planes - 1)
        s_pl[side] = body[x] + wc_pl[side] * other[...]
        for y, b, halo in ((0, 0, yl), (rows - 1, 1, yh)):
            s_pl[side, y : y + 1, :] = (
                s_pl[side, y : y + 1, :] + wc_row[b, x : x + 1, :] * halo[x : x + 1, :]
            )
        copies[2 + side].start()
    for c in copies:
        c.wait()


def coarse_kernel(got, interp, coef, b_ref, u_ref, *, nx, ny, rows):
    nz = got.shape[1]
    per = 2 * 2

    def field(start):
        return [
            jnp.stack([got[pl.ds(p * ny * per + start + t, ny, stride=per), :] for p in range(nx)], 0)
            for t in range(2)
        ]

    resid, cond = field(0), field(2)

    def beside(a, t):
        mine = a[t]
        nxt = jnp.concatenate([mine[1:], mine[:1]], 0)
        prv = jnp.concatenate([mine[-1:], mine[:-1]], 0)
        up = a[1] if t == 0 else pltpu.roll(a[0], ny - 1, 1)
        down = a[0] if t == 1 else pltpu.roll(a[1], 1, 1)
        return nxt, prv, up, down, pltpu.roll(mine, 1, 2), pltpu.roll(mine, nz - 1, 2)

    for t in range(2):
        cs = [(0.5 * COARSE_FACTOR) * (cond[t] + other) for other in beside(cond, t)]
        diag = REACTION
        for c in cs:
            diag = diag + c
        inv = DAMPING / diag
        for i, c in enumerate(cs):
            coef[i, t] = inv * c
        b_ref[t] = inv * resid[t]
        u_ref[0, t] = b_ref[t]

    def sweep(src, dst):
        for p in range(nx):
            pn, pp = (p + 1) % nx, (p - 1) % nx
            u = [u_ref[src, t, p] for t in range(2)]
            for t in range(2):
                up = u[1] if t == 0 else pltpu.roll(u[0], ny - 1, 0)
                down = u[0] if t == 1 else pltpu.roll(u[1], 1, 0)
                a = b_ref[t, p] + (1.0 - DAMPING) * u[t]
                a = a + coef[0, t, p] * u_ref[src, t, pn]
                a = a + coef[1, t, p] * u_ref[src, t, pp]
                c = coef[2, t, p] * up + coef[3, t, p] * down
                c = c + coef[4, t, p] * pltpu.roll(u[t], 1, 1)
                c = c + coef[5, t, p] * pltpu.roll(u[t], nz - 1, 1)
                u_ref[dst, t, p] = a + c

    def pair(i, carry):
        sweep(0, 1)
        sweep(1, 0)
        return carry

    steps = CSWEEPS - 1
    lax.fori_loop(0, steps // 2, pair, 0)
    last = 0
    if steps % 2:
        sweep(0, 1)
        last = 1

    gx, gy = lax.axis_index("gx"), lax.axis_index("gy")
    lines = []
    for d in (-1, 0, 1):
        p = lax.rem(gx + d + nx, nx)
        prev_s, next_s = lax.rem(gy + ny - 1, ny), lax.rem(gy + 1, ny)
        for t, s in ((1, prev_s), (0, gy), (1, gy), (0, next_s)):
            lines.append(u_ref[last, t, p, pl.ds(s, 1), :])
    lines = jnp.concatenate(lines + lines[:4], 0)
    cols = nz * F
    cell = lax.broadcasted_iota(jnp.int32, (nz, cols), 0)
    col = lax.broadcasted_iota(jnp.int32, (nz, cols), 1)
    base = col // F
    offset = ((col % F).astype(F32) + 0.5) / F - 0.5
    side = jnp.where(offset > 0, base + 1, base - 1)
    side = jnp.where(side < 0, side + nz, jnp.where(side >= nz, side - nz, side))
    weight = jnp.abs(offset)
    matrix = jnp.where(cell == base, 1.0 - weight, 0.0) + jnp.where(cell == side, weight, 0.0)
    wide = joined3(jnp.dot(split3(lines), matrix.astype(BF16), preferred_element_type=F32))
    sub = lax.broadcasted_iota(jnp.int32, (STRIP, cols), 0)
    for plane in range(3):
        for r in range(rows // STRIP):
            row = r * STRIP + sub
            off = ((row % F).astype(F32) + 0.5) / F - 0.5
            wt = jnp.abs(off)
            block = r * STRIP // F
            near = block + 1
            far = near + (1 if (r * STRIP) % F >= F // 2 else -1)
            a = wide[plane * 4 + near : plane * 4 + near + 1]
            c = wide[plane * 4 + far : plane * 4 + far + 1]
            interp[plane, r * STRIP : (r + 1) * STRIP, :] = (1.0 - wt) * a + wt * c


def swap(axis, low, high):
    count = lax.axis_size(axis)
    forward = [(i, (i + 1) % count) for i in range(count)]
    backward = [(i, (i - 1) % count) for i in range(count)]
    return lax.ppermute(high, axis, forward), lax.ppermute(low, axis, backward)


def per_device(nx, ny, v, s, k):
    planes, rows, cols = v.shape
    n = planes * rows * cols
    vm = pltpu.VMEM
    dma = pltpu.SemaphoreType.DMA
    full, edge, line = sds(planes, rows, cols), sds(rows, cols), sds(planes, cols)
    edges, lines = sds(2, rows, cols), sds(2, planes, cols)

    rw_lo, rw_hi, pl_lo, pl_hi = pl.pallas_call(
        ends_kernel,
        out_shape=(lines, lines, edges, edges),
        in_specs=[HBM] * 2,
        out_specs=(VM,) * 4,
        scratch_shapes=[dma((2, 4))],
        compiler_params=params(58),
        cost_estimate=cost(0, n // 2),
        name="ends",
    )(v, k)
    yl, yh = swap("gy", rw_lo, rw_hi)
    xl, xh = swap("gx", pl_lo, pl_hi)

    w, f, d_lo, d_hi, r_lo, r_hi, drow, rrow, sums = pl.pallas_call(
        inner_kernel,
        out_shape=(full, full) + (edge,) * 4 + (lines, lines, sds(4 * STRIP, cols)),
        in_specs=[HBM] * 3,
        out_specs=(HBM,) * 2 + (VM,) * 7,
        scratch_shapes=[vm(full.shape, F32)] * 5
        + [vm(edge.shape, F32)] * 2
        + [vm((2, 2, STRIP, cols), F32)]
        + [dma((3, planes)), dma((2, planes))],
        compiler_params=params(52),
        cost_estimate=cost(50 * n, 20 * n),
        name="inner",
    )(v, s, k)

    devices = nx * ny
    out = pl.pallas_call(
        edge_kernel,
        out_shape=(edge, edge, line, line) * 2 + (edges, lines, sds(devices * 4, cols // F)),
        in_specs=[VM] * 15,
        out_specs=(VM,) * 11,
        scratch_shapes=[vm(edges.shape, F32), vm(lines.shape, F32)],
        compiler_params=params(6),
        cost_estimate=cost(10 * n // 8, n),
        name="edge",
    )(d_lo, d_hi, r_lo, r_hi, drow, rrow, pl_lo, pl_hi, rw_lo, rw_hi, xl, xh, yl, yh, sums)
    f_edges, w_edges, (wc_pl, wc_row, payload) = out[:4], out[4:8], out[8:]

    fyl, fyh = swap("gy", f_edges[2], f_edges[3])
    fxl, fxh = swap("gx", f_edges[0], f_edges[1])
    got = lax.all_to_all(payload, ("gx", "gy"), 0, 0, tiled=True)

    got, w, f, k = lax.optimization_barrier((got, w, f, k))

    w, f, cx, cy, cz, g, g_pl, g_row = pl.pallas_call(
        sweep_kernel,
        out_shape=(full, full, sds(planes + 1, rows, cols), full, full, full, edges, lines),
        in_specs=[HBM] * 3 + [VM] * 8,
        out_specs=(VM, VM, HBM) + (VM,) * 5,
        scratch_shapes=[
            vm(full.shape, F32),
            vm((planes + 1, rows, cols), F32),
            dma((3, planes)),
            dma((planes + 1,)),
        ],
        compiler_params=params(30),
        cost_estimate=cost(40 * n, 12 * n),
        name="sweep",
    )(k, w, f, *w_edges, *f_edges)

    g_edges = pl.pallas_call(
        mid_kernel,
        out_shape=(edge, edge, line, line),
        in_specs=[VM] * 8,
        out_specs=(VM,) * 4,
        scratch_shapes=[vm(edges.shape, F32), vm(lines.shape, F32)],
        compiler_params=params(4),
        cost_estimate=cost(n // 8, n // 2),
        name="mid",
    )(g_pl, g_row, wc_pl, wc_row, fxl, fxh, fyl, fyh)

    gyl, gyh = swap("gy", g_edges[2], g_edges[3])
    gxl, gxh = swap("gx", g_edges[0], g_edges[1])

    cells = (nx, ny, cols // F)
    interp = pl.pallas_call(
        functools.partial(coarse_kernel, nx=nx, ny=ny, rows=rows),
        out_shape=sds(3, rows, cols),
        in_specs=[VM],
        out_specs=VM,
        scratch_shapes=[
            vm((6, 2) + cells, F32),
            vm((2,) + cells, F32),
            vm((2, 2) + cells, F32),
        ],
        compiler_params=params(8),
        cost_estimate=cost(20 * n, n),
        name="coarse",
    )(got)

    b_side = sds(planes - 2, STRIP, cols)
    out, body = pl.pallas_call(
        last_kernel,
        out_shape=(full, full),
        in_specs=[VM] * 2 + [HBM] + [VM] * 2 + [ANY] + [VM] * 5,
        out_specs=(HBM, VM),
        scratch_shapes=[
            vm(full.shape, F32),
            vm((planes + 1, rows, cols), F32),
            dma((planes,)),
            dma((planes + 1,)),
            dma((planes,)),
        ],
        compiler_params=params(27),
        cost_estimate=cost(40 * n, 20 * n),
        name="last",
    )(w, f, cx, cy, cz, g, interp, *g_edges)

    b_side = (planes - 2, STRIP, cols)
    return pl.pallas_call(
        finish_kernel,
        out_shape=full,
        in_specs=[HBM] + [VM] * 7,
        out_specs=HBM,
        scratch_shapes=[vm(edges.shape, F32), vm(b_side, F32), vm(b_side, F32), dma((4,))],
        input_output_aliases={0: 0},
        compiler_params=params(6),
        cost_estimate=cost(n // 4, 3 * n),
        name="finish",
    )(out, body, wc_pl, wc_row, gxl, gxh, gyl, gyh)


def solution(mesh):
    placed = P("gx", "gy", None)
    body = functools.partial(per_device, mesh.shape["gx"], mesh.shape["gy"])
    return jax.shard_map(
        body, mesh=mesh, in_specs=(placed,) * 3, out_specs=placed, check_vma=False
    )
```

```python
import functools
import jax
import jax.numpy as jnp
from jax import lax
from jax.experimental import pallas as pl
from jax.experimental.pallas import tpu as pltpu
from jax.sharding import PartitionSpec as P

F = 16
CSWEEPS = 32
REACTION = 0.2
DAMPING = 0.8
COARSE_FACTOR = 0.25
F32 = jnp.float32
BF16 = jnp.bfloat16
STRIP = 8
LANES = 512

VM = pl.BlockSpec(memory_space=pltpu.VMEM)
ANY = pl.BlockSpec(memory_space=pl.ANY)
HBM = pl.BlockSpec(memory_space=pltpu.HBM)


def params(mib):
    return pltpu.CompilerParams(vmem_limit_bytes=mib * 1024 * 1024)


def cost(flops, nbytes):
    return pl.CostEstimate(flops=int(flops), bytes_accessed=int(nbytes), transcendentals=0)


def sds(*shape):
    return jax.ShapeDtypeStruct(shape, F32)


def left(a):
    return pltpu.roll(a, a.shape[1] - 1, 1)


def right(a):
    return pltpu.roll(a, 1, 1)


def upward(a):
    return pltpu.roll(a, STRIP - 1, 0)


def downward(a):
    return pltpu.roll(a, 1, 0)


def strips(rows):
    return [slice(r * STRIP, (r + 1) * STRIP) for r in range(rows // STRIP)]


def edge_spots(axis, count):
    odd = lax.rem(lax.axis_index(axis), 2)
    return (1 - odd) * (count - 1), odd * (count - 1)


def low_high(axis):
    odd = lax.rem(lax.axis_index(axis), 2)
    return 1 - odd, odd


def ends_kernel(v, k, rw_a, rw_b, pl_a, pl_b, sems):
    planes, rows, _ = v.shape
    xs, ys = edge_spots("gx", planes), edge_spots("gy", rows)
    copies = []
    for i, a in enumerate((v, k)):
        for j, (src, dst) in enumerate(
            (
                (a.at[:, ys[0], :], rw_a.at[i]),
                (a.at[:, ys[1], :], rw_b.at[i]),
                (a.at[xs[0]], pl_a.at[i]),
                (a.at[xs[1]], pl_b.at[i]),
            )
        ):
            copies.append(pltpu.make_async_copy(src, dst, sems.at[i, j]))
    for c in copies:
        c.start()
    for c in copies:
        c.wait()


def inner_kernel(
    v_hbm, s_hbm, k_hbm,
    w_hbm, f_hbm, w_pl, f_pl, w_row, f_row, sums,
    v, s, k, w_ref, f_ref, cx, fx, sems, out_sems,
):
    planes, rows, cols = v.shape
    sl = strips(rows)
    n = len(sl)
    low, high = low_high("gy")

    def copy(i, x):
        src, dst = ((k_hbm, k), (v_hbm, v), (s_hbm, s))[i]
        return pltpu.make_async_copy(src.at[x], dst.at[x], sems.at[i, x])

    def out_copy(i, x):
        src, dst = ((w_ref, w_hbm), (f_ref, f_hbm))[i]
        return pltpu.make_async_copy(src.at[x], dst.at[x], out_sems.at[i, x])

    for x in range(planes):
        for i in range(3):
            copy(i, x).start()
    sums[...] = jnp.zeros_like(sums)
    fx[...] = jnp.zeros_like(fx)
    cx[...] = jnp.zeros_like(cx)
    copy(0, 0).wait()
    copy(1, 0).wait()
    sub = lax.broadcasted_iota(jnp.int32, (STRIP, cols), 0)
    sub0, sub1 = sub == 0, sub == STRIP - 1

    def plane(x, carry):
        @pl.when(x < planes - 1)
        def _():
            copy(0, x + 1).wait()
            copy(1, x + 1).wait()

        copy(2, x).wait()
        xn = jnp.minimum(x + 1, planes - 1)
        h_next = jnp.where(x < planes - 1, 0.5, 0.0).astype(F32)
        dc = df = 0.0
        k0, v0 = k[x, sl[0], :], v[x, sl[0], :]
        ku, vu = upward(k0), upward(v0)
        res_sum = k_sum = None
        for r, a in enumerate(sl):
            c_z = 0.5 * (k0 + left(k0))
            f_z = c_z * (v0 - left(v0))
            diag = c_z + right(c_z)
            res = right(f_z) - f_z
            if r + 1 < n:
                k1, v1 = k[x, sl[r + 1], :], v[x, sl[r + 1], :]
                ku1, vu1 = upward(k1), upward(v1)
                c_y = 0.5 * (k0 + jnp.where(sub1, ku1, ku))
                f_y = c_y * (v0 - jnp.where(sub1, vu1, vu))
            else:
                c_y = jnp.where(sub1, 0.0, 0.5 * (k0 + ku))
                f_y = c_y * (v0 - vu)
            nc, nf = downward(c_y), downward(f_y)
            diag = diag + (c_y + jnp.where(sub0, dc, nc))
            res = res + (jnp.where(sub0, df, nf) - f_y)
            dc, df = nc, nf
            c_x = h_next * (k0 + k[xn, a, :])
            f_x = c_x * (v0 - v[xn, a, :])
            diag = diag + ((cx[a, :] + c_x) + REACTION)
            res = res + ((fx[a, :] - f_x) + (s[x, a, :] - REACTION * v0))
            cx[a, :] = c_x
            fx[a, :] = f_x
            w = DAMPING / diag
            w_ref[x, a, :] = w
            f_ref[x, a, :] = w * res
            half = r * STRIP // F
            res_sum = res if r * STRIP % F == 0 else res_sum + res
            k_sum = k0 if r * STRIP % F == 0 else k_sum + k0
            if (r + 1) * STRIP % F == 0:
                sums[half * STRIP : (half + 1) * STRIP, :] += res_sum
                sums[(2 + half) * STRIP : (3 + half) * STRIP, :] += k_sum
            if r + 1 < n:
                k0, v0, ku, vu = k1, v1, ku1, vu1
        out_copy(0, x).start()
        out_copy(1, x).start()
        for place, y in ((low, 0), (high, rows - 1)):
            w_row[place, pl.ds(x, 1), :] = w_ref[x, y : y + 1, :]
            f_row[place, pl.ds(x, 1), :] = f_ref[x, y : y + 1, :]
        return carry

    lax.fori_loop(0, planes, plane, 0)
    for side, x in enumerate(edge_spots("gx", planes)):
        w_pl[side] = w_ref[x]
        f_pl[side] = f_ref[x]
    for x in range(planes):
        for i in range(2):
            out_copy(i, x).wait()


def cross(q_pl, q_row, pls, rws, sign):
    rows, planes = q_pl.shape[1], q_row.shape[1]
    for a in range(2):
        pls[a][...] = pls[a][...] + sign * q_pl[a]
        rws[a][...] = rws[a][...] + sign * q_row[a]
    for a, x in enumerate(edge_spots("gx", planes)):
        for b, y in enumerate(edge_spots("gy", rows)):
            px, py = pl.ds(x, 1), pl.ds(y, 1)
            pls[a][py, :] = pls[a][py, :] + sign * q_row[b, px, :]
            rws[b][px, :] = rws[b][px, :] + sign * q_pl[a, py, :]


def split3(a):
    one = a.astype(BF16)
    rest = a - one.astype(F32)
    two = rest.astype(BF16)
    three = (rest - two.astype(F32)).astype(BF16)
    return jnp.concatenate([one, two, three], 0)


def joined3(a):
    n = a.shape[0] // 3
    return a[:n] + a[n : 2 * n] + a[2 * n :]


def edge_kernel(
    wi_pl, fi_pl, wi_row, fi_row, pl_a, pl_b, rw_a, rw_b, xa, xb, ya, yb, sums,
    f_pl0, f_pl1, f_row0, f_row1, w_pl0, w_pl1, w_row0, w_row1, wc_pl, wc_row, payload,
    q_pl, q_row,
):
    rows, cols = f_pl0.shape
    f_pl, f_row, w_pl, w_row = (f_pl0, f_pl1), (f_row0, f_row1), (w_pl0, w_pl1), (w_row0, w_row1)
    for side, mine, other in ((0, pl_a, xa), (1, pl_b, xb)):
        c = 0.5 * (mine[1] + other[1])
        wc_pl[side] = c
        q_pl[side] = c * (mine[0] - other[0])
    for side, mine, other in ((0, rw_a, ya), (1, rw_b, yb)):
        c = 0.5 * (mine[1] + other[1])
        wc_row[side] = c
        q_row[side] = c * (mine[0] - other[0])
    for w, f, wi, fi in ((w_pl, f_pl, wi_pl, fi_pl), (w_row, f_row, wi_row, fi_row)):
        for side in range(2):
            diag = DAMPING / wi[side]
            w[side][...] = diag
            f[side][...] = fi[side] * (diag * (1.0 / DAMPING))
    cross(wc_pl, wc_row, w_pl, w_row, 1.0)
    cross(q_pl, q_row, f_pl, f_row, -1.0)
    for w, f, wc in ((w_pl, f_pl, wc_pl), (w_row, f_row, wc_row)):
        for side in range(2):
            inv = DAMPING / w[side][...]
            w[side][...] = inv
            f[side][...] = f[side][...] * inv
            wc[side] = wc[side] * inv
    low, high = low_high("gy")
    parts = []
    for half in range(rows // F):
        total = sums[half * STRIP : (half + 1) * STRIP, :]
        for side in range(2):
            for r in range(half * F // STRIP, (half + 1) * F // STRIP):
                total = total - q_pl[side, r * STRIP : (r + 1) * STRIP, :]
        if half == 0:
            for r in range(q_row.shape[1] // STRIP):
                total = total - q_row[low, r * STRIP : (r + 1) * STRIP, :]
        if half == rows // F - 1:
            for r in range(q_row.shape[1] // STRIP):
                total = total - q_row[high, r * STRIP : (r + 1) * STRIP, :]
        parts.append(total)
    parts.append(sums[2 * STRIP :, :])
    col = lax.broadcasted_iota(jnp.int32, (cols, cols // F), 0)
    cell = lax.broadcasted_iota(jnp.int32, (cols, cols // F), 1)
    gather = jnp.where(col // F == cell, 1.0, 0.0).astype(BF16)
    reduced = joined3(
        jnp.dot(split3(jnp.concatenate(parts, 0)), gather, preferred_element_type=F32)
    )
    means = [
        jnp.sum(reduced[i * STRIP : (i + 1) * STRIP], axis=0, keepdims=True) * (1.0 / F**3)
        for i in range(4)
    ]
    tile = jnp.concatenate(means + means, 0)
    for i in range(payload.shape[0] // STRIP):
        payload[i * STRIP : (i + 1) * STRIP, :] = tile


def put_edges(ref, x, e_pl0, e_pl1, e_row0, e_row1):
    planes, rows, _ = ref.shape
    for y, line in zip(edge_spots("gy", rows), (e_row0, e_row1)):
        ref[x, pl.ds(y, 1), :] = line[pl.ds(x, 1), :]
    for spot, plane in zip(edge_spots("gx", planes), (e_pl0, e_pl1)):

        @pl.when(x == spot)
        def _():
            ref[x] = plane[...]


def shifted_up(rolled, r):
    nxt = rolled[min(r + 1, len(rolled) - 1)]
    sub = lax.broadcasted_iota(jnp.int32, nxt.shape, 0)
    return jnp.where(sub == STRIP - 1, nxt, rolled[r])


def shifted_down(rolled, r):
    prv = rolled[r - 1]
    sub = lax.broadcasted_iota(jnp.int32, prv.shape, 0)
    return jnp.where(sub == 0, prv, rolled[r])


def up_coupling(k0, k_up, r):
    c = 0.5 * (k0[r] + shifted_up(k_up, r))
    if r == len(k0) - 1:
        sub = lax.broadcasted_iota(jnp.int32, c.shape, 0)
        c = jnp.where(sub == STRIP - 1, 0.0, c)
    return c


def neighbour_sums(x, u, cx, cy, cz):
    planes, rows, _ = u.shape
    sl = strips(rows)
    xn, xp = jnp.minimum(x + 1, planes - 1), jnp.maximum(x - 1, 0)
    u0 = [u[x, a, :] for a in sl]
    u_up = [pltpu.roll(a, STRIP - 1, 0) for a in u0]
    c_y = [cy[x, a, :] for a in sl]
    q_dn = [pltpu.roll(c * a, 1, 0) for c, a in zip(c_y, u0)]
    for r, a in enumerate(sl):
        c_z = cz[x, a, :]
        total = (
            (cx[x + 1, a, :] * u[xn, a, :] + cx[x, a, :] * u[xp, a, :])
            + (c_y[r] * shifted_up(u_up, r) + shifted_down(q_dn, r))
            + (c_z * left(u0[r]) + right(c_z * u0[r]))
        )
        yield r, a, u0[r], total


def sweep_kernel(
    k_hbm, w_hbm, f_hbm, w_pl0, w_pl1, w_row0, w_row1, f_pl0, f_pl1, f_row0, f_row1,
    w, f, cx_hbm, cy, cz, g_ref, g_pl, g_row, k, cx, sems, out_sems,
):
    planes, rows, cols = w.shape
    sl = strips(rows)
    low, high = low_high("gy")

    def out_copy(x):
        return pltpu.make_async_copy(cx.at[x], cx_hbm.at[x], out_sems.at[x])

    def copy(i, x):
        src, dst = ((k_hbm, k), (f_hbm, f), (w_hbm, w))[i]
        return pltpu.make_async_copy(src.at[x], dst.at[x], sems.at[i, x])

    def arrive(x):
        for i in range(3):
            copy(i, x).wait()
        put_edges(f, x, f_pl0, f_pl1, f_row0, f_row1)
        put_edges(w, x, w_pl0, w_pl1, w_row0, w_row1)

    for x in range(planes):
        for i in range(3):
            copy(i, x).start()
    cx[0] = jnp.zeros_like(k[0])
    out_copy(0).start()
    arrive(0)

    def plane(x, carry):
        @pl.when(x < planes - 1)
        def _():
            arrive(x + 1)

        xn = jnp.minimum(x + 1, planes - 1)
        h_next = jnp.where(x < planes - 1, 0.5, 0.0).astype(F32)
        k0 = [k[x, a, :] for a in sl]
        k_up = [pltpu.roll(a, STRIP - 1, 0) for a in k0]
        for r, a in enumerate(sl):
            cx[x + 1, a, :] = h_next * (k0[r] + k[xn, a, :])
            cy[x, a, :] = up_coupling(k0, k_up, r)
            cz[x, a, :] = 0.5 * (k0[r] + left(k0[r]))
        for r, a, u0, total in neighbour_sums(x, f, cx, cy, cz):
            new = (2.0 - DAMPING) * u0 + w[x, a, :] * total
            g_ref[x, a, :] = new
            if r == 0:
                g_row[low, pl.ds(x, 1), :] = new[0:1]
            if (r + 1) * STRIP == rows:
                g_row[high, pl.ds(x, 1), :] = new[STRIP - 1 :]
        out_copy(x + 1).start()
        return carry

    lax.fori_loop(0, planes, plane, 0)
    for side, x in enumerate(edge_spots("gx", planes)):
        g_pl[side] = g_ref[x]
    for x in range(planes + 1):
        out_copy(x).wait()


def mid_kernel(
    g_pl, g_row, wc_pl, wc_row, xa, xb, ya, yb, o_pl0, o_pl1, o_row0, o_row1, q_pl, q_row
):
    for side, x, y in ((0, xa, ya), (1, xb, yb)):
        q_pl[side] = wc_pl[side] * x[...]
        q_row[side] = wc_row[side] * y[...]
    for side, p, r in ((0, o_pl0, o_row0), (1, o_pl1, o_row1)):
        p[...] = g_pl[side]
        r[...] = g_row[side]
    cross(q_pl, q_row, (o_pl0, o_pl1), (o_row0, o_row1), 1.0)


def tile_sums(x, u, cx, cy, cz):
    planes, rows, cols = u.shape
    sl = strips(rows)
    tl = [slice(j, j + LANES) for j in range(0, cols, LANES)]
    lane = lax.broadcasted_iota(jnp.int32, (STRIP, LANES), 1)
    sub = lax.broadcasted_iota(jnp.int32, (STRIP, LANES), 0)
    xn, xp = jnp.minimum(x + 1, planes - 1), jnp.maximum(x - 1, 0)
    ru = [left(u[x, a, tl[0]]) for a in sl]
    pm = [right(cz[x, a, tl[-1]] * u[x, a, tl[-1]]) for a in sl]
    for j, t in enumerate(tl):
        us = [u[x, a, t] for a in sl]
        uu = [upward(a) for a in us]
        dn = 0.0
        for r, a in enumerate(sl):
            u0, c_y, c_z = us[r], cy[x, a, t], cz[x, a, t]
            nu = left(u[x, a, tl[(j + 1) % len(tl)]])
            total = cx[x + 1, a, t] * u[xn, a, t] + cx[x, a, t] * u[xp, a, t]
            total = total + c_z * jnp.where(lane == LANES - 1, nu, ru[r])
            mu = right(c_z * u0)
            total = total + jnp.where(lane == 0, pm[r], mu)
            ru[r], pm[r] = nu, mu
            above = jnp.where(sub == STRIP - 1, uu[r + 1], uu[r]) if r + 1 < len(sl) else uu[r]
            nd = downward(c_y * u0)
            total = total + (c_y * above + jnp.where(sub == 0, dn, nd))
            dn = nd
            yield a, t, u0, total


def last_kernel(
    w, f, cx_hbm, cy, cz, g_any, interp, g_pl0, g_pl1, g_row0, g_row1,
    out, body, g, cx, in_sems, cx_sems, sems,
):
    planes, rows, cols = w.shape

    def in_copy(x):
        return pltpu.make_async_copy(g_any.at[x], g.at[x], in_sems.at[x])

    def copy(x):
        return pltpu.make_async_copy(
            body.at[x, STRIP : rows - STRIP, :], out.at[x, STRIP : rows - STRIP, :], sems.at[x]
        )

    def cx_copy(x):
        return pltpu.make_async_copy(cx_hbm.at[x], cx.at[x], cx_sems.at[x])

    def arrive(x):
        cx_copy(x + 1).wait()
        in_copy(x).wait()
        put_edges(g, x, g_pl0, g_pl1, g_row0, g_row1)

    cx_copy(0).start()
    for x in range(planes):
        in_copy(x).start()
        cx_copy(x + 1).start()
    cx_copy(0).wait()
    arrive(0)

    def plane(x, carry):
        @pl.when(x < planes - 1)
        def _():
            arrive(x + 1)

        offset = ((x % F).astype(F32) + 0.5) / F - 0.5
        weight = jnp.abs(offset)
        side = jnp.where(offset > 0, 2, 0)
        for a, t, u0, total in tile_sums(x, g, cx, cy, cz):
            coarse = (1.0 - weight) * interp[1, a, t] + weight * interp[side, a, t]
            new = f[x, a, t] + (1.0 - DAMPING) * u0 + coarse
            body[x, a, t] = new + w[x, a, t] * total

        @pl.when((x > 0) & (x < planes - 1))
        def _():
            copy(x).start()

        return carry

    lax.fori_loop(0, planes, plane, 0)
    for x in range(1, planes - 1):
        copy(x).wait()


def finish_kernel(
    src, body, wc_pl, wc_row, xa, xb, ya, yb, out, s_pl, s_lo, s_hi, q_row, sems
):
    del src
    planes, rows, cols = out.shape
    xs, ys = edge_spots("gx", planes), edge_spots("gy", rows)
    low, high = low_high("gy")
    spots = (
        (s_lo, out.at[1 : planes - 1, 0:STRIP, :]),
        (s_hi, out.at[1 : planes - 1, rows - STRIP : rows, :]),
        (s_pl.at[0], out.at[xs[0]]),
        (s_pl.at[1], out.at[xs[1]]),
    )
    copies = [pltpu.make_async_copy(a, b, sems.at[i]) for i, (a, b) in enumerate(spots)]
    sub = lax.broadcasted_iota(jnp.int32, (STRIP, cols), 0)
    q_row[0] = wc_row[0] * ya[...]
    q_row[1] = wc_row[1] * yb[...]
    for x in range(1, planes - 1):
        q = q_row[low, x : x + 1, :]
        s_lo[x - 1] = body[x, :STRIP, :] + jnp.where(sub == 0, q, 0.0)
    copies[0].start()
    for x in range(1, planes - 1):
        q = q_row[high, x : x + 1, :]
        s_hi[x - 1] = body[x, rows - STRIP :, :] + jnp.where(sub == STRIP - 1, q, 0.0)
    copies[1].start()
    for side, other in ((0, xa), (1, xb)):
        x = xs[side]
        s_pl[side] = body[x] + wc_pl[side] * other[...]
        for b, y in enumerate(ys):
            py = pl.ds(y, 1)
            s_pl[side, py, :] = s_pl[side, py, :] + q_row[b, pl.ds(x, 1), :]
        copies[2 + side].start()
    for c in copies:
        c.wait()


def coarse_kernel(got, interp, coef, b_ref, u_ref, *, nx, ny, rows):
    nz = got.shape[1]
    per = 2 * 2

    def field(start):
        return [
            jnp.stack([got[pl.ds(p * ny * per + start + t, ny, stride=per), :] for p in range(nx)], 0)
            for t in range(2)
        ]

    resid, cond = field(0), field(2)

    def beside(a, t):
        mine = a[t]
        nxt = jnp.concatenate([mine[1:], mine[:1]], 0)
        prv = jnp.concatenate([mine[-1:], mine[:-1]], 0)
        up = a[1] if t == 0 else pltpu.roll(a[0], ny - 1, 1)
        down = a[0] if t == 1 else pltpu.roll(a[1], 1, 1)
        return nxt, prv, up, down, pltpu.roll(mine, 1, 2), pltpu.roll(mine, nz - 1, 2)

    for t in range(2):
        cs = [(0.5 * COARSE_FACTOR) * (cond[t] + other) for other in beside(cond, t)]
        diag = REACTION
        for c in cs:
            diag = diag + c
        inv = DAMPING / diag
        for i, c in enumerate(cs):
            coef[i, t] = inv * c
        b_ref[t] = inv * resid[t]
        u_ref[0, t] = b_ref[t]

    def sweep(src, dst):
        for p in range(nx):
            pn, pp = (p + 1) % nx, (p - 1) % nx
            u = [u_ref[src, t, p] for t in range(2)]
            for t in range(2):
                up = u[1] if t == 0 else pltpu.roll(u[0], ny - 1, 0)
                down = u[0] if t == 1 else pltpu.roll(u[1], 1, 0)
                a = b_ref[t, p] + (1.0 - DAMPING) * u[t]
                a = a + coef[0, t, p] * u_ref[src, t, pn]
                a = a + coef[1, t, p] * u_ref[src, t, pp]
                c = coef[2, t, p] * up + coef[3, t, p] * down
                c = c + coef[4, t, p] * pltpu.roll(u[t], 1, 1)
                c = c + coef[5, t, p] * pltpu.roll(u[t], nz - 1, 1)
                u_ref[dst, t, p] = a + c

    def pair(i, carry):
        sweep(0, 1)
        sweep(1, 0)
        return carry

    steps = CSWEEPS - 1
    lax.fori_loop(0, steps // 2, pair, 0)
    last = 0
    if steps % 2:
        sweep(0, 1)
        last = 1

    gx, gy = lax.axis_index("gx"), lax.axis_index("gy")
    lines = []
    for d in (-1, 0, 1):
        p = lax.rem(gx + d + nx, nx)
        prev_s, next_s = lax.rem(gy + ny - 1, ny), lax.rem(gy + 1, ny)
        for t, s in ((1, prev_s), (0, gy), (1, gy), (0, next_s)):
            lines.append(u_ref[last, t, p, pl.ds(s, 1), :])
    lines = jnp.concatenate(lines + lines[:4], 0)
    cols = nz * F
    cell = lax.broadcasted_iota(jnp.int32, (nz, cols), 0)
    col = lax.broadcasted_iota(jnp.int32, (nz, cols), 1)
    base = col // F
    offset = ((col % F).astype(F32) + 0.5) / F - 0.5
    side = jnp.where(offset > 0, base + 1, base - 1)
    side = jnp.where(side < 0, side + nz, jnp.where(side >= nz, side - nz, side))
    weight = jnp.abs(offset)
    matrix = jnp.where(cell == base, 1.0 - weight, 0.0) + jnp.where(cell == side, weight, 0.0)
    wide = joined3(jnp.dot(split3(lines), matrix.astype(BF16), preferred_element_type=F32))
    sub = lax.broadcasted_iota(jnp.int32, (STRIP, cols), 0)
    for plane in range(3):
        for r in range(rows // STRIP):
            row = r * STRIP + sub
            off = ((row % F).astype(F32) + 0.5) / F - 0.5
            wt = jnp.abs(off)
            block = r * STRIP // F
            near = block + 1
            far = near + (1 if (r * STRIP) % F >= F // 2 else -1)
            a = wide[plane * 4 + near : plane * 4 + near + 1]
            c = wide[plane * 4 + far : plane * 4 + far + 1]
            interp[plane, r * STRIP : (r + 1) * STRIP, :] = (1.0 - wt) * a + wt * c


def swap(axis, first, second):
    count = lax.axis_size(axis)
    pairs = [(i, i ^ 1) for i in range(count)]
    others = [(i, (i + 1 if i % 2 else i - 1) % count) for i in range(count)]
    return lax.ppermute(first, axis, pairs), lax.ppermute(second, axis, others)


def per_device(nx, ny, v, s, k):
    planes, rows, cols = v.shape
    n = planes * rows * cols
    vm = pltpu.VMEM
    dma = pltpu.SemaphoreType.DMA
    full, edge, line = sds(planes, rows, cols), sds(rows, cols), sds(planes, cols)
    edges, lines = sds(2, rows, cols), sds(2, planes, cols)

    rw_a, rw_b, pl_a, pl_b = pl.pallas_call(
        ends_kernel,
        out_shape=(lines, lines, edges, edges),
        in_specs=[HBM] * 2,
        out_specs=(VM,) * 4,
        scratch_shapes=[dma((2, 4))],
        compiler_params=params(58),
        cost_estimate=cost(0, n // 2),
        name="ends",
    )(v, k)
    ya, yb = swap("gy", rw_a, rw_b)
    xa, xb = swap("gx", pl_a, pl_b)

    w, f, wi_pl, fi_pl, wi_row, fi_row, sums = pl.pallas_call(
        inner_kernel,
        out_shape=(full, full, edges, edges, lines, lines, sds(4 * STRIP, cols)),
        in_specs=[HBM] * 3,
        out_specs=(HBM,) * 2 + (VM,) * 5,
        scratch_shapes=[vm(full.shape, F32)] * 5
        + [vm(edge.shape, F32)] * 2
        + [dma((3, planes)), dma((2, planes))],
        compiler_params=params(52),
        cost_estimate=cost(50 * n, 20 * n),
        name="inner",
    )(v, s, k)

    devices = nx * ny
    out = pl.pallas_call(
        edge_kernel,
        out_shape=(edge, edge, line, line) * 2 + (edges, lines, sds(devices * 4, cols // F)),
        in_specs=[VM] * 13,
        out_specs=(VM,) * 11,
        scratch_shapes=[vm(edges.shape, F32), vm(lines.shape, F32)],
        compiler_params=params(6),
        cost_estimate=cost(10 * n // 8, n),
        name="edge",
    )(wi_pl, fi_pl, wi_row, fi_row, pl_a, pl_b, rw_a, rw_b, xa, xb, ya, yb, sums)
    f_edges, w_edges, (wc_pl, wc_row, payload) = out[:4], out[4:8], out[8:]

    fya, fyb = swap("gy", f_edges[2], f_edges[3])
    fxa, fxb = swap("gx", f_edges[0], f_edges[1])
    got = lax.all_to_all(payload, ("gx", "gy"), 0, 0, tiled=True)

    got, w, f, k = lax.optimization_barrier((got, w, f, k))

    w, f, cx, cy, cz, g, g_pl, g_row = pl.pallas_call(
        sweep_kernel,
        out_shape=(full, full, sds(planes + 1, rows, cols), full, full, full, edges, lines),
        in_specs=[HBM] * 3 + [VM] * 8,
        out_specs=(VM, VM, HBM) + (VM,) * 5,
        scratch_shapes=[
            vm(full.shape, F32),
            vm((planes + 1, rows, cols), F32),
            dma((3, planes)),
            dma((planes + 1,)),
        ],
        compiler_params=params(30),
        cost_estimate=cost(40 * n, 12 * n),
        name="sweep",
    )(k, w, f, *w_edges, *f_edges)

    g_edges = pl.pallas_call(
        mid_kernel,
        out_shape=(edge, edge, line, line),
        in_specs=[VM] * 8,
        out_specs=(VM,) * 4,
        scratch_shapes=[vm(edges.shape, F32), vm(lines.shape, F32)],
        compiler_params=params(4),
        cost_estimate=cost(n // 8, n // 2),
        name="mid",
    )(g_pl, g_row, wc_pl, wc_row, fxa, fxb, fya, fyb)

    gya, gyb = swap("gy", g_edges[2], g_edges[3])
    gxa, gxb = swap("gx", g_edges[0], g_edges[1])

    cells = (nx, ny, cols // F)
    interp = pl.pallas_call(
        functools.partial(coarse_kernel, nx=nx, ny=ny, rows=rows),
        out_shape=sds(3, rows, cols),
        in_specs=[VM],
        out_specs=VM,
        scratch_shapes=[
            vm((6, 2) + cells, F32),
            vm((2,) + cells, F32),
            vm((2, 2) + cells, F32),
        ],
        compiler_params=params(8),
        cost_estimate=cost(20 * n, n),
        name="coarse",
    )(got)

    b_side = sds(planes - 2, STRIP, cols)
    out, body = pl.pallas_call(
        last_kernel,
        out_shape=(full, full),
        in_specs=[VM] * 2 + [HBM] + [VM] * 2 + [ANY] + [VM] * 5,
        out_specs=(HBM, VM),
        scratch_shapes=[
            vm(full.shape, F32),
            vm((planes + 1, rows, cols), F32),
            dma((planes,)),
            dma((planes + 1,)),
            dma((planes,)),
        ],
        compiler_params=params(27),
        cost_estimate=cost(40 * n, 20 * n),
        name="last",
    )(w, f, cx, cy, cz, g, interp, *g_edges)

    b_side = (planes - 2, STRIP, cols)
    return pl.pallas_call(
        finish_kernel,
        out_shape=full,
        in_specs=[HBM] + [VM] * 7,
        out_specs=HBM,
        scratch_shapes=[
            vm(edges.shape, F32), vm(b_side, F32), vm(b_side, F32), vm(lines.shape, F32), dma((4,)),
        ],
        input_output_aliases={0: 0},
        compiler_params=params(6),
        cost_estimate=cost(n // 4, 3 * n),
        name="finish",
    )(out, body, wc_pl, wc_row, gxa, gxb, gya, gyb)


def solution(mesh):
    placed = P("gx", "gy", None)
    body = functools.partial(per_device, mesh.shape["gx"], mesh.shape["gy"])
    return jax.shard_map(
        body, mesh=mesh, in_specs=(placed,) * 3, out_specs=placed, check_vma=False
    )
```

```python
import functools
import jax
import jax.numpy as jnp
from jax import lax
from jax.experimental import pallas as pl
from jax.experimental.pallas import tpu as pltpu
from jax.sharding import PartitionSpec as P

F = 16
CSWEEPS = 32
REACTION = 0.2
DAMPING = 0.8
COARSE_FACTOR = 0.25
F32 = jnp.float32
BF16 = jnp.bfloat16
STRIP = 8
LANES = 512

VM = pl.BlockSpec(memory_space=pltpu.VMEM)
ANY = pl.BlockSpec(memory_space=pl.ANY)
HBM = pl.BlockSpec(memory_space=pltpu.HBM)


def params(mib):
    return pltpu.CompilerParams(vmem_limit_bytes=mib * 1024 * 1024)


def cost(flops, nbytes):
    return pl.CostEstimate(flops=int(flops), bytes_accessed=int(nbytes), transcendentals=0)


def sds(*shape):
    return jax.ShapeDtypeStruct(shape, F32)


def left(a):
    return pltpu.roll(a, a.shape[1] - 1, 1)


def right(a):
    return pltpu.roll(a, 1, 1)


def upward(a):
    return pltpu.roll(a, STRIP - 1, 0)


def downward(a):
    return pltpu.roll(a, 1, 0)


def strips(rows):
    return [slice(r * STRIP, (r + 1) * STRIP) for r in range(rows // STRIP)]


def edge_spots(axis, count):
    odd = lax.rem(lax.axis_index(axis), 2)
    return (1 - odd) * (count - 1), odd * (count - 1)


def low_high(axis):
    odd = lax.rem(lax.axis_index(axis), 2)
    return 1 - odd, odd


def ends_kernel(v, k, rw_a, rw_b, pl_a, pl_b, sems):
    planes, rows, _ = v.shape
    xs, ys = edge_spots("gx", planes), edge_spots("gy", rows)
    copies = []
    for i, a in enumerate((v, k)):
        for j, (src, dst) in enumerate(
            (
                (a.at[:, ys[0], :], rw_a.at[i]),
                (a.at[:, ys[1], :], rw_b.at[i]),
                (a.at[xs[0]], pl_a.at[i]),
                (a.at[xs[1]], pl_b.at[i]),
            )
        ):
            copies.append(pltpu.make_async_copy(src, dst, sems.at[i, j]))
    for c in copies:
        c.start()
    for c in copies:
        c.wait()


def inner_kernel(
    v_hbm, s_hbm, k_hbm,
    w_hbm, f_hbm, w_pl, f_pl, w_row, f_row, sums,
    v, s, k, w_ref, f_ref, cx, fx, sems, out_sems,
):
    planes, rows, cols = v.shape
    sl = strips(rows)
    n = len(sl)
    low, high = low_high("gy")

    def copy(i, x):
        src, dst = ((k_hbm, k), (v_hbm, v), (s_hbm, s))[i]
        return pltpu.make_async_copy(src.at[x], dst.at[x], sems.at[i, x])

    def out_copy(i, x):
        src, dst = ((w_ref, w_hbm), (f_ref, f_hbm))[i]
        return pltpu.make_async_copy(src.at[x], dst.at[x], out_sems.at[i, x])

    for x in range(planes):
        for i in range(3):
            copy(i, x).start()
    sums[...] = jnp.zeros_like(sums)
    fx[...] = jnp.zeros_like(fx)
    cx[...] = jnp.zeros_like(cx)
    copy(0, 0).wait()
    copy(1, 0).wait()
    sub = lax.broadcasted_iota(jnp.int32, (STRIP, cols), 0)
    sub0, sub1 = sub == 0, sub == STRIP - 1

    def plane(x, carry):
        @pl.when(x < planes - 1)
        def _():
            copy(0, x + 1).wait()
            copy(1, x + 1).wait()

        copy(2, x).wait()
        xn = jnp.minimum(x + 1, planes - 1)
        h_next = jnp.where(x < planes - 1, 0.5, 0.0).astype(F32)
        dc = df = 0.0
        k0, v0 = k[x, sl[0], :], v[x, sl[0], :]
        ku, vu = upward(k0), upward(v0)
        res_sum = k_sum = None
        for r, a in enumerate(sl):
            c_z = 0.5 * (k0 + left(k0))
            f_z = c_z * (v0 - left(v0))
            diag = c_z + right(c_z)
            res = right(f_z) - f_z
            if r + 1 < n:
                k1, v1 = k[x, sl[r + 1], :], v[x, sl[r + 1], :]
                ku1, vu1 = upward(k1), upward(v1)
                c_y = 0.5 * (k0 + jnp.where(sub1, ku1, ku))
                f_y = c_y * (v0 - jnp.where(sub1, vu1, vu))
            else:
                c_y = jnp.where(sub1, 0.0, 0.5 * (k0 + ku))
                f_y = c_y * (v0 - vu)
            nc, nf = downward(c_y), downward(f_y)
            diag = diag + (c_y + jnp.where(sub0, dc, nc))
            res = res + (jnp.where(sub0, df, nf) - f_y)
            dc, df = nc, nf
            c_x = h_next * (k0 + k[xn, a, :])
            f_x = c_x * (v0 - v[xn, a, :])
            diag = diag + ((cx[a, :] + c_x) + REACTION)
            res = res + ((fx[a, :] - f_x) + (s[x, a, :] - REACTION * v0))
            cx[a, :] = c_x
            fx[a, :] = f_x
            w = DAMPING / diag
            w_ref[x, a, :] = w
            f_ref[x, a, :] = w * res
            half = r * STRIP // F
            res_sum = res if r * STRIP % F == 0 else res_sum + res
            k_sum = k0 if r * STRIP % F == 0 else k_sum + k0
            if (r + 1) * STRIP % F == 0:
                sums[half * STRIP : (half + 1) * STRIP, :] += res_sum
                sums[(2 + half) * STRIP : (3 + half) * STRIP, :] += k_sum
            if r + 1 < n:
                k0, v0, ku, vu = k1, v1, ku1, vu1
        out_copy(0, x).start()
        out_copy(1, x).start()
        for place, y in ((low, 0), (high, rows - 1)):
            w_row[place, pl.ds(x, 1), :] = w_ref[x, y : y + 1, :]
            f_row[place, pl.ds(x, 1), :] = f_ref[x, y : y + 1, :]
        return carry

    lax.fori_loop(0, planes, plane, 0)
    for side, x in enumerate(edge_spots("gx", planes)):
        w_pl[side] = w_ref[x]
        f_pl[side] = f_ref[x]
    for x in range(planes):
        for i in range(2):
            out_copy(i, x).wait()


def cross(q_pl, q_row, pls, rws, sign):
    rows, planes = q_pl.shape[1], q_row.shape[1]
    for a in range(2):
        pls[a][...] = pls[a][...] + sign * q_pl[a]
        rws[a][...] = rws[a][...] + sign * q_row[a]
    for a, x in enumerate(edge_spots("gx", planes)):
        for b, y in enumerate(edge_spots("gy", rows)):
            px, py = pl.ds(x, 1), pl.ds(y, 1)
            pls[a][py, :] = pls[a][py, :] + sign * q_row[b, px, :]
            rws[b][px, :] = rws[b][px, :] + sign * q_pl[a, py, :]


def split3(a):
    one = a.astype(BF16)
    rest = a - one.astype(F32)
    two = rest.astype(BF16)
    three = (rest - two.astype(F32)).astype(BF16)
    return jnp.concatenate([one, two, three], 0)


def joined3(a):
    n = a.shape[0] // 3
    return a[:n] + a[n : 2 * n] + a[2 * n :]


def edge_kernel(
    wi_pl, fi_pl, wi_row, fi_row, pl_a, pl_b, rw_a, rw_b, xa, xb, ya, yb, sums,
    f_pl0, f_pl1, f_row0, f_row1, w_pl0, w_pl1, w_row0, w_row1, wc_pl, wc_row, payload,
    q_pl, q_row,
):
    rows, cols = f_pl0.shape
    f_pl, f_row, w_pl, w_row = (f_pl0, f_pl1), (f_row0, f_row1), (w_pl0, w_pl1), (w_row0, w_row1)
    for side, mine, other in ((0, pl_a, xa), (1, pl_b, xb)):
        c = 0.5 * (mine[1] + other[1])
        wc_pl[side] = c
        q_pl[side] = c * (mine[0] - other[0])
    for side, mine, other in ((0, rw_a, ya), (1, rw_b, yb)):
        c = 0.5 * (mine[1] + other[1])
        wc_row[side] = c
        q_row[side] = c * (mine[0] - other[0])
    for w, f, wi, fi in ((w_pl, f_pl, wi_pl, fi_pl), (w_row, f_row, wi_row, fi_row)):
        for side in range(2):
            diag = DAMPING / wi[side]
            w[side][...] = diag
            f[side][...] = fi[side] * (diag * (1.0 / DAMPING))
    cross(wc_pl, wc_row, w_pl, w_row, 1.0)
    cross(q_pl, q_row, f_pl, f_row, -1.0)
    for w, f, wc in ((w_pl, f_pl, wc_pl), (w_row, f_row, wc_row)):
        for side in range(2):
            inv = DAMPING / w[side][...]
            w[side][...] = inv
            f[side][...] = f[side][...] * inv
            wc[side] = wc[side] * inv
    low, high = low_high("gy")
    parts = []
    for half in range(rows // F):
        total = sums[half * STRIP : (half + 1) * STRIP, :]
        for side in range(2):
            for r in range(half * F // STRIP, (half + 1) * F // STRIP):
                total = total - q_pl[side, r * STRIP : (r + 1) * STRIP, :]
        if half == 0:
            for r in range(q_row.shape[1] // STRIP):
                total = total - q_row[low, r * STRIP : (r + 1) * STRIP, :]
        if half == rows // F - 1:
            for r in range(q_row.shape[1] // STRIP):
                total = total - q_row[high, r * STRIP : (r + 1) * STRIP, :]
        parts.append(total)
    parts.append(sums[2 * STRIP :, :])
    col = lax.broadcasted_iota(jnp.int32, (cols, cols // F), 0)
    cell = lax.broadcasted_iota(jnp.int32, (cols, cols // F), 1)
    gather = jnp.where(col // F == cell, 1.0, 0.0).astype(BF16)
    reduced = joined3(
        jnp.dot(split3(jnp.concatenate(parts, 0)), gather, preferred_element_type=F32)
    )
    means = [
        jnp.sum(reduced[i * STRIP : (i + 1) * STRIP], axis=0, keepdims=True) * (1.0 / F**3)
        for i in range(4)
    ]
    tile = jnp.concatenate(means + means, 0)
    for i in range(payload.shape[0] // STRIP):
        payload[i * STRIP : (i + 1) * STRIP, :] = tile


def put_edges(ref, x, e_pl0, e_pl1, e_row0, e_row1):
    planes, rows, _ = ref.shape
    for y, line in zip(edge_spots("gy", rows), (e_row0, e_row1)):
        ref[x, pl.ds(y, 1), :] = line[pl.ds(x, 1), :]
    for spot, plane in zip(edge_spots("gx", planes), (e_pl0, e_pl1)):

        @pl.when(x == spot)
        def _():
            ref[x] = plane[...]


def sweep_kernel(
    k_hbm, w_hbm, f_hbm, w_pl0, w_pl1, w_row0, w_row1, f_pl0, f_pl1, f_row0, f_row1,
    w, f, k, cy, cz, g_ref, g_pl, g_row, cx, sems,
):
    planes, rows, cols = w.shape
    sl = strips(rows)
    low, high = low_high("gy")
    sub = lax.broadcasted_iota(jnp.int32, (STRIP, cols), 0)
    sub0, sub1 = sub == 0, sub == STRIP - 1

    def copy(i, x):
        src, dst = ((k_hbm, k), (f_hbm, f), (w_hbm, w))[i]
        return pltpu.make_async_copy(src.at[x], dst.at[x], sems.at[i, x])

    def arrive(x):
        for i in range(3):
            copy(i, x).wait()
        put_edges(f, x, f_pl0, f_pl1, f_row0, f_row1)
        put_edges(w, x, w_pl0, w_pl1, w_row0, w_row1)

    for x in range(planes):
        for i in range(3):
            copy(i, x).start()
    cx[...] = jnp.zeros_like(cx)
    arrive(0)

    def plane(x, carry):
        @pl.when(x < planes - 1)
        def _():
            arrive(x + 1)

        xn = jnp.minimum(x + 1, planes - 1)
        h_next = jnp.where(x < planes - 1, 0.5, 0.0).astype(F32)
        xp = jnp.maximum(x - 1, 0)
        dn = 0.0
        k0, u0 = k[x, sl[0], :], f[x, sl[0], :]
        ku, uu = upward(k0), upward(u0)
        for r, a in enumerate(sl):
            c_z = 0.5 * (k0 + left(k0))
            total = c_z * left(u0) + right(c_z * u0)
            if r + 1 < len(sl):
                k1, u1 = k[x, sl[r + 1], :], f[x, sl[r + 1], :]
                ku1, uu1 = upward(k1), upward(u1)
                c_y = 0.5 * (k0 + jnp.where(sub1, ku1, ku))
                above = jnp.where(sub1, uu1, uu)
            else:
                c_y = jnp.where(sub1, 0.0, 0.5 * (k0 + ku))
                above = uu
            nd = downward(c_y * u0)
            total = total + (c_y * above + jnp.where(sub0, dn, nd))
            dn = nd
            c_x = h_next * (k0 + k[xn, a, :])
            total = total + (c_x * f[xn, a, :] + cx[a, :] * f[xp, a, :])
            cx[a, :] = c_x
            cy[x, a, :] = c_y
            cz[x, a, :] = c_z
            g_ref[x, a, :] = (2.0 - DAMPING) * u0 + w[x, a, :] * total
            if r + 1 < len(sl):
                k0, u0, ku, uu = k1, u1, ku1, uu1
        for place, y in ((low, 0), (high, rows - 1)):
            g_row[place, pl.ds(x, 1), :] = g_ref[x, y : y + 1, :]
        return carry

    lax.fori_loop(0, planes, plane, 0)
    for side, x in enumerate(edge_spots("gx", planes)):
        g_pl[side] = g_ref[x]


def mid_kernel(
    g_pl, g_row, wc_pl, wc_row, xa, xb, ya, yb, o_pl0, o_pl1, o_row0, o_row1, q_pl, q_row
):
    for side, x, y in ((0, xa, ya), (1, xb, yb)):
        q_pl[side] = wc_pl[side] * x[...]
        q_row[side] = wc_row[side] * y[...]
    for side, p, r in ((0, o_pl0, o_row0), (1, o_pl1, o_row1)):
        p[...] = g_pl[side]
        r[...] = g_row[side]
    cross(q_pl, q_row, (o_pl0, o_pl1), (o_row0, o_row1), 1.0)


def tile_sums(x, u, k, cx, cy, cz):
    planes, rows, cols = u.shape
    sl = strips(rows)
    tl = [slice(j, j + LANES) for j in range(0, cols, LANES)]
    lane = lax.broadcasted_iota(jnp.int32, (STRIP, LANES), 1)
    sub = lax.broadcasted_iota(jnp.int32, (STRIP, LANES), 0)
    xn, xp = jnp.minimum(x + 1, planes - 1), jnp.maximum(x - 1, 0)
    h_next = jnp.where(x < planes - 1, 0.5, 0.0).astype(F32)
    ru = [left(u[x, a, tl[0]]) for a in sl]
    pm = [right(cz[x, a, tl[-1]] * u[x, a, tl[-1]]) for a in sl]
    for j, t in enumerate(tl):
        us = [u[x, a, t] for a in sl]
        uu = [upward(a) for a in us]
        dn = 0.0
        for r, a in enumerate(sl):
            u0, c_y, c_z = us[r], cy[x, a, t], cz[x, a, t]
            nu = left(u[x, a, tl[(j + 1) % len(tl)]])
            c_x = h_next * (k[x, a, t] + k[xn, a, t])
            total = c_x * u[xn, a, t] + cx[a, t] * u[xp, a, t]
            cx[a, t] = c_x
            total = total + c_z * jnp.where(lane == LANES - 1, nu, ru[r])
            mu = right(c_z * u0)
            total = total + jnp.where(lane == 0, pm[r], mu)
            ru[r], pm[r] = nu, mu
            above = jnp.where(sub == STRIP - 1, uu[r + 1], uu[r]) if r + 1 < len(sl) else uu[r]
            nd = downward(c_y * u0)
            total = total + (c_y * above + jnp.where(sub == 0, dn, nd))
            dn = nd
            yield a, t, u0, total


def last_kernel(
    w, f, k, cy, cz, g_in, interp, g_pl0, g_pl1, g_row0, g_row1,
    out, body, g, cx, sems,
):
    planes, rows, cols = w.shape

    def copy(x):
        return pltpu.make_async_copy(
            body.at[x, STRIP : rows - STRIP, :], out.at[x, STRIP : rows - STRIP, :], sems.at[x]
        )

    def arrive(x):
        g[x] = g_in[x]
        put_edges(g, x, g_pl0, g_pl1, g_row0, g_row1)

    cx[...] = jnp.zeros_like(cx)
    arrive(0)

    def plane(x, carry):
        @pl.when(x < planes - 1)
        def _():
            arrive(x + 1)

        offset = ((x % F).astype(F32) + 0.5) / F - 0.5
        weight = jnp.abs(offset)
        side = jnp.where(offset > 0, 2, 0)
        for a, t, u0, total in tile_sums(x, g, k, cx, cy, cz):
            coarse = (1.0 - weight) * interp[1, a, t] + weight * interp[side, a, t]
            new = f[x, a, t] + (1.0 - DAMPING) * u0 + coarse
            body[x, a, t] = new + w[x, a, t] * total

        @pl.when((x > 0) & (x < planes - 1))
        def _():
            copy(x).start()

        return carry

    lax.fori_loop(0, planes, plane, 0)
    for x in range(1, planes - 1):
        copy(x).wait()


def finish_kernel(
    src, body, wc_pl, wc_row, xa, xb, ya, yb, out, s_pl, s_lo, s_hi, q_row, sems
):
    del src
    planes, rows, cols = out.shape
    xs, ys = edge_spots("gx", planes), edge_spots("gy", rows)
    low, high = low_high("gy")
    spots = (
        (s_lo, out.at[1 : planes - 1, 0:STRIP, :]),
        (s_hi, out.at[1 : planes - 1, rows - STRIP : rows, :]),
        (s_pl.at[0], out.at[xs[0]]),
        (s_pl.at[1], out.at[xs[1]]),
    )
    copies = [pltpu.make_async_copy(a, b, sems.at[i]) for i, (a, b) in enumerate(spots)]
    sub = lax.broadcasted_iota(jnp.int32, (STRIP, cols), 0)
    q_row[0] = wc_row[0] * ya[...]
    q_row[1] = wc_row[1] * yb[...]
    for x in range(1, planes - 1):
        q = q_row[low, x : x + 1, :]
        s_lo[x - 1] = body[x, :STRIP, :] + jnp.where(sub == 0, q, 0.0)
    copies[0].start()
    for x in range(1, planes - 1):
        q = q_row[high, x : x + 1, :]
        s_hi[x - 1] = body[x, rows - STRIP :, :] + jnp.where(sub == STRIP - 1, q, 0.0)
    copies[1].start()
    for side, other in ((0, xa), (1, xb)):
        x = xs[side]
        s_pl[side] = body[x] + wc_pl[side] * other[...]
        for b, y in enumerate(ys):
            py = pl.ds(y, 1)
            s_pl[side, py, :] = s_pl[side, py, :] + q_row[b, pl.ds(x, 1), :]
        copies[2 + side].start()
    for c in copies:
        c.wait()


def coarse_kernel(got, interp, coef, b_ref, u_ref, *, nx, ny, rows):
    nz = got.shape[1]
    per = 2 * 2

    def field(start):
        return [
            jnp.stack([got[pl.ds(p * ny * per + start + t, ny, stride=per), :] for p in range(nx)], 0)
            for t in range(2)
        ]

    resid, cond = field(0), field(2)

    def beside(a, t):
        mine = a[t]
        nxt = jnp.concatenate([mine[1:], mine[:1]], 0)
        prv = jnp.concatenate([mine[-1:], mine[:-1]], 0)
        up = a[1] if t == 0 else pltpu.roll(a[0], ny - 1, 1)
        down = a[0] if t == 1 else pltpu.roll(a[1], 1, 1)
        return nxt, prv, up, down, pltpu.roll(mine, 1, 2), pltpu.roll(mine, nz - 1, 2)

    for t in range(2):
        cs = [(0.5 * COARSE_FACTOR) * (cond[t] + other) for other in beside(cond, t)]
        diag = REACTION
        for c in cs:
            diag = diag + c
        inv = DAMPING / diag
        for i, c in enumerate(cs):
            coef[i, t] = inv * c
        b_ref[t] = inv * resid[t]
        u_ref[0, t] = b_ref[t]

    def sweep(src, dst):
        for p in range(nx):
            pn, pp = (p + 1) % nx, (p - 1) % nx
            u = [u_ref[src, t, p] for t in range(2)]
            for t in range(2):
                up = u[1] if t == 0 else pltpu.roll(u[0], ny - 1, 0)
                down = u[0] if t == 1 else pltpu.roll(u[1], 1, 0)
                a = b_ref[t, p] + (1.0 - DAMPING) * u[t]
                a = a + coef[0, t, p] * u_ref[src, t, pn]
                a = a + coef[1, t, p] * u_ref[src, t, pp]
                c = coef[2, t, p] * up + coef[3, t, p] * down
                c = c + coef[4, t, p] * pltpu.roll(u[t], 1, 1)
                c = c + coef[5, t, p] * pltpu.roll(u[t], nz - 1, 1)
                u_ref[dst, t, p] = a + c

    def pair(i, carry):
        sweep(0, 1)
        sweep(1, 0)
        return carry

    steps = CSWEEPS - 1
    lax.fori_loop(0, steps // 2, pair, 0)
    last = 0
    if steps % 2:
        sweep(0, 1)
        last = 1

    gx, gy = lax.axis_index("gx"), lax.axis_index("gy")
    lines = []
    for d in (-1, 0, 1):
        p = lax.rem(gx + d + nx, nx)
        prev_s, next_s = lax.rem(gy + ny - 1, ny), lax.rem(gy + 1, ny)
        for t, s in ((1, prev_s), (0, gy), (1, gy), (0, next_s)):
            lines.append(u_ref[last, t, p, pl.ds(s, 1), :])
    lines = jnp.concatenate(lines + lines[:4], 0)
    cols = nz * F
    cell = lax.broadcasted_iota(jnp.int32, (nz, cols), 0)
    col = lax.broadcasted_iota(jnp.int32, (nz, cols), 1)
    base = col // F
    offset = ((col % F).astype(F32) + 0.5) / F - 0.5
    side = jnp.where(offset > 0, base + 1, base - 1)
    side = jnp.where(side < 0, side + nz, jnp.where(side >= nz, side - nz, side))
    weight = jnp.abs(offset)
    matrix = jnp.where(cell == base, 1.0 - weight, 0.0) + jnp.where(cell == side, weight, 0.0)
    wide = joined3(jnp.dot(split3(lines), matrix.astype(BF16), preferred_element_type=F32))
    sub = lax.broadcasted_iota(jnp.int32, (STRIP, cols), 0)
    for plane in range(3):
        for r in range(rows // STRIP):
            row = r * STRIP + sub
            off = ((row % F).astype(F32) + 0.5) / F - 0.5
            wt = jnp.abs(off)
            block = r * STRIP // F
            near = block + 1
            far = near + (1 if (r * STRIP) % F >= F // 2 else -1)
            a = wide[plane * 4 + near : plane * 4 + near + 1]
            c = wide[plane * 4 + far : plane * 4 + far + 1]
            interp[plane, r * STRIP : (r + 1) * STRIP, :] = (1.0 - wt) * a + wt * c


def swap(axis, first, second):
    count = lax.axis_size(axis)
    pairs = [(i, i ^ 1) for i in range(count)]
    others = [(i, (i + 1 if i % 2 else i - 1) % count) for i in range(count)]
    return lax.ppermute(first, axis, pairs), lax.ppermute(second, axis, others)


def per_device(nx, ny, v, s, k):
    planes, rows, cols = v.shape
    n = planes * rows * cols
    vm = pltpu.VMEM
    dma = pltpu.SemaphoreType.DMA
    full, edge, line = sds(planes, rows, cols), sds(rows, cols), sds(planes, cols)
    edges, lines = sds(2, rows, cols), sds(2, planes, cols)

    rw_a, rw_b, pl_a, pl_b = pl.pallas_call(
        ends_kernel,
        out_shape=(lines, lines, edges, edges),
        in_specs=[HBM] * 2,
        out_specs=(VM,) * 4,
        scratch_shapes=[dma((2, 4))],
        compiler_params=params(58),
        cost_estimate=cost(0, n // 2),
        name="ends",
    )(v, k)
    ya, yb = swap("gy", rw_a, rw_b)
    xa, xb = swap("gx", pl_a, pl_b)

    w, f, wi_pl, fi_pl, wi_row, fi_row, sums = pl.pallas_call(
        inner_kernel,
        out_shape=(full, full, edges, edges, lines, lines, sds(4 * STRIP, cols)),
        in_specs=[HBM] * 3,
        out_specs=(HBM,) * 2 + (VM,) * 5,
        scratch_shapes=[vm(full.shape, F32)] * 5
        + [vm(edge.shape, F32)] * 2
        + [dma((3, planes)), dma((2, planes))],
        compiler_params=params(52),
        cost_estimate=cost(50 * n, 20 * n),
        name="inner",
    )(v, s, k)

    devices = nx * ny
    out = pl.pallas_call(
        edge_kernel,
        out_shape=(edge, edge, line, line) * 2 + (edges, lines, sds(devices * 4, cols // F)),
        in_specs=[VM] * 13,
        out_specs=(VM,) * 11,
        scratch_shapes=[vm(edges.shape, F32), vm(lines.shape, F32)],
        compiler_params=params(6),
        cost_estimate=cost(10 * n // 8, n),
        name="edge",
    )(wi_pl, fi_pl, wi_row, fi_row, pl_a, pl_b, rw_a, rw_b, xa, xb, ya, yb, sums)
    f_edges, w_edges, (wc_pl, wc_row, payload) = out[:4], out[4:8], out[8:]

    fya, fyb = swap("gy", f_edges[2], f_edges[3])
    fxa, fxb = swap("gx", f_edges[0], f_edges[1])
    got = lax.all_to_all(payload, ("gx", "gy"), 0, 0, tiled=True)

    got, w, f, k = lax.optimization_barrier((got, w, f, k))

    w, f, k, cy, cz, g, g_pl, g_row = pl.pallas_call(
        sweep_kernel,
        out_shape=(full,) * 6 + (edges, lines),
        in_specs=[HBM] * 3 + [VM] * 8,
        out_specs=(VM,) * 8,
        scratch_shapes=[vm(edge.shape, F32), dma((3, planes))],
        compiler_params=params(33),
        cost_estimate=cost(40 * n, 12 * n),
        name="sweep",
    )(k, w, f, *w_edges, *f_edges)

    g_edges = pl.pallas_call(
        mid_kernel,
        out_shape=(edge, edge, line, line),
        in_specs=[VM] * 8,
        out_specs=(VM,) * 4,
        scratch_shapes=[vm(edges.shape, F32), vm(lines.shape, F32)],
        compiler_params=params(4),
        cost_estimate=cost(n // 8, n // 2),
        name="mid",
    )(g_pl, g_row, wc_pl, wc_row, fxa, fxb, fya, fyb)

    gya, gyb = swap("gy", g_edges[2], g_edges[3])
    gxa, gxb = swap("gx", g_edges[0], g_edges[1])

    cells = (nx, ny, cols // F)
    interp = pl.pallas_call(
        functools.partial(coarse_kernel, nx=nx, ny=ny, rows=rows),
        out_shape=sds(3, rows, cols),
        in_specs=[VM],
        out_specs=VM,
        scratch_shapes=[
            vm((6, 2) + cells, F32),
            vm((2,) + cells, F32),
            vm((2, 2) + cells, F32),
        ],
        compiler_params=params(8),
        cost_estimate=cost(20 * n, n),
        name="coarse",
    )(got)

    b_side = sds(planes - 2, STRIP, cols)
    out, body = pl.pallas_call(
        last_kernel,
        out_shape=(full, full),
        in_specs=[VM] * 11,
        out_specs=(HBM, VM),
        scratch_shapes=[vm(full.shape, F32), vm(edge.shape, F32), dma((planes,))],
        compiler_params=params(31),
        cost_estimate=cost(40 * n, 20 * n),
        name="last",
    )(w, f, k, cy, cz, g, interp, *g_edges)

    b_side = (planes - 2, STRIP, cols)
    return pl.pallas_call(
        finish_kernel,
        out_shape=full,
        in_specs=[HBM] + [VM] * 7,
        out_specs=HBM,
        scratch_shapes=[
            vm(edges.shape, F32), vm(b_side, F32), vm(b_side, F32), vm(lines.shape, F32), dma((4,)),
        ],
        input_output_aliases={0: 0},
        compiler_params=params(6),
        cost_estimate=cost(n // 4, 3 * n),
        name="finish",
    )(out, body, wc_pl, wc_row, gxa, gxb, gya, gyb)


def solution(mesh):
    placed = P("gx", "gy", None)
    body = functools.partial(per_device, mesh.shape["gx"], mesh.shape["gy"])
    return jax.shard_map(
        body, mesh=mesh, in_specs=(placed,) * 3, out_specs=placed, check_vma=False
    )
```

```python
import functools
import jax
import jax.numpy as jnp
from jax import lax
from jax.experimental import pallas as pl
from jax.experimental.pallas import tpu as pltpu
from jax.sharding import PartitionSpec as P

F = 16
CSWEEPS = 32
REACTION = 0.2
DAMPING = 0.8
COARSE_FACTOR = 0.25
F32 = jnp.float32
BF16 = jnp.bfloat16
STRIP = 8
LANES = 512

VM = pl.BlockSpec(memory_space=pltpu.VMEM)
ANY = pl.BlockSpec(memory_space=pl.ANY)
HBM = pl.BlockSpec(memory_space=pltpu.HBM)


def params(mib):
    return pltpu.CompilerParams(vmem_limit_bytes=mib * 1024 * 1024)


def cost(flops, nbytes):
    return pl.CostEstimate(flops=int(flops), bytes_accessed=int(nbytes), transcendentals=0)


def sds(*shape):
    return jax.ShapeDtypeStruct(shape, F32)


def left(a):
    return pltpu.roll(a, a.shape[1] - 1, 1)


def right(a):
    return pltpu.roll(a, 1, 1)


def upward(a):
    return pltpu.roll(a, STRIP - 1, 0)


def downward(a):
    return pltpu.roll(a, 1, 0)


def strips(rows):
    return [slice(r * STRIP, (r + 1) * STRIP) for r in range(rows // STRIP)]


def edge_spots(axis, count):
    odd = lax.rem(lax.axis_index(axis), 2)
    return (1 - odd) * (count - 1), odd * (count - 1)


def low_high(axis):
    odd = lax.rem(lax.axis_index(axis), 2)
    return 1 - odd, odd


def planes_kernel(v, k, pl_a, pl_b, sems):
    copies = [
        pltpu.make_async_copy(src.at[x], dst.at[i], sems.at[i, j])
        for i, src in enumerate((v, k))
        for j, (x, dst) in enumerate(zip(edge_spots("gx", v.shape[0]), (pl_a, pl_b)))
    ]
    for c in copies:
        c.start()
    for c in copies:
        c.wait()


def rows_kernel(v, k, rw_a, rw_b, sems):
    copies = [
        pltpu.make_async_copy(src.at[:, y, :], dst.at[i], sems.at[i, j])
        for i, src in enumerate((v, k))
        for j, (y, dst) in enumerate(zip(edge_spots("gy", v.shape[1]), (rw_a, rw_b)))
    ]
    for c in copies:
        c.start()
    for c in copies:
        c.wait()


def inner_kernel(
    v_hbm, s_hbm, k_hbm,
    w_hbm, f_hbm, w_pl, f_pl, w_row, f_row, sums,
    v, s, k, w_ref, f_ref, sems, out_sems,
):
    planes, rows, cols = v.shape
    sl = strips(rows)
    n = len(sl)
    low, high = low_high("gy")

    def copy(i, x):
        src, dst = ((k_hbm, k), (v_hbm, v), (s_hbm, s))[i]
        return pltpu.make_async_copy(src.at[x], dst.at[x], sems.at[i, x])

    def out_copy(i, x):
        src, dst = ((w_ref, w_hbm), (f_ref, f_hbm))[i]
        return pltpu.make_async_copy(src.at[x], dst.at[x], out_sems.at[i, x])

    for x in range(planes):
        for i in range(3):
            copy(i, x).start()
    sums[...] = jnp.zeros_like(sums)
    copy(0, 0).wait()
    copy(1, 0).wait()
    sub = lax.broadcasted_iota(jnp.int32, (STRIP, cols), 0)
    sub0, sub1 = sub == 0, sub == STRIP - 1

    def plane(x, carry):
        @pl.when(x < planes - 1)
        def _():
            copy(0, x + 1).wait()
            copy(1, x + 1).wait()

        copy(2, x).wait()
        xn, xp = jnp.minimum(x + 1, planes - 1), jnp.maximum(x - 1, 0)
        h_prev = jnp.where(x > 0, 0.5, 0.0).astype(F32)
        h_next = jnp.where(x < planes - 1, 0.5, 0.0).astype(F32)
        dc = df = 0.0
        k0, v0 = k[x, sl[0], :], v[x, sl[0], :]
        ku, vu = upward(k0), upward(v0)
        res_sum = k_sum = None
        for r, a in enumerate(sl):
            c_z = 0.5 * (k0 + left(k0))
            f_z = c_z * (v0 - left(v0))
            diag = c_z + right(c_z)
            res = right(f_z) - f_z
            if r + 1 < n:
                k1, v1 = k[x, sl[r + 1], :], v[x, sl[r + 1], :]
                ku1, vu1 = upward(k1), upward(v1)
                c_y = 0.5 * (k0 + jnp.where(sub1, ku1, ku))
                f_y = c_y * (v0 - jnp.where(sub1, vu1, vu))
            else:
                c_y = jnp.where(sub1, 0.0, 0.5 * (k0 + ku))
                f_y = c_y * (v0 - vu)
            nc, nf = downward(c_y), downward(f_y)
            diag = diag + (c_y + jnp.where(sub0, dc, nc))
            res = res + (jnp.where(sub0, df, nf) - f_y)
            dc, df = nc, nf
            c_x = h_next * (k0 + k[xn, a, :])
            f_x = c_x * (v0 - v[xn, a, :])
            c_p = h_prev * (k0 + k[xp, a, :])
            f_p = c_p * (v[xp, a, :] - v0)
            diag = diag + ((c_p + c_x) + REACTION)
            res = res + ((f_p - f_x) + (s[x, a, :] - REACTION * v0))
            w = DAMPING / diag
            w_ref[x, a, :] = w
            f_ref[x, a, :] = w * res
            half = r * STRIP // F
            res_sum = res if r * STRIP % F == 0 else res_sum + res
            k_sum = k0 if r * STRIP % F == 0 else k_sum + k0
            if (r + 1) * STRIP % F == 0:
                sums[half * STRIP : (half + 1) * STRIP, :] += res_sum
                sums[(2 + half) * STRIP : (3 + half) * STRIP, :] += k_sum
            if r + 1 < n:
                k0, v0, ku, vu = k1, v1, ku1, vu1
        out_copy(0, x).start()
        out_copy(1, x).start()
        for place, y in ((low, 0), (high, rows - 1)):
            w_row[place, pl.ds(x, 1), :] = w_ref[x, y : y + 1, :]
            f_row[place, pl.ds(x, 1), :] = f_ref[x, y : y + 1, :]
        return carry

    lax.fori_loop(0, planes, plane, 0)
    for side, x in enumerate(edge_spots("gx", planes)):
        w_pl[side] = w_ref[x]
        f_pl[side] = f_ref[x]
    for x in range(planes):
        for i in range(2):
            out_copy(i, x).wait()


def cross(q_pl, q_row, pls, rws, sign):
    rows, planes = q_pl.shape[1], q_row.shape[1]
    for a in range(2):
        pls[a][...] = pls[a][...] + sign * q_pl[a]
        rws[a][...] = rws[a][...] + sign * q_row[a]
    for a, x in enumerate(edge_spots("gx", planes)):
        for b, y in enumerate(edge_spots("gy", rows)):
            px, py = pl.ds(x, 1), pl.ds(y, 1)
            pls[a][py, :] = pls[a][py, :] + sign * q_row[b, px, :]
            rws[b][px, :] = rws[b][px, :] + sign * q_pl[a, py, :]


def split3(a):
    one = a.astype(BF16)
    rest = a - one.astype(F32)
    two = rest.astype(BF16)
    three = (rest - two.astype(F32)).astype(BF16)
    return jnp.concatenate([one, two, three], 0)


def joined3(a):
    n = a.shape[0] // 3
    return a[:n] + a[n : 2 * n] + a[2 * n :]


def edge_kernel(
    wi_pl, fi_pl, wi_row, fi_row, pl_a, pl_b, rw_a, rw_b, xa, xb, ya, yb, sums,
    f_pl0, f_pl1, f_row0, f_row1, w_pl0, w_pl1, w_row0, w_row1, wc_pl, wc_row, payload,
    q_pl, q_row,
):
    rows, cols = f_pl0.shape
    f_pl, f_row, w_pl, w_row = (f_pl0, f_pl1), (f_row0, f_row1), (w_pl0, w_pl1), (w_row0, w_row1)
    for side, mine, other in ((0, pl_a, xa), (1, pl_b, xb)):
        c = 0.5 * (mine[1] + other[1])
        wc_pl[side] = c
        q_pl[side] = c * (mine[0] - other[0])
    for side, mine, other in ((0, rw_a, ya), (1, rw_b, yb)):
        c = 0.5 * (mine[1] + other[1])
        wc_row[side] = c
        q_row[side] = c * (mine[0] - other[0])
    for w, f, wi, fi in ((w_pl, f_pl, wi_pl, fi_pl), (w_row, f_row, wi_row, fi_row)):
        for side in range(2):
            diag = DAMPING / wi[side]
            w[side][...] = diag
            f[side][...] = fi[side] * (diag * (1.0 / DAMPING))
    cross(wc_pl, wc_row, w_pl, w_row, 1.0)
    cross(q_pl, q_row, f_pl, f_row, -1.0)
    for w, f, wc in ((w_pl, f_pl, wc_pl), (w_row, f_row, wc_row)):
        for side in range(2):
            inv = DAMPING / w[side][...]
            w[side][...] = inv
            f[side][...] = f[side][...] * inv
            wc[side] = wc[side] * inv
    low, high = low_high("gy")
    parts = []
    for half in range(rows // F):
        total = sums[half * STRIP : (half + 1) * STRIP, :]
        for side in range(2):
            for r in range(half * F // STRIP, (half + 1) * F // STRIP):
                total = total - q_pl[side, r * STRIP : (r + 1) * STRIP, :]
        if half == 0:
            for r in range(q_row.shape[1] // STRIP):
                total = total - q_row[low, r * STRIP : (r + 1) * STRIP, :]
        if half == rows // F - 1:
            for r in range(q_row.shape[1] // STRIP):
                total = total - q_row[high, r * STRIP : (r + 1) * STRIP, :]
        parts.append(total)
    parts.append(sums[2 * STRIP :, :])
    col = lax.broadcasted_iota(jnp.int32, (cols, cols // F), 0)
    cell = lax.broadcasted_iota(jnp.int32, (cols, cols // F), 1)
    gather = jnp.where(col // F == cell, 1.0, 0.0).astype(BF16)
    reduced = joined3(
        jnp.dot(split3(jnp.concatenate(parts, 0)), gather, preferred_element_type=F32)
    )
    means = [
        jnp.sum(reduced[i * STRIP : (i + 1) * STRIP], axis=0, keepdims=True) * (1.0 / F**3)
        for i in range(4)
    ]
    tile = jnp.concatenate(means + means, 0)
    for i in range(payload.shape[0] // STRIP):
        payload[i * STRIP : (i + 1) * STRIP, :] = tile


def put_edges(ref, x, e_pl0, e_pl1, e_row0, e_row1):
    planes, rows, _ = ref.shape
    for y, line in zip(edge_spots("gy", rows), (e_row0, e_row1)):
        ref[x, pl.ds(y, 1), :] = line[pl.ds(x, 1), :]
    for spot, plane in zip(edge_spots("gx", planes), (e_pl0, e_pl1)):

        @pl.when(x == spot)
        def _():
            ref[x] = plane[...]


def sweep_kernel(
    k_hbm, w_hbm, f_hbm, w_pl0, w_pl1, w_row0, w_row1, f_pl0, f_pl1, f_row0, f_row1,
    w, f, k, cy, cz, g_ref, g_pl, g_row, sems,
):
    planes, rows, cols = w.shape
    sl = strips(rows)
    low, high = low_high("gy")
    sub = lax.broadcasted_iota(jnp.int32, (STRIP, cols), 0)
    sub0, sub1 = sub == 0, sub == STRIP - 1

    def copy(i, x):
        src, dst = ((k_hbm, k), (f_hbm, f), (w_hbm, w))[i]
        return pltpu.make_async_copy(src.at[x], dst.at[x], sems.at[i, x])

    def arrive(x):
        for i in range(3):
            copy(i, x).wait()
        put_edges(f, x, f_pl0, f_pl1, f_row0, f_row1)
        put_edges(w, x, w_pl0, w_pl1, w_row0, w_row1)

    for x in range(planes):
        for i in range(3):
            copy(i, x).start()
    arrive(0)

    def plane(x, carry):
        @pl.when(x < planes - 1)
        def _():
            arrive(x + 1)

        xn = jnp.minimum(x + 1, planes - 1)
        h_next = jnp.where(x < planes - 1, 0.5, 0.0).astype(F32)
        h_prev = jnp.where(x > 0, 0.5, 0.0).astype(F32)
        xp = jnp.maximum(x - 1, 0)
        dn = 0.0
        k0, u0 = k[x, sl[0], :], f[x, sl[0], :]
        ku, uu = upward(k0), upward(u0)
        for r, a in enumerate(sl):
            c_z = 0.5 * (k0 + left(k0))
            total = c_z * left(u0) + right(c_z * u0)
            if r + 1 < len(sl):
                k1, u1 = k[x, sl[r + 1], :], f[x, sl[r + 1], :]
                ku1, uu1 = upward(k1), upward(u1)
                c_y = 0.5 * (k0 + jnp.where(sub1, ku1, ku))
                above = jnp.where(sub1, uu1, uu)
            else:
                c_y = jnp.where(sub1, 0.0, 0.5 * (k0 + ku))
                above = uu
            nd = downward(c_y * u0)
            total = total + (c_y * above + jnp.where(sub0, dn, nd))
            dn = nd
            c_x = h_next * (k0 + k[xn, a, :])
            c_p = h_prev * (k0 + k[xp, a, :])
            total = total + (c_x * f[xn, a, :] + c_p * f[xp, a, :])
            cy[x, a, :] = c_y
            cz[x, a, :] = c_z
            g_ref[x, a, :] = (2.0 - DAMPING) * u0 + w[x, a, :] * total
            if r + 1 < len(sl):
                k0, u0, ku, uu = k1, u1, ku1, uu1
        for place, y in ((low, 0), (high, rows - 1)):
            g_row[place, pl.ds(x, 1), :] = g_ref[x, y : y + 1, :]
        return carry

    lax.fori_loop(0, planes, plane, 0)
    for side, x in enumerate(edge_spots("gx", planes)):
        g_pl[side] = g_ref[x]


def mid_kernel(
    g_pl, g_row, wc_pl, wc_row, xa, xb, ya, yb, o_pl0, o_pl1, o_row0, o_row1, q_pl, q_row
):
    for side, x, y in ((0, xa, ya), (1, xb, yb)):
        q_pl[side] = wc_pl[side] * x[...]
        q_row[side] = wc_row[side] * y[...]
    for side, p, r in ((0, o_pl0, o_row0), (1, o_pl1, o_row1)):
        p[...] = g_pl[side]
        r[...] = g_row[side]
    cross(q_pl, q_row, (o_pl0, o_pl1), (o_row0, o_row1), 1.0)


def tile_sums(x, u, k, cy, cz):
    planes, rows, cols = u.shape
    sl = strips(rows)
    tl = [slice(j, j + LANES) for j in range(0, cols, LANES)]
    lane = lax.broadcasted_iota(jnp.int32, (STRIP, LANES), 1)
    sub = lax.broadcasted_iota(jnp.int32, (STRIP, LANES), 0)
    xn, xp = jnp.minimum(x + 1, planes - 1), jnp.maximum(x - 1, 0)
    h_next = jnp.where(x < planes - 1, 0.5, 0.0).astype(F32)
    h_prev = jnp.where(x > 0, 0.5, 0.0).astype(F32)
    ru = [left(u[x, a, tl[0]]) for a in sl]
    pm = [right(cz[x, a, tl[-1]] * u[x, a, tl[-1]]) for a in sl]
    for j, t in enumerate(tl):
        us = [u[x, a, t] for a in sl]
        uu = [upward(a) for a in us]
        dn = 0.0
        for r, a in enumerate(sl):
            u0, c_y, c_z = us[r], cy[x, a, t], cz[x, a, t]
            nu = left(u[x, a, tl[(j + 1) % len(tl)]])
            c_x = h_next * (k[x, a, t] + k[xn, a, t])
            c_p = h_prev * (k[x, a, t] + k[xp, a, t])
            total = c_x * u[xn, a, t] + c_p * u[xp, a, t]
            total = total + c_z * jnp.where(lane == LANES - 1, nu, ru[r])
            mu = right(c_z * u0)
            total = total + jnp.where(lane == 0, pm[r], mu)
            ru[r], pm[r] = nu, mu
            above = jnp.where(sub == STRIP - 1, uu[r + 1], uu[r]) if r + 1 < len(sl) else uu[r]
            nd = downward(c_y * u0)
            total = total + (c_y * above + jnp.where(sub == 0, dn, nd))
            dn = nd
            yield a, t, u0, total


def last_kernel(
    w, f, k, cy, cz, g_in, interp, g_pl0, g_pl1, g_row0, g_row1,
    out, body, g, sems,
):
    planes, rows, cols = w.shape

    def copy(x):
        return pltpu.make_async_copy(
            body.at[x, STRIP : rows - STRIP, :], out.at[x, STRIP : rows - STRIP, :], sems.at[x]
        )

    def arrive(x):
        g[x] = g_in[x]
        put_edges(g, x, g_pl0, g_pl1, g_row0, g_row1)

    arrive(0)

    def plane(x, carry):
        @pl.when(x < planes - 1)
        def _():
            arrive(x + 1)

        offset = ((x % F).astype(F32) + 0.5) / F - 0.5
        weight = jnp.abs(offset)
        side = jnp.where(offset > 0, 2, 0)
        for a, t, u0, total in tile_sums(x, g, k, cy, cz):
            coarse = (1.0 - weight) * interp[1, a, t] + weight * interp[side, a, t]
            new = f[x, a, t] + (1.0 - DAMPING) * u0 + coarse
            body[x, a, t] = new + w[x, a, t] * total

        @pl.when((x > 0) & (x < planes - 1))
        def _():
            copy(x).start()

        return carry

    lax.fori_loop(0, planes, plane, 0)
    for x in range(1, planes - 1):
        copy(x).wait()


def finish_kernel(
    src, body, wc_pl, wc_row, xa, xb, ya, yb, out, s_pl, s_lo, s_hi, q_row, sems
):
    del src
    planes, rows, cols = out.shape
    xs, ys = edge_spots("gx", planes), edge_spots("gy", rows)
    low, high = low_high("gy")
    spots = (
        (s_lo, out.at[1 : planes - 1, 0:STRIP, :]),
        (s_hi, out.at[1 : planes - 1, rows - STRIP : rows, :]),
        (s_pl.at[0], out.at[xs[0]]),
        (s_pl.at[1], out.at[xs[1]]),
    )
    copies = [pltpu.make_async_copy(a, b, sems.at[i]) for i, (a, b) in enumerate(spots)]
    sub = lax.broadcasted_iota(jnp.int32, (STRIP, cols), 0)
    q_row[0] = wc_row[0] * ya[...]
    q_row[1] = wc_row[1] * yb[...]
    for x in range(1, planes - 1):
        q = q_row[low, x : x + 1, :]
        s_lo[x - 1] = body[x, :STRIP, :] + jnp.where(sub == 0, q, 0.0)
    copies[0].start()
    for x in range(1, planes - 1):
        q = q_row[high, x : x + 1, :]
        s_hi[x - 1] = body[x, rows - STRIP :, :] + jnp.where(sub == STRIP - 1, q, 0.0)
    copies[1].start()
    for side, other in ((0, xa), (1, xb)):
        x = xs[side]
        s_pl[side] = body[x] + wc_pl[side] * other[...]
        for b, y in enumerate(ys):
            py = pl.ds(y, 1)
            s_pl[side, py, :] = s_pl[side, py, :] + q_row[b, pl.ds(x, 1), :]
        copies[2 + side].start()
    for c in copies:
        c.wait()


def coarse_kernel(got, interp, coef, b_ref, u_ref, *, nx, ny, rows):
    nz = got.shape[1]
    per = 2 * 2

    def field(start):
        return [
            jnp.stack([got[pl.ds(p * ny * per + start + t, ny, stride=per), :] for p in range(nx)], 0)
            for t in range(2)
        ]

    resid, cond = field(0), field(2)

    def beside(a, t):
        mine = a[t]
        nxt = jnp.concatenate([mine[1:], mine[:1]], 0)
        prv = jnp.concatenate([mine[-1:], mine[:-1]], 0)
        up = a[1] if t == 0 else pltpu.roll(a[0], ny - 1, 1)
        down = a[0] if t == 1 else pltpu.roll(a[1], 1, 1)
        return nxt, prv, up, down, pltpu.roll(mine, 1, 2), pltpu.roll(mine, nz - 1, 2)

    for t in range(2):
        cs = [(0.5 * COARSE_FACTOR) * (cond[t] + other) for other in beside(cond, t)]
        diag = REACTION
        for c in cs:
            diag = diag + c
        inv = DAMPING / diag
        for i, c in enumerate(cs):
            coef[i, t] = inv * c
        b_ref[t] = inv * resid[t]
        u_ref[0, t] = b_ref[t]

    def sweep(src, dst):
        for p in range(nx):
            pn, pp = (p + 1) % nx, (p - 1) % nx
            u = [u_ref[src, t, p] for t in range(2)]
            for t in range(2):
                up = u[1] if t == 0 else pltpu.roll(u[0], ny - 1, 0)
                down = u[0] if t == 1 else pltpu.roll(u[1], 1, 0)
                a = b_ref[t, p] + (1.0 - DAMPING) * u[t]
                a = a + coef[0, t, p] * u_ref[src, t, pn]
                a = a + coef[1, t, p] * u_ref[src, t, pp]
                c = coef[2, t, p] * up + coef[3, t, p] * down
                c = c + coef[4, t, p] * pltpu.roll(u[t], 1, 1)
                c = c + coef[5, t, p] * pltpu.roll(u[t], nz - 1, 1)
                u_ref[dst, t, p] = a + c

    def pair(i, carry):
        sweep(0, 1)
        sweep(1, 0)
        return carry

    steps = CSWEEPS - 1
    lax.fori_loop(0, steps // 2, pair, 0)
    last = 0
    if steps % 2:
        sweep(0, 1)
        last = 1

    gx, gy = lax.axis_index("gx"), lax.axis_index("gy")
    lines = []
    for d in (-1, 0, 1):
        p = lax.rem(gx + d + nx, nx)
        prev_s, next_s = lax.rem(gy + ny - 1, ny), lax.rem(gy + 1, ny)
        for t, s in ((1, prev_s), (0, gy), (1, gy), (0, next_s)):
            lines.append(u_ref[last, t, p, pl.ds(s, 1), :])
    lines = jnp.concatenate(lines + lines[:4], 0)
    cols = nz * F
    cell = lax.broadcasted_iota(jnp.int32, (nz, cols), 0)
    col = lax.broadcasted_iota(jnp.int32, (nz, cols), 1)
    base = col // F
    offset = ((col % F).astype(F32) + 0.5) / F - 0.5
    side = jnp.where(offset > 0, base + 1, base - 1)
    side = jnp.where(side < 0, side + nz, jnp.where(side >= nz, side - nz, side))
    weight = jnp.abs(offset)
    matrix = jnp.where(cell == base, 1.0 - weight, 0.0) + jnp.where(cell == side, weight, 0.0)
    wide = joined3(jnp.dot(split3(lines), matrix.astype(BF16), preferred_element_type=F32))
    sub = lax.broadcasted_iota(jnp.int32, (STRIP, cols), 0)
    for plane in range(3):
        for r in range(rows // STRIP):
            row = r * STRIP + sub
            off = ((row % F).astype(F32) + 0.5) / F - 0.5
            wt = jnp.abs(off)
            block = r * STRIP // F
            near = block + 1
            far = near + (1 if (r * STRIP) % F >= F // 2 else -1)
            a = wide[plane * 4 + near : plane * 4 + near + 1]
            c = wide[plane * 4 + far : plane * 4 + far + 1]
            interp[plane, r * STRIP : (r + 1) * STRIP, :] = (1.0 - wt) * a + wt * c


def swap(axis, first, second):
    count = lax.axis_size(axis)
    pairs = [(i, i ^ 1) for i in range(count)]
    others = [(i, (i + 1 if i % 2 else i - 1) % count) for i in range(count)]
    return lax.ppermute(first, axis, pairs), lax.ppermute(second, axis, others)


def per_device(nx, ny, v, s, k):
    planes, rows, cols = v.shape
    n = planes * rows * cols
    vm = pltpu.VMEM
    dma = pltpu.SemaphoreType.DMA
    full, edge, line = sds(planes, rows, cols), sds(rows, cols), sds(planes, cols)
    edges, lines = sds(2, rows, cols), sds(2, planes, cols)

    pl_a, pl_b = pl.pallas_call(
        planes_kernel,
        out_shape=(edges, edges),
        in_specs=[HBM] * 2,
        out_specs=(VM,) * 2,
        scratch_shapes=[dma((2, 2))],
        compiler_params=params(58),
        cost_estimate=cost(0, n // 4),
        name="planes",
    )(v, k)
    xa, xb = swap("gx", pl_a, pl_b)
    rw_a, rw_b = pl.pallas_call(
        rows_kernel,
        out_shape=(lines, lines),
        in_specs=[HBM] * 2,
        out_specs=(VM,) * 2,
        scratch_shapes=[dma((2, 2))],
        compiler_params=params(58),
        cost_estimate=cost(0, n // 4),
        name="rows",
    )(v, k)
    ya, yb = swap("gy", rw_a, rw_b)

    w, f, wi_pl, fi_pl, wi_row, fi_row, sums = pl.pallas_call(
        inner_kernel,
        out_shape=(full, full, edges, edges, lines, lines, sds(4 * STRIP, cols)),
        in_specs=[HBM] * 3,
        out_specs=(HBM,) * 2 + (VM,) * 5,
        scratch_shapes=[vm(full.shape, F32)] * 5
        + [dma((3, planes)), dma((2, planes))],
        compiler_params=params(52),
        cost_estimate=cost(50 * n, 20 * n),
        name="inner",
    )(v, s, k)

    devices = nx * ny
    out = pl.pallas_call(
        edge_kernel,
        out_shape=(edge, edge, line, line) * 2 + (edges, lines, sds(devices * 4, cols // F)),
        in_specs=[VM] * 13,
        out_specs=(VM,) * 11,
        scratch_shapes=[vm(edges.shape, F32), vm(lines.shape, F32)],
        compiler_params=params(6),
        cost_estimate=cost(10 * n // 8, n),
        name="edge",
    )(wi_pl, fi_pl, wi_row, fi_row, pl_a, pl_b, rw_a, rw_b, xa, xb, ya, yb, sums)
    f_edges, w_edges, (wc_pl, wc_row, payload) = out[:4], out[4:8], out[8:]

    fya, fyb = swap("gy", f_edges[2], f_edges[3])
    fxa, fxb = swap("gx", f_edges[0], f_edges[1])
    got = lax.all_to_all(payload, ("gx", "gy"), 0, 0, tiled=True)

    got, w, f, k = lax.optimization_barrier((got, w, f, k))

    w, f, k, cy, cz, g, g_pl, g_row = pl.pallas_call(
        sweep_kernel,
        out_shape=(full,) * 6 + (edges, lines),
        in_specs=[HBM] * 3 + [VM] * 8,
        out_specs=(VM,) * 8,
        scratch_shapes=[dma((3, planes))],
        compiler_params=params(26),
        cost_estimate=cost(40 * n, 12 * n),
        name="sweep",
    )(k, w, f, *w_edges, *f_edges)

    g_edges = pl.pallas_call(
        mid_kernel,
        out_shape=(edge, edge, line, line),
        in_specs=[VM] * 8,
        out_specs=(VM,) * 4,
        scratch_shapes=[vm(edges.shape, F32), vm(lines.shape, F32)],
        compiler_params=params(4),
        cost_estimate=cost(n // 8, n // 2),
        name="mid",
    )(g_pl, g_row, wc_pl, wc_row, fxa, fxb, fya, fyb)

    gya, gyb = swap("gy", g_edges[2], g_edges[3])
    gxa, gxb = swap("gx", g_edges[0], g_edges[1])

    cells = (nx, ny, cols // F)
    interp = pl.pallas_call(
        functools.partial(coarse_kernel, nx=nx, ny=ny, rows=rows),
        out_shape=sds(3, rows, cols),
        in_specs=[VM],
        out_specs=VM,
        scratch_shapes=[
            vm((6, 2) + cells, F32),
            vm((2,) + cells, F32),
            vm((2, 2) + cells, F32),
        ],
        compiler_params=params(8),
        cost_estimate=cost(20 * n, n),
        name="coarse",
    )(got)

    b_side = sds(planes - 2, STRIP, cols)
    out, body = pl.pallas_call(
        last_kernel,
        out_shape=(full, full),
        in_specs=[VM] * 11,
        out_specs=(HBM, VM),
        scratch_shapes=[vm(full.shape, F32), dma((planes,))],
        compiler_params=params(22),
        cost_estimate=cost(40 * n, 20 * n),
        name="last",
    )(w, f, k, cy, cz, g, interp, *g_edges)

    b_side = (planes - 2, STRIP, cols)
    return pl.pallas_call(
        finish_kernel,
        out_shape=full,
        in_specs=[HBM] + [VM] * 7,
        out_specs=HBM,
        scratch_shapes=[
            vm(edges.shape, F32), vm(b_side, F32), vm(b_side, F32), vm(lines.shape, F32), dma((4,)),
        ],
        input_output_aliases={0: 0},
        compiler_params=params(6),
        cost_estimate=cost(n // 4, 3 * n),
        name="finish",
    )(out, body, wc_pl, wc_row, gxa, gxb, gya, gyb)


def solution(mesh):
    placed = P("gx", "gy", None)
    body = functools.partial(per_device, mesh.shape["gx"], mesh.shape["gy"])
    return jax.shard_map(
        body, mesh=mesh, in_specs=(placed,) * 3, out_specs=placed, check_vma=False
    )
```

```python
import functools
import jax
import jax.numpy as jnp
from jax import lax
from jax.experimental import pallas as pl
from jax.experimental.pallas import tpu as pltpu
from jax.sharding import PartitionSpec as P

F = 16
CSWEEPS = 32
REACTION = 0.2
DAMPING = 0.8
COARSE_FACTOR = 0.25
F32 = jnp.float32
BF16 = jnp.bfloat16
STRIP = 8
LANES = 512

VM = pl.BlockSpec(memory_space=pltpu.VMEM)
ANY = pl.BlockSpec(memory_space=pl.ANY)
HBM = pl.BlockSpec(memory_space=pltpu.HBM)


def params(mib):
    return pltpu.CompilerParams(vmem_limit_bytes=mib * 1024 * 1024)


def cost(flops, nbytes):
    return pl.CostEstimate(flops=int(flops), bytes_accessed=int(nbytes), transcendentals=0)


def sds(*shape):
    return jax.ShapeDtypeStruct(shape, F32)


def left(a):
    return pltpu.roll(a, a.shape[1] - 1, 1)


def right(a):
    return pltpu.roll(a, 1, 1)


def upward(a):
    return pltpu.roll(a, STRIP - 1, 0)


def downward(a):
    return pltpu.roll(a, 1, 0)


def strips(rows):
    return [slice(r * STRIP, (r + 1) * STRIP) for r in range(rows // STRIP)]


def edge_spots(axis, count):
    odd = lax.rem(lax.axis_index(axis), 2)
    return (1 - odd) * (count - 1), odd * (count - 1)


def low_high(axis):
    odd = lax.rem(lax.axis_index(axis), 2)
    return 1 - odd, odd


def planes_kernel(v, k, pl_a, pl_b, sems):
    copies = [
        pltpu.make_async_copy(src.at[x], dst.at[i], sems.at[i, j])
        for i, src in enumerate((v, k))
        for j, (x, dst) in enumerate(zip(edge_spots("gx", v.shape[0]), (pl_a, pl_b)))
    ]
    for c in copies:
        c.start()
    for c in copies:
        c.wait()


def rows_kernel(v, k, rw_a, rw_b, sems):
    copies = [
        pltpu.make_async_copy(src.at[:, y, :], dst.at[i], sems.at[i, j])
        for i, src in enumerate((v, k))
        for j, (y, dst) in enumerate(zip(edge_spots("gy", v.shape[1]), (rw_a, rw_b)))
    ]
    for c in copies:
        c.start()
    for c in copies:
        c.wait()


def inner_kernel(
    v_hbm, s_hbm, k_hbm,
    w_hbm, f_hbm, w_pl, f_pl, w_row, f_row, sums,
    v, s, k, w_ref, f_ref, sems, out_sems,
):
    planes, rows, cols = v.shape
    sl = strips(rows)
    n = len(sl)
    low, high = low_high("gy")

    def copy(i, x):
        src, dst = ((k_hbm, k), (v_hbm, v), (s_hbm, s))[i]
        return pltpu.make_async_copy(src.at[x], dst.at[x], sems.at[i, x])

    def out_copy(i, x):
        src, dst = ((w_ref, w_hbm), (f_ref, f_hbm))[i]
        return pltpu.make_async_copy(src.at[x], dst.at[x], out_sems.at[i, x])

    for x in range(planes):
        for i in range(3):
            copy(i, x).start()
    sums[...] = jnp.zeros_like(sums)
    copy(0, 0).wait()
    copy(1, 0).wait()
    sub = lax.broadcasted_iota(jnp.int32, (STRIP, cols), 0)
    sub0, sub1 = sub == 0, sub == STRIP - 1

    def plane(x, carry):
        @pl.when(x < planes - 1)
        def _():
            copy(0, x + 1).wait()
            copy(1, x + 1).wait()

        copy(2, x).wait()
        xn, xp = jnp.minimum(x + 1, planes - 1), jnp.maximum(x - 1, 0)
        h_prev = jnp.where(x > 0, 0.5, 0.0).astype(F32)
        h_next = jnp.where(x < planes - 1, 0.5, 0.0).astype(F32)
        dc = df = 0.0
        k0, v0 = k[x, sl[0], :], v[x, sl[0], :]
        ku, vu = upward(k0), upward(v0)
        res_sum = k_sum = None
        for r, a in enumerate(sl):
            c_z = 0.5 * (k0 + left(k0))
            f_z = c_z * (v0 - left(v0))
            diag = c_z + right(c_z)
            res = right(f_z) - f_z
            if r + 1 < n:
                k1, v1 = k[x, sl[r + 1], :], v[x, sl[r + 1], :]
                ku1, vu1 = upward(k1), upward(v1)
                c_y = 0.5 * (k0 + jnp.where(sub1, ku1, ku))
                f_y = c_y * (v0 - jnp.where(sub1, vu1, vu))
            else:
                c_y = jnp.where(sub1, 0.0, 0.5 * (k0 + ku))
                f_y = c_y * (v0 - vu)
            nc, nf = downward(c_y), downward(f_y)
            diag = diag + (c_y + jnp.where(sub0, dc, nc))
            res = res + (jnp.where(sub0, df, nf) - f_y)
            dc, df = nc, nf
            c_x = h_next * (k0 + k[xn, a, :])
            f_x = c_x * (v0 - v[xn, a, :])
            c_p = h_prev * (k0 + k[xp, a, :])
            f_p = c_p * (v[xp, a, :] - v0)
            diag = diag + ((c_p + c_x) + REACTION)
            res = res + ((f_p - f_x) + (s[x, a, :] - REACTION * v0))
            w = DAMPING / diag
            w_ref[x, a, :] = w
            f_ref[x, a, :] = w * res
            half = r * STRIP // F
            res_sum = res if r * STRIP % F == 0 else res_sum + res
            k_sum = k0 if r * STRIP % F == 0 else k_sum + k0
            if (r + 1) * STRIP % F == 0:
                sums[half * STRIP : (half + 1) * STRIP, :] += res_sum
                sums[(2 + half) * STRIP : (3 + half) * STRIP, :] += k_sum
            if r + 1 < n:
                k0, v0, ku, vu = k1, v1, ku1, vu1
        out_copy(0, x).start()
        out_copy(1, x).start()
        for place, y in ((low, 0), (high, rows - 1)):
            w_row[place, pl.ds(x, 1), :] = w_ref[x, y : y + 1, :]
            f_row[place, pl.ds(x, 1), :] = f_ref[x, y : y + 1, :]
        return carry

    lax.fori_loop(0, planes, plane, 0)
    for side, x in enumerate(edge_spots("gx", planes)):
        w_pl[side] = w_ref[x]
        f_pl[side] = f_ref[x]
    for x in range(planes):
        for i in range(2):
            out_copy(i, x).wait()


def cross(q_pl, q_row, pls, rws, sign):
    rows, planes = q_pl.shape[1], q_row.shape[1]
    for a in range(2):
        pls[a][...] = pls[a][...] + sign * q_pl[a]
        rws[a][...] = rws[a][...] + sign * q_row[a]
    for a, x in enumerate(edge_spots("gx", planes)):
        for b, y in enumerate(edge_spots("gy", rows)):
            px, py = pl.ds(x, 1), pl.ds(y, 1)
            pls[a][py, :] = pls[a][py, :] + sign * q_row[b, px, :]
            rws[b][px, :] = rws[b][px, :] + sign * q_pl[a, py, :]


def split3(a):
    one = a.astype(BF16)
    rest = a - one.astype(F32)
    two = rest.astype(BF16)
    three = (rest - two.astype(F32)).astype(BF16)
    return jnp.concatenate([one, two, three], 0)


def joined3(a):
    n = a.shape[0] // 3
    return a[:n] + a[n : 2 * n] + a[2 * n :]


def edge_kernel(
    wi_pl, fi_pl, wi_row, fi_row, pl_a, pl_b, rw_a, rw_b, xa, xb, ya, yb, sums,
    f_pl0, f_pl1, f_row0, f_row1, w_pl0, w_pl1, w_row0, w_row1, wc_pl, wc_row, payload,
    q_pl, q_row,
):
    rows, cols = f_pl0.shape
    f_pl, f_row, w_pl, w_row = (f_pl0, f_pl1), (f_row0, f_row1), (w_pl0, w_pl1), (w_row0, w_row1)
    for side, mine, other in ((0, pl_a, xa), (1, pl_b, xb)):
        c = 0.5 * (mine[1] + other[1])
        wc_pl[side] = c
        q_pl[side] = c * (mine[0] - other[0])
    for side, mine, other in ((0, rw_a, ya), (1, rw_b, yb)):
        c = 0.5 * (mine[1] + other[1])
        wc_row[side] = c
        q_row[side] = c * (mine[0] - other[0])
    for w, f, wi, fi in ((w_pl, f_pl, wi_pl, fi_pl), (w_row, f_row, wi_row, fi_row)):
        for side in range(2):
            diag = DAMPING / wi[side]
            w[side][...] = diag
            f[side][...] = fi[side] * (diag * (1.0 / DAMPING))
    cross(wc_pl, wc_row, w_pl, w_row, 1.0)
    cross(q_pl, q_row, f_pl, f_row, -1.0)
    for w, f, wc in ((w_pl, f_pl, wc_pl), (w_row, f_row, wc_row)):
        for side in range(2):
            inv = DAMPING / w[side][...]
            w[side][...] = inv
            f[side][...] = f[side][...] * inv
            wc[side] = wc[side] * inv
    low, high = low_high("gy")
    parts = []
    for half in range(rows // F):
        total = sums[half * STRIP : (half + 1) * STRIP, :]
        for side in range(2):
            for r in range(half * F // STRIP, (half + 1) * F // STRIP):
                total = total - q_pl[side, r * STRIP : (r + 1) * STRIP, :]
        if half == 0:
            for r in range(q_row.shape[1] // STRIP):
                total = total - q_row[low, r * STRIP : (r + 1) * STRIP, :]
        if half == rows // F - 1:
            for r in range(q_row.shape[1] // STRIP):
                total = total - q_row[high, r * STRIP : (r + 1) * STRIP, :]
        parts.append(total)
    parts.append(sums[2 * STRIP :, :])
    col = lax.broadcasted_iota(jnp.int32, (cols, cols // F), 0)
    cell = lax.broadcasted_iota(jnp.int32, (cols, cols // F), 1)
    gather = jnp.where(col // F == cell, 1.0, 0.0).astype(BF16)
    reduced = joined3(
        jnp.dot(split3(jnp.concatenate(parts, 0)), gather, preferred_element_type=F32)
    )
    means = [
        jnp.sum(reduced[i * STRIP : (i + 1) * STRIP], axis=0, keepdims=True) * (1.0 / F**3)
        for i in range(4)
    ]
    tile = jnp.concatenate(means + means, 0)
    for i in range(payload.shape[0] // STRIP):
        payload[i * STRIP : (i + 1) * STRIP, :] = tile


def put_edges(ref, x, e_pl0, e_pl1, e_row0, e_row1):
    planes, rows, _ = ref.shape
    for y, line in zip(edge_spots("gy", rows), (e_row0, e_row1)):
        ref[x, pl.ds(y, 1), :] = line[pl.ds(x, 1), :]
    for spot, plane in zip(edge_spots("gx", planes), (e_pl0, e_pl1)):

        @pl.when(x == spot)
        def _():
            ref[x] = plane[...]


def sweep_kernel(
    k_hbm, w_hbm, f_hbm, w_pl0, w_pl1, w_row0, w_row1, f_pl0, f_pl1, f_row0, f_row1,
    w, f, k, cy, cz, g_ref, g_pl, g_row, sems,
):
    planes, rows, cols = w.shape
    sl = strips(rows)
    low, high = low_high("gy")
    sub = lax.broadcasted_iota(jnp.int32, (STRIP, cols), 0)
    sub0, sub1 = sub == 0, sub == STRIP - 1

    def copy(i, x):
        src, dst = ((k_hbm, k), (f_hbm, f), (w_hbm, w))[i]
        return pltpu.make_async_copy(src.at[x], dst.at[x], sems.at[i, x])

    def arrive(x):
        for i in range(3):
            copy(i, x).wait()
        put_edges(f, x, f_pl0, f_pl1, f_row0, f_row1)
        put_edges(w, x, w_pl0, w_pl1, w_row0, w_row1)

    for x in range(planes):
        for i in range(3):
            copy(i, x).start()
    arrive(0)

    def plane(x, carry):
        @pl.when(x < planes - 1)
        def _():
            arrive(x + 1)

        xn = jnp.minimum(x + 1, planes - 1)
        h_next = jnp.where(x < planes - 1, 0.5, 0.0).astype(F32)
        h_prev = jnp.where(x > 0, 0.5, 0.0).astype(F32)
        xp = jnp.maximum(x - 1, 0)
        dn = 0.0
        k0, u0 = k[x, sl[0], :], f[x, sl[0], :]
        ku, uu = upward(k0), upward(u0)
        for r, a in enumerate(sl):
            c_z = 0.5 * (k0 + left(k0))
            total = c_z * left(u0) + right(c_z * u0)
            if r + 1 < len(sl):
                k1, u1 = k[x, sl[r + 1], :], f[x, sl[r + 1], :]
                ku1, uu1 = upward(k1), upward(u1)
                c_y = 0.5 * (k0 + jnp.where(sub1, ku1, ku))
                above = jnp.where(sub1, uu1, uu)
            else:
                c_y = jnp.where(sub1, 0.0, 0.5 * (k0 + ku))
                above = uu
            nd = downward(c_y * u0)
            total = total + (c_y * above + jnp.where(sub0, dn, nd))
            dn = nd
            c_x = h_next * (k0 + k[xn, a, :])
            c_p = h_prev * (k0 + k[xp, a, :])
            total = total + (c_x * f[xn, a, :] + c_p * f[xp, a, :])
            cy[x, a, :] = c_y
            cz[x, a, :] = c_z
            g_ref[x, a, :] = (2.0 - DAMPING) * u0 + w[x, a, :] * total
            if r + 1 < len(sl):
                k0, u0, ku, uu = k1, u1, ku1, uu1
        for place, y in ((low, 0), (high, rows - 1)):
            g_row[place, pl.ds(x, 1), :] = g_ref[x, y : y + 1, :]
        return carry

    lax.fori_loop(0, planes, plane, 0)
    for side, x in enumerate(edge_spots("gx", planes)):
        g_pl[side] = g_ref[x]


def mid_kernel(
    g_pl, g_row, wc_pl, wc_row, xa, xb, ya, yb, o_pl0, o_pl1, o_row0, o_row1, q_pl, q_row
):
    for side, x, y in ((0, xa, ya), (1, xb, yb)):
        q_pl[side] = wc_pl[side] * x[...]
        q_row[side] = wc_row[side] * y[...]
    for side, p, r in ((0, o_pl0, o_row0), (1, o_pl1, o_row1)):
        p[...] = g_pl[side]
        r[...] = g_row[side]
    cross(q_pl, q_row, (o_pl0, o_pl1), (o_row0, o_row1), 1.0)


def tile_sums(x, u, k, cy, cz):
    planes, rows, cols = u.shape
    sl = strips(rows)
    tl = [slice(j, j + LANES) for j in range(0, cols, LANES)]
    lane = lax.broadcasted_iota(jnp.int32, (STRIP, LANES), 1)
    sub = lax.broadcasted_iota(jnp.int32, (STRIP, LANES), 0)
    xn, xp = jnp.minimum(x + 1, planes - 1), jnp.maximum(x - 1, 0)
    h_next = jnp.where(x < planes - 1, 0.5, 0.0).astype(F32)
    h_prev = jnp.where(x > 0, 0.5, 0.0).astype(F32)
    ru = [left(u[x, a, tl[0]]) for a in sl]
    pm = [right(cz[x, a, tl[-1]] * u[x, a, tl[-1]]) for a in sl]
    for j, t in enumerate(tl):
        us = [u[x, a, t] for a in sl]
        uu = [upward(a) for a in us]
        dn = 0.0
        for r, a in enumerate(sl):
            u0, c_y, c_z = us[r], cy[x, a, t], cz[x, a, t]
            nu = left(u[x, a, tl[(j + 1) % len(tl)]])
            c_x = h_next * (k[x, a, t] + k[xn, a, t])
            c_p = h_prev * (k[x, a, t] + k[xp, a, t])
            total = c_x * u[xn, a, t] + c_p * u[xp, a, t]
            total = total + c_z * jnp.where(lane == LANES - 1, nu, ru[r])
            mu = right(c_z * u0)
            total = total + jnp.where(lane == 0, pm[r], mu)
            ru[r], pm[r] = nu, mu
            above = jnp.where(sub == STRIP - 1, uu[r + 1], uu[r]) if r + 1 < len(sl) else uu[r]
            nd = downward(c_y * u0)
            total = total + (c_y * above + jnp.where(sub == 0, dn, nd))
            dn = nd
            yield a, t, u0, total


def last_kernel(
    w, f, k, cy, cz, g_in, interp, g_pl0, g_pl1, g_row0, g_row1,
    out, body, g, sems,
):
    planes, rows, cols = w.shape

    def copy(x):
        return pltpu.make_async_copy(
            body.at[x, STRIP : rows - STRIP, :], out.at[x, STRIP : rows - STRIP, :], sems.at[x]
        )

    def arrive(x):
        g[x] = g_in[x]
        put_edges(g, x, g_pl0, g_pl1, g_row0, g_row1)

    arrive(0)

    def plane(x, carry):
        @pl.when(x < planes - 1)
        def _():
            arrive(x + 1)

        offset = ((x % F).astype(F32) + 0.5) / F - 0.5
        weight = jnp.abs(offset)
        side = jnp.where(offset > 0, 2, 0)
        for a, t, u0, total in tile_sums(x, g, k, cy, cz):
            coarse = (1.0 - weight) * interp[1, a, t] + weight * interp[side, a, t]
            new = f[x, a, t] + (1.0 - DAMPING) * u0 + coarse
            body[x, a, t] = new + w[x, a, t] * total

        @pl.when((x > 0) & (x < planes - 1))
        def _():
            copy(x).start()

        return carry

    lax.fori_loop(0, planes, plane, 0)
    for x in range(1, planes - 1):
        copy(x).wait()


def finish_kernel(
    src, body, wc_pl, wc_row, xa, xb, ya, yb, out, s_pl, s_lo, s_hi, q_row, sems
):
    del src
    planes, rows, cols = out.shape
    xs, ys = edge_spots("gx", planes), edge_spots("gy", rows)
    low, high = low_high("gy")
    spots = (
        (s_lo, out.at[1 : planes - 1, 0:STRIP, :]),
        (s_hi, out.at[1 : planes - 1, rows - STRIP : rows, :]),
        (s_pl.at[0], out.at[xs[0]]),
        (s_pl.at[1], out.at[xs[1]]),
    )
    copies = [pltpu.make_async_copy(a, b, sems.at[i]) for i, (a, b) in enumerate(spots)]
    sub = lax.broadcasted_iota(jnp.int32, (STRIP, cols), 0)
    q_row[0] = wc_row[0] * ya[...]
    q_row[1] = wc_row[1] * yb[...]
    for x in range(1, planes - 1):
        q = q_row[low, x : x + 1, :]
        s_lo[x - 1] = body[x, :STRIP, :] + jnp.where(sub == 0, q, 0.0)
    copies[0].start()
    for x in range(1, planes - 1):
        q = q_row[high, x : x + 1, :]
        s_hi[x - 1] = body[x, rows - STRIP :, :] + jnp.where(sub == STRIP - 1, q, 0.0)
    copies[1].start()
    for side, other in ((0, xa), (1, xb)):
        x = xs[side]
        s_pl[side] = body[x] + wc_pl[side] * other[...]
        for b, y in enumerate(ys):
            py = pl.ds(y, 1)
            s_pl[side, py, :] = s_pl[side, py, :] + q_row[b, pl.ds(x, 1), :]
        copies[2 + side].start()
    for c in copies:
        c.wait()


def coarse_kernel(got, interp, coef, b_ref, u_ref, *, nx, ny, rows):
    nz = got.shape[1]
    per = 2 * 2

    def field(start):
        return [
            jnp.stack([got[pl.ds(p * ny * per + start + t, ny, stride=per), :] for p in range(nx)], 0)
            for t in range(2)
        ]

    resid, cond = field(0), field(2)

    half = 0.5 * COARSE_FACTOR

    def up(a):
        return pltpu.roll(a, ny - 1, a.ndim - 2)

    def down(a):
        return pltpu.roll(a, 1, a.ndim - 2)

    def after(a):
        return pltpu.roll(a, nz - 1, a.ndim - 1)

    def before(a):
        return pltpu.roll(a, 1, a.ndim - 1)

    inside = half * (cond[0] + cond[1])
    across = half * (cond[1] + up(cond[0]))
    coef[2, 0], coef[2, 1] = inside, across
    for t in range(2):
        c_x = half * (cond[t] + jnp.concatenate([cond[t][1:], cond[t][:1]], 0))
        c_z = half * (cond[t] + after(cond[t]))
        diag = REACTION + (c_x + jnp.concatenate([c_x[-1:], c_x[:-1]], 0))
        diag = diag + (c_z + before(c_z)) + (inside + (across if t else down(across)))
        inv = DAMPING / diag
        coef[0, t], coef[1, t], coef[3, t] = c_x, c_z, inv
        b_ref[t] = inv * resid[t]
        u_ref[0, t] = b_ref[t]

    def sweep(src, dst):
        prv, cur = [[u_ref[src, t, p] for t in range(2)] for p in (nx - 1, 0)]
        c_prv = [coef[0, t, nx - 1] for t in range(2)]
        for p in range(nx):
            nxt = [u_ref[src, t, (p + 1) % nx] for t in range(2)]
            c_x = [coef[0, t, p] for t in range(2)]
            c_in, c_ac = coef[2, 0, p], coef[2, 1, p]
            rows_part = (
                c_in * cur[1] + down(c_ac * cur[1]),
                c_in * cur[0] + c_ac * up(cur[0]),
            )
            for t in range(2):
                c_z = coef[1, t, p]
                total = (c_x[t] * nxt[t] + c_prv[t] * prv[t]) + rows_part[t]
                total = total + (c_z * after(cur[t]) + before(c_z * cur[t]))
                new = (b_ref[t, p] + (1.0 - DAMPING) * cur[t]) + coef[3, t, p] * total
                u_ref[dst, t, p] = new
            prv, cur, c_prv = cur, nxt, c_x

    def pair(i, carry):
        sweep(0, 1)
        sweep(1, 0)
        return carry

    steps = CSWEEPS - 1
    lax.fori_loop(0, steps // 2, pair, 0)
    last = 0
    if steps % 2:
        sweep(0, 1)
        last = 1

    gx, gy = lax.axis_index("gx"), lax.axis_index("gy")
    lines = []
    for d in (-1, 0, 1):
        p = lax.rem(gx + d + nx, nx)
        prev_s, next_s = lax.rem(gy + ny - 1, ny), lax.rem(gy + 1, ny)
        for t, s in ((1, prev_s), (0, gy), (1, gy), (0, next_s)):
            lines.append(u_ref[last, t, p, pl.ds(s, 1), :])
    lines = jnp.concatenate(lines + lines[:4], 0)
    cols = nz * F
    cell = lax.broadcasted_iota(jnp.int32, (nz, cols), 0)
    col = lax.broadcasted_iota(jnp.int32, (nz, cols), 1)
    base = col // F
    offset = ((col % F).astype(F32) + 0.5) / F - 0.5
    side = jnp.where(offset > 0, base + 1, base - 1)
    side = jnp.where(side < 0, side + nz, jnp.where(side >= nz, side - nz, side))
    weight = jnp.abs(offset)
    matrix = jnp.where(cell == base, 1.0 - weight, 0.0) + jnp.where(cell == side, weight, 0.0)
    wide = joined3(jnp.dot(split3(lines), matrix.astype(BF16), preferred_element_type=F32))
    sub = lax.broadcasted_iota(jnp.int32, (STRIP, cols), 0)
    for plane in range(3):
        for r in range(rows // STRIP):
            row = r * STRIP + sub
            off = ((row % F).astype(F32) + 0.5) / F - 0.5
            wt = jnp.abs(off)
            block = r * STRIP // F
            near = block + 1
            far = near + (1 if (r * STRIP) % F >= F // 2 else -1)
            a = wide[plane * 4 + near : plane * 4 + near + 1]
            c = wide[plane * 4 + far : plane * 4 + far + 1]
            interp[plane, r * STRIP : (r + 1) * STRIP, :] = (1.0 - wt) * a + wt * c


def swap(axis, first, second):
    count = lax.axis_size(axis)
    pairs = [(i, i ^ 1) for i in range(count)]
    others = [(i, (i + 1 if i % 2 else i - 1) % count) for i in range(count)]
    return lax.ppermute(first, axis, pairs), lax.ppermute(second, axis, others)


def per_device(nx, ny, v, s, k):
    planes, rows, cols = v.shape
    n = planes * rows * cols
    vm = pltpu.VMEM
    dma = pltpu.SemaphoreType.DMA
    full, edge, line = sds(planes, rows, cols), sds(rows, cols), sds(planes, cols)
    edges, lines = sds(2, rows, cols), sds(2, planes, cols)

    pl_a, pl_b = pl.pallas_call(
        planes_kernel,
        out_shape=(edges, edges),
        in_specs=[HBM] * 2,
        out_specs=(VM,) * 2,
        scratch_shapes=[dma((2, 2))],
        compiler_params=params(50),
        cost_estimate=cost(0, n // 4),
        name="planes",
    )(v, k)
    xa, xb = swap("gx", pl_a, pl_b)
    rw_a, rw_b = pl.pallas_call(
        rows_kernel,
        out_shape=(lines, lines),
        in_specs=[HBM] * 2,
        out_specs=(VM,) * 2,
        scratch_shapes=[dma((2, 2))],
        compiler_params=params(50),
        cost_estimate=cost(0, n // 4),
        name="rows",
    )(v, k)
    ya, yb = swap("gy", rw_a, rw_b)

    w, f, wi_pl, fi_pl, wi_row, fi_row, sums = pl.pallas_call(
        inner_kernel,
        out_shape=(full, full, edges, edges, lines, lines, sds(4 * STRIP, cols)),
        in_specs=[HBM] * 3,
        out_specs=(HBM,) * 2 + (VM,) * 5,
        scratch_shapes=[vm(full.shape, F32)] * 5
        + [dma((3, planes)), dma((2, planes))],
        compiler_params=params(52),
        cost_estimate=cost(50 * n, 20 * n),
        name="inner",
    )(v, s, k)

    devices = nx * ny
    out = pl.pallas_call(
        edge_kernel,
        out_shape=(edge, edge, line, line) * 2 + (edges, lines, sds(devices * 4, cols // F)),
        in_specs=[VM] * 13,
        out_specs=(VM,) * 11,
        scratch_shapes=[vm(edges.shape, F32), vm(lines.shape, F32)],
        compiler_params=params(6),
        cost_estimate=cost(10 * n // 8, n),
        name="edge",
    )(wi_pl, fi_pl, wi_row, fi_row, pl_a, pl_b, rw_a, rw_b, xa, xb, ya, yb, sums)
    f_edges, w_edges, (wc_pl, wc_row, payload) = out[:4], out[4:8], out[8:]

    fya, fyb = swap("gy", f_edges[2], f_edges[3])
    fxa, fxb = swap("gx", f_edges[0], f_edges[1])
    got = lax.all_to_all(payload, ("gx", "gy"), 0, 0, tiled=True)

    got, w, f, k = lax.optimization_barrier((got, w, f, k))

    w, f, k, cy, cz, g, g_pl, g_row = pl.pallas_call(
        sweep_kernel,
        out_shape=(full,) * 6 + (edges, lines),
        in_specs=[HBM] * 3 + [VM] * 8,
        out_specs=(VM,) * 8,
        scratch_shapes=[dma((3, planes))],
        compiler_params=params(26),
        cost_estimate=cost(40 * n, 12 * n),
        name="sweep",
    )(k, w, f, *w_edges, *f_edges)

    g_edges = pl.pallas_call(
        mid_kernel,
        out_shape=(edge, edge, line, line),
        in_specs=[VM] * 8,
        out_specs=(VM,) * 4,
        scratch_shapes=[vm(edges.shape, F32), vm(lines.shape, F32)],
        compiler_params=params(4),
        cost_estimate=cost(n // 8, n // 2),
        name="mid",
    )(g_pl, g_row, wc_pl, wc_row, fxa, fxb, fya, fyb)

    gya, gyb = swap("gy", g_edges[2], g_edges[3])
    gxa, gxb = swap("gx", g_edges[0], g_edges[1])

    cells = (nx, ny, cols // F)
    interp = pl.pallas_call(
        functools.partial(coarse_kernel, nx=nx, ny=ny, rows=rows),
        out_shape=sds(3, rows, cols),
        in_specs=[VM],
        out_specs=VM,
        scratch_shapes=[
            vm((4, 2) + cells, F32),
            vm((2,) + cells, F32),
            vm((2, 2) + cells, F32),
        ],
        compiler_params=params(8),
        cost_estimate=cost(20 * n, n),
        name="coarse",
    )(got)

    b_side = sds(planes - 2, STRIP, cols)
    out, body = pl.pallas_call(
        last_kernel,
        out_shape=(full, full),
        in_specs=[VM] * 11,
        out_specs=(HBM, VM),
        scratch_shapes=[vm(full.shape, F32), dma((planes,))],
        compiler_params=params(22),
        cost_estimate=cost(40 * n, 20 * n),
        name="last",
    )(w, f, k, cy, cz, g, interp, *g_edges)

    b_side = (planes - 2, STRIP, cols)
    return pl.pallas_call(
        finish_kernel,
        out_shape=full,
        in_specs=[HBM] + [VM] * 7,
        out_specs=HBM,
        scratch_shapes=[
            vm(edges.shape, F32), vm(b_side, F32), vm(b_side, F32), vm(lines.shape, F32), dma((4,)),
        ],
        input_output_aliases={0: 0},
        compiler_params=params(6),
        cost_estimate=cost(n // 4, 3 * n),
        name="finish",
    )(out, body, wc_pl, wc_row, gxa, gxb, gya, gyb)


def solution(mesh):
    placed = P("gx", "gy", None)
    body = functools.partial(per_device, mesh.shape["gx"], mesh.shape["gy"])
    return jax.shard_map(
        body, mesh=mesh, in_specs=(placed,) * 3, out_specs=placed, check_vma=False
    )
```

```python
import functools
import jax
import jax.numpy as jnp
from jax import lax
from jax.experimental import pallas as pl
from jax.experimental.pallas import tpu as pltpu
from jax.sharding import PartitionSpec as P

F = 16
CSWEEPS = 32
REACTION = 0.2
DAMPING = 0.8
COARSE_FACTOR = 0.25
F32 = jnp.float32
BF16 = jnp.bfloat16
STRIP = 8
LANES = 512

VM = pl.BlockSpec(memory_space=pltpu.VMEM)
ANY = pl.BlockSpec(memory_space=pl.ANY)
HBM = pl.BlockSpec(memory_space=pltpu.HBM)


def params(mib):
    return pltpu.CompilerParams(vmem_limit_bytes=mib * 1024 * 1024)


def cost(flops, nbytes):
    return pl.CostEstimate(flops=int(flops), bytes_accessed=int(nbytes), transcendentals=0)


def sds(*shape):
    return jax.ShapeDtypeStruct(shape, F32)


def left(a):
    return pltpu.roll(a, a.shape[-1] - 1, a.ndim - 1)


def right(a):
    return pltpu.roll(a, 1, a.ndim - 1)


def upward(a):
    return pltpu.roll(a, a.shape[-2] - 1, a.ndim - 2)


def downward(a):
    return pltpu.roll(a, 1, a.ndim - 2)


def strips(rows):
    return [slice(r * STRIP, (r + 1) * STRIP) for r in range(rows // STRIP)]


def edge_spots(axis, count):
    odd = lax.rem(lax.axis_index(axis), 2)
    return (1 - odd) * (count - 1), odd * (count - 1)


def low_high(axis):
    odd = lax.rem(lax.axis_index(axis), 2)
    return 1 - odd, odd


def planes_kernel(v, k, pl_a, pl_b, sems):
    copies = [
        pltpu.make_async_copy(src.at[x], dst.at[i], sems.at[i, j])
        for i, src in enumerate((v, k))
        for j, (x, dst) in enumerate(zip(edge_spots("gx", v.shape[0]), (pl_a, pl_b)))
    ]
    for c in copies:
        c.start()
    for c in copies:
        c.wait()


def rows_kernel(v, k, rw_a, rw_b, sems):
    copies = [
        pltpu.make_async_copy(src.at[:, y, :], dst.at[i], sems.at[i, j])
        for i, src in enumerate((v, k))
        for j, (y, dst) in enumerate(zip(edge_spots("gy", v.shape[1]), (rw_a, rw_b)))
    ]
    for c in copies:
        c.start()
    for c in copies:
        c.wait()


def inner_kernel(
    v_hbm, s_hbm, k_hbm,
    w_hbm, f_hbm, w_pl, f_pl, w_row, f_row, sums,
    v, s, k, w_ref, f_ref, sems, out_sems,
):
    planes, rows, cols = v.shape
    sl = strips(rows)
    n = len(sl)
    low, high = low_high("gy")

    def copy(i, x):
        src, dst = ((k_hbm, k), (v_hbm, v), (s_hbm, s))[i]
        return pltpu.make_async_copy(src.at[x], dst.at[x], sems.at[i, x])

    def out_copy(i, x):
        src, dst = ((w_ref, w_hbm), (f_ref, f_hbm))[i]
        return pltpu.make_async_copy(src.at[x], dst.at[x], out_sems.at[i, x])

    for x in range(planes):
        for i in range(3):
            copy(i, x).start()
    sums[...] = jnp.zeros_like(sums)
    copy(0, 0).wait()
    copy(1, 0).wait()
    sub = lax.broadcasted_iota(jnp.int32, (STRIP, cols), 0)
    sub0, sub1 = sub == 0, sub == STRIP - 1

    def plane(x, carry):
        @pl.when(x < planes - 1)
        def _():
            copy(0, x + 1).wait()
            copy(1, x + 1).wait()

        copy(2, x).wait()
        xn, xp = jnp.minimum(x + 1, planes - 1), jnp.maximum(x - 1, 0)
        h_prev = jnp.where(x > 0, 0.5, 0.0).astype(F32)
        h_next = jnp.where(x < planes - 1, 0.5, 0.0).astype(F32)
        dc = df = 0.0
        k0, v0 = k[x, sl[0], :], v[x, sl[0], :]
        ku, vu = upward(k0), upward(v0)
        res_sum = k_sum = None
        for r, a in enumerate(sl):
            c_z = 0.5 * (k0 + left(k0))
            f_z = c_z * (v0 - left(v0))
            diag = c_z + right(c_z)
            res = right(f_z) - f_z
            if r + 1 < n:
                k1, v1 = k[x, sl[r + 1], :], v[x, sl[r + 1], :]
                ku1, vu1 = upward(k1), upward(v1)
                c_y = 0.5 * (k0 + jnp.where(sub1, ku1, ku))
                f_y = c_y * (v0 - jnp.where(sub1, vu1, vu))
            else:
                c_y = jnp.where(sub1, 0.0, 0.5 * (k0 + ku))
                f_y = c_y * (v0 - vu)
            nc, nf = downward(c_y), downward(f_y)
            diag = diag + (c_y + jnp.where(sub0, dc, nc))
            res = res + (jnp.where(sub0, df, nf) - f_y)
            dc, df = nc, nf
            c_x = h_next * (k0 + k[xn, a, :])
            f_x = c_x * (v0 - v[xn, a, :])
            c_p = h_prev * (k0 + k[xp, a, :])
            f_p = c_p * (v[xp, a, :] - v0)
            diag = diag + ((c_p + c_x) + REACTION)
            res = res + ((f_p - f_x) + (s[x, a, :] - REACTION * v0))
            w = DAMPING / diag
            w_ref[x, a, :] = w
            f_ref[x, a, :] = w * res
            half = r * STRIP // F
            res_sum = res if r * STRIP % F == 0 else res_sum + res
            k_sum = k0 if r * STRIP % F == 0 else k_sum + k0
            if (r + 1) * STRIP % F == 0:
                sums[half * STRIP : (half + 1) * STRIP, :] += res_sum
                sums[(2 + half) * STRIP : (3 + half) * STRIP, :] += k_sum
            if r + 1 < n:
                k0, v0, ku, vu = k1, v1, ku1, vu1
        out_copy(0, x).start()
        out_copy(1, x).start()
        for place, y in ((low, 0), (high, rows - 1)):
            w_row[place, pl.ds(x, 1), :] = w_ref[x, y : y + 1, :]
            f_row[place, pl.ds(x, 1), :] = f_ref[x, y : y + 1, :]
        return carry

    lax.fori_loop(0, planes, plane, 0)
    for side, x in enumerate(edge_spots("gx", planes)):
        w_pl[side] = w_ref[x]
        f_pl[side] = f_ref[x]
    for x in range(planes):
        for i in range(2):
            out_copy(i, x).wait()


def cross(q_pl, q_row, pls, rws, sign):
    rows, planes = q_pl.shape[1], q_row.shape[1]
    for a in range(2):
        pls[a][...] = pls[a][...] + sign * q_pl[a]
        rws[a][...] = rws[a][...] + sign * q_row[a]
    for a, x in enumerate(edge_spots("gx", planes)):
        for b, y in enumerate(edge_spots("gy", rows)):
            px, py = pl.ds(x, 1), pl.ds(y, 1)
            pls[a][py, :] = pls[a][py, :] + sign * q_row[b, px, :]
            rws[b][px, :] = rws[b][px, :] + sign * q_pl[a, py, :]


def split3(a):
    one = a.astype(BF16)
    rest = a - one.astype(F32)
    two = rest.astype(BF16)
    three = (rest - two.astype(F32)).astype(BF16)
    return jnp.concatenate([one, two, three], 0)


def joined3(a):
    n = a.shape[0] // 3
    return a[:n] + a[n : 2 * n] + a[2 * n :]


def edge_kernel(
    wi_pl, fi_pl, wi_row, fi_row, pl_a, pl_b, rw_a, rw_b, xa, xb, ya, yb, sums,
    f_pl0, f_pl1, f_row0, f_row1, w_pl0, w_pl1, w_row0, w_row1, wc_pl, wc_row, payload,
    q_pl, q_row,
):
    rows, cols = f_pl0.shape
    f_pl, f_row, w_pl, w_row = (f_pl0, f_pl1), (f_row0, f_row1), (w_pl0, w_pl1), (w_row0, w_row1)
    for side, mine, other in ((0, pl_a, xa), (1, pl_b, xb)):
        c = 0.5 * (mine[1] + other[1])
        wc_pl[side] = c
        q_pl[side] = c * (mine[0] - other[0])
    for side, mine, other in ((0, rw_a, ya), (1, rw_b, yb)):
        c = 0.5 * (mine[1] + other[1])
        wc_row[side] = c
        q_row[side] = c * (mine[0] - other[0])
    for w, f, wi, fi in ((w_pl, f_pl, wi_pl, fi_pl), (w_row, f_row, wi_row, fi_row)):
        for side in range(2):
            diag = DAMPING / wi[side]
            w[side][...] = diag
            f[side][...] = fi[side] * (diag * (1.0 / DAMPING))
    cross(wc_pl, wc_row, w_pl, w_row, 1.0)
    cross(q_pl, q_row, f_pl, f_row, -1.0)
    for w, f, wc in ((w_pl, f_pl, wc_pl), (w_row, f_row, wc_row)):
        for side in range(2):
            inv = DAMPING / w[side][...]
            w[side][...] = inv
            f[side][...] = f[side][...] * inv
            wc[side] = wc[side] * inv
    low, high = low_high("gy")
    parts = []
    for half in range(rows // F):
        total = sums[half * STRIP : (half + 1) * STRIP, :]
        for side in range(2):
            for r in range(half * F // STRIP, (half + 1) * F // STRIP):
                total = total - q_pl[side, r * STRIP : (r + 1) * STRIP, :]
        if half == 0:
            for r in range(q_row.shape[1] // STRIP):
                total = total - q_row[low, r * STRIP : (r + 1) * STRIP, :]
        if half == rows // F - 1:
            for r in range(q_row.shape[1] // STRIP):
                total = total - q_row[high, r * STRIP : (r + 1) * STRIP, :]
        parts.append(total)
    parts.append(sums[2 * STRIP :, :])
    col = lax.broadcasted_iota(jnp.int32, (cols, cols // F), 0)
    cell = lax.broadcasted_iota(jnp.int32, (cols, cols // F), 1)
    gather = jnp.where(col // F == cell, 1.0, 0.0).astype(BF16)
    reduced = joined3(
        jnp.dot(split3(jnp.concatenate(parts, 0)), gather, preferred_element_type=F32)
    )
    means = [
        jnp.sum(reduced[i * STRIP : (i + 1) * STRIP], axis=0, keepdims=True) * (1.0 / F**3)
        for i in range(4)
    ]
    tile = jnp.concatenate(means + means, 0)
    for i in range(payload.shape[0] // STRIP):
        payload[i * STRIP : (i + 1) * STRIP, :] = tile


def put_edges(ref, x, e_pl0, e_pl1, e_row0, e_row1):
    planes, rows, _ = ref.shape
    for y, line in zip(edge_spots("gy", rows), (e_row0, e_row1)):
        ref[x, pl.ds(y, 1), :] = line[pl.ds(x, 1), :]
    for spot, plane in zip(edge_spots("gx", planes), (e_pl0, e_pl1)):

        @pl.when(x == spot)
        def _():
            ref[x] = plane[...]


def coarse_start(got, coef, b_ref, u_ref):
    nx, ny, nz = u_ref.shape[2:]
    per = 2 * 2

    def field(start):
        return [
            jnp.stack([got[pl.ds(p * ny * per + start + t, ny, stride=per), :] for p in range(nx)], 0)
            for t in range(2)
        ]

    resid, cond = field(0), field(2)

    half = 0.5 * COARSE_FACTOR

    inside = half * (cond[0] + cond[1])
    across = half * (cond[1] + upward(cond[0]))
    coef[2, 0], coef[2, 1] = inside, across
    for t in range(2):
        c_x = half * (cond[t] + jnp.concatenate([cond[t][1:], cond[t][:1]], 0))
        c_z = half * (cond[t] + left(cond[t]))
        diag = REACTION + (c_x + jnp.concatenate([c_x[-1:], c_x[:-1]], 0))
        diag = diag + (c_z + right(c_z)) + (inside + (across if t else downward(across)))
        inv = DAMPING / diag
        coef[0, t], coef[1, t], coef[3, t] = c_x, c_z, inv
        b_ref[t] = inv * resid[t]
        u_ref[0, t] = jnp.zeros_like(inv)


def coarse_sweep(src, dst, coef, b_ref, u_ref):
    nx = u_ref.shape[2]
    prv, cur = [[u_ref[src, t, p] for t in range(2)] for p in (nx - 1, 0)]
    c_prv = [coef[0, t, nx - 1] for t in range(2)]
    for p in range(nx):
        nxt = [u_ref[src, t, (p + 1) % nx] for t in range(2)]
        c_x = [coef[0, t, p] for t in range(2)]
        c_in, c_ac = coef[2, 0, p], coef[2, 1, p]
        rows_part = (
            c_in * cur[1] + downward(c_ac * cur[1]),
            c_in * cur[0] + c_ac * upward(cur[0]),
        )
        for t in range(2):
            c_z = coef[1, t, p]
            total = (c_x[t] * nxt[t] + c_prv[t] * prv[t]) + rows_part[t]
            total = total + (c_z * left(cur[t]) + right(c_z * cur[t]))
            new = (b_ref[t, p] + (1.0 - DAMPING) * cur[t]) + coef[3, t, p] * total
            u_ref[dst, t, p] = new
        prv, cur, c_prv = cur, nxt, c_x


def coarse_finish(u_ref, interp):
    nx, ny, nz = u_ref.shape[2:]
    rows = interp.shape[1]
    gx, gy = lax.axis_index("gx"), lax.axis_index("gy")
    lines = []
    for d in (-1, 0, 1):
        p = lax.rem(gx + d + nx, nx)
        prev_s, next_s = lax.rem(gy + ny - 1, ny), lax.rem(gy + 1, ny)
        for t, s in ((1, prev_s), (0, gy), (1, gy), (0, next_s)):
            lines.append(u_ref[0, t, p, pl.ds(s, 1), :])
    lines = jnp.concatenate(lines + lines[:4], 0)
    cols = nz * F
    cell = lax.broadcasted_iota(jnp.int32, (nz, cols), 0)
    col = lax.broadcasted_iota(jnp.int32, (nz, cols), 1)
    base = col // F
    offset = ((col % F).astype(F32) + 0.5) / F - 0.5
    side = jnp.where(offset > 0, base + 1, base - 1)
    side = jnp.where(side < 0, side + nz, jnp.where(side >= nz, side - nz, side))
    weight = jnp.abs(offset)
    matrix = jnp.where(cell == base, 1.0 - weight, 0.0) + jnp.where(cell == side, weight, 0.0)
    wide = joined3(jnp.dot(split3(lines), matrix.astype(BF16), preferred_element_type=F32))
    sub = lax.broadcasted_iota(jnp.int32, (STRIP, cols), 0)
    for plane in range(3):
        for r in range(rows // STRIP):
            row = r * STRIP + sub
            off = ((row % F).astype(F32) + 0.5) / F - 0.5
            wt = jnp.abs(off)
            block = r * STRIP // F
            near = block + 1
            far = near + (1 if (r * STRIP) % F >= F // 2 else -1)
            a = wide[plane * 4 + near : plane * 4 + near + 1]
            c = wide[plane * 4 + far : plane * 4 + far + 1]
            interp[plane, r * STRIP : (r + 1) * STRIP, :] = (1.0 - wt) * a + wt * c


def sweep_kernel(
    k_hbm, w_hbm, f_hbm, got, w_pl0, w_pl1, w_row0, w_row1, f_pl0, f_pl1, f_row0, f_row1,
    w, f, k, cy, cz, g_ref, g_pl, g_row, interp, coef, b_ref, u_ref, sems,
):
    planes, rows, cols = w.shape
    sl = strips(rows)
    low, high = low_high("gy")
    sub = lax.broadcasted_iota(jnp.int32, (STRIP, cols), 0)
    sub0, sub1 = sub == 0, sub == STRIP - 1

    def copy(i, x):
        src, dst = ((k_hbm, k), (f_hbm, f), (w_hbm, w))[i]
        return pltpu.make_async_copy(src.at[x], dst.at[x], sems.at[i, x])

    def arrive(x):
        for i in range(3):
            copy(i, x).wait()
        put_edges(f, x, f_pl0, f_pl1, f_row0, f_row1)
        put_edges(w, x, w_pl0, w_pl1, w_row0, w_row1)

    for x in range(planes):
        for i in range(3):
            copy(i, x).start()
    coarse_start(got, coef, b_ref, u_ref)
    arrive(0)

    def plane(x, carry):
        @pl.when(x < planes - 1)
        def _():
            arrive(x + 1)

        xn = jnp.minimum(x + 1, planes - 1)
        h_next = jnp.where(x < planes - 1, 0.5, 0.0).astype(F32)
        h_prev = jnp.where(x > 0, 0.5, 0.0).astype(F32)
        xp = jnp.maximum(x - 1, 0)
        dn = 0.0
        k0, u0 = k[x, sl[0], :], f[x, sl[0], :]
        ku, uu = upward(k0), upward(u0)
        for r, a in enumerate(sl):
            c_z = 0.5 * (k0 + left(k0))
            total = c_z * left(u0) + right(c_z * u0)
            if r + 1 < len(sl):
                k1, u1 = k[x, sl[r + 1], :], f[x, sl[r + 1], :]
                ku1, uu1 = upward(k1), upward(u1)
                c_y = 0.5 * (k0 + jnp.where(sub1, ku1, ku))
                above = jnp.where(sub1, uu1, uu)
            else:
                c_y = jnp.where(sub1, 0.0, 0.5 * (k0 + ku))
                above = uu
            nd = downward(c_y * u0)
            total = total + (c_y * above + jnp.where(sub0, dn, nd))
            dn = nd
            c_x = h_next * (k0 + k[xn, a, :])
            c_p = h_prev * (k0 + k[xp, a, :])
            total = total + (c_x * f[xn, a, :] + c_p * f[xp, a, :])
            cy[x, a, :] = c_y
            cz[x, a, :] = c_z
            g_ref[x, a, :] = (2.0 - DAMPING) * u0 + w[x, a, :] * total
            if r + 1 < len(sl):
                k0, u0, ku, uu = k1, u1, ku1, uu1
        for _ in range(CSWEEPS // (2 * planes)):
            coarse_sweep(0, 1, coef, b_ref, u_ref)
            coarse_sweep(1, 0, coef, b_ref, u_ref)
        for place, y in ((low, 0), (high, rows - 1)):
            g_row[place, pl.ds(x, 1), :] = g_ref[x, y : y + 1, :]
        return carry

    lax.fori_loop(0, planes, plane, 0)
    for side, x in enumerate(edge_spots("gx", planes)):
        g_pl[side] = g_ref[x]
    coarse_finish(u_ref, interp)


def mid_kernel(
    g_pl, g_row, wc_pl, wc_row, xa, xb, ya, yb, o_pl0, o_pl1, o_row0, o_row1, q_pl, q_row
):
    for side, x, y in ((0, xa, ya), (1, xb, yb)):
        q_pl[side] = wc_pl[side] * x[...]
        q_row[side] = wc_row[side] * y[...]
    for side, p, r in ((0, o_pl0, o_row0), (1, o_pl1, o_row1)):
        p[...] = g_pl[side]
        r[...] = g_row[side]
    cross(q_pl, q_row, (o_pl0, o_pl1), (o_row0, o_row1), 1.0)


def tile_sums(x, u, k, cy, cz):
    planes, rows, cols = u.shape
    sl = strips(rows)
    tl = [slice(j, j + LANES) for j in range(0, cols, LANES)]
    lane = lax.broadcasted_iota(jnp.int32, (STRIP, LANES), 1)
    sub = lax.broadcasted_iota(jnp.int32, (STRIP, LANES), 0)
    xn, xp = jnp.minimum(x + 1, planes - 1), jnp.maximum(x - 1, 0)
    h_next = jnp.where(x < planes - 1, 0.5, 0.0).astype(F32)
    h_prev = jnp.where(x > 0, 0.5, 0.0).astype(F32)
    ru = [left(u[x, a, tl[0]]) for a in sl]
    pm = [right(cz[x, a, tl[-1]] * u[x, a, tl[-1]]) for a in sl]
    for j, t in enumerate(tl):
        us = [u[x, a, t] for a in sl]
        uu = [upward(a) for a in us]
        dn = 0.0
        for r, a in enumerate(sl):
            u0, c_y, c_z = us[r], cy[x, a, t], cz[x, a, t]
            nu = left(u[x, a, tl[(j + 1) % len(tl)]])
            c_x = h_next * (k[x, a, t] + k[xn, a, t])
            c_p = h_prev * (k[x, a, t] + k[xp, a, t])
            total = c_x * u[xn, a, t] + c_p * u[xp, a, t]
            total = total + c_z * jnp.where(lane == LANES - 1, nu, ru[r])
            mu = right(c_z * u0)
            total = total + jnp.where(lane == 0, pm[r], mu)
            ru[r], pm[r] = nu, mu
            above = jnp.where(sub == STRIP - 1, uu[r + 1], uu[r]) if r + 1 < len(sl) else uu[r]
            nd = downward(c_y * u0)
            total = total + (c_y * above + jnp.where(sub == 0, dn, nd))
            dn = nd
            yield a, t, u0, total


def last_kernel(
    w, f, k, cy, cz, g_in, interp, g_pl0, g_pl1, g_row0, g_row1,
    out, body, g, sems,
):
    planes, rows, cols = w.shape

    def copy(x):
        return pltpu.make_async_copy(
            body.at[x, STRIP : rows - STRIP, :], out.at[x, STRIP : rows - STRIP, :], sems.at[x]
        )

    def arrive(x):
        g[x] = g_in[x]
        put_edges(g, x, g_pl0, g_pl1, g_row0, g_row1)

    arrive(0)

    def plane(x, carry):
        @pl.when(x < planes - 1)
        def _():
            arrive(x + 1)

        offset = ((x % F).astype(F32) + 0.5) / F - 0.5
        weight = jnp.abs(offset)
        side = jnp.where(offset > 0, 2, 0)
        for a, t, u0, total in tile_sums(x, g, k, cy, cz):
            coarse = (1.0 - weight) * interp[1, a, t] + weight * interp[side, a, t]
            new = f[x, a, t] + (1.0 - DAMPING) * u0 + coarse
            body[x, a, t] = new + w[x, a, t] * total

        @pl.when((x > 0) & (x < planes - 1))
        def _():
            copy(x).start()

        return carry

    lax.fori_loop(0, planes, plane, 0)
    for x in range(1, planes - 1):
        copy(x).wait()


def finish_kernel(
    src, body, wc_pl, wc_row, xa, xb, ya, yb, out, s_pl, s_lo, s_hi, q_row, sems
):
    del src
    planes, rows, cols = out.shape
    xs, ys = edge_spots("gx", planes), edge_spots("gy", rows)
    low, high = low_high("gy")
    spots = (
        (s_lo, out.at[1 : planes - 1, 0:STRIP, :]),
        (s_hi, out.at[1 : planes - 1, rows - STRIP : rows, :]),
        (s_pl.at[0], out.at[xs[0]]),
        (s_pl.at[1], out.at[xs[1]]),
    )
    copies = [pltpu.make_async_copy(a, b, sems.at[i]) for i, (a, b) in enumerate(spots)]
    sub = lax.broadcasted_iota(jnp.int32, (STRIP, cols), 0)
    q_row[0] = wc_row[0] * ya[...]
    q_row[1] = wc_row[1] * yb[...]
    for x in range(1, planes - 1):
        q = q_row[low, x : x + 1, :]
        s_lo[x - 1] = body[x, :STRIP, :] + jnp.where(sub == 0, q, 0.0)
    copies[0].start()
    for x in range(1, planes - 1):
        q = q_row[high, x : x + 1, :]
        s_hi[x - 1] = body[x, rows - STRIP :, :] + jnp.where(sub == STRIP - 1, q, 0.0)
    copies[1].start()
    for side, other in ((0, xa), (1, xb)):
        x = xs[side]
        s_pl[side] = body[x] + wc_pl[side] * other[...]
        for b, y in enumerate(ys):
            py = pl.ds(y, 1)
            s_pl[side, py, :] = s_pl[side, py, :] + q_row[b, pl.ds(x, 1), :]
        copies[2 + side].start()
    for c in copies:
        c.wait()


def swap(axis, first, second):
    count = lax.axis_size(axis)
    pairs = [(i, i ^ 1) for i in range(count)]
    others = [(i, (i + 1 if i % 2 else i - 1) % count) for i in range(count)]
    return lax.ppermute(first, axis, pairs), lax.ppermute(second, axis, others)


def per_device(nx, ny, v, s, k):
    planes, rows, cols = v.shape
    n = planes * rows * cols
    vm = pltpu.VMEM
    dma = pltpu.SemaphoreType.DMA
    full, edge, line = sds(planes, rows, cols), sds(rows, cols), sds(planes, cols)
    edges, lines = sds(2, rows, cols), sds(2, planes, cols)

    pl_a, pl_b = pl.pallas_call(
        planes_kernel,
        out_shape=(edges, edges),
        in_specs=[HBM] * 2,
        out_specs=(VM,) * 2,
        scratch_shapes=[dma((2, 2))],
        compiler_params=params(50),
        cost_estimate=cost(0, n // 4),
        name="planes",
    )(v, k)
    xa, xb = swap("gx", pl_a, pl_b)
    rw_a, rw_b = pl.pallas_call(
        rows_kernel,
        out_shape=(lines, lines),
        in_specs=[HBM] * 2,
        out_specs=(VM,) * 2,
        scratch_shapes=[dma((2, 2))],
        compiler_params=params(50),
        cost_estimate=cost(0, n // 4),
        name="rows",
    )(v, k)
    ya, yb = swap("gy", rw_a, rw_b)

    w, f, wi_pl, fi_pl, wi_row, fi_row, sums = pl.pallas_call(
        inner_kernel,
        out_shape=(full, full, edges, edges, lines, lines, sds(4 * STRIP, cols)),
        in_specs=[HBM] * 3,
        out_specs=(HBM,) * 2 + (VM,) * 5,
        scratch_shapes=[vm(full.shape, F32)] * 5
        + [dma((3, planes)), dma((2, planes))],
        compiler_params=params(52),
        cost_estimate=cost(50 * n, 20 * n),
        name="inner",
    )(v, s, k)

    devices = nx * ny
    cells = (nx, ny, cols // F)
    out = pl.pallas_call(
        edge_kernel,
        out_shape=(edge, edge, line, line) * 2 + (edges, lines, sds(devices * 4, cols // F)),
        in_specs=[VM] * 13,
        out_specs=(VM,) * 11,
        scratch_shapes=[vm(edges.shape, F32), vm(lines.shape, F32)],
        compiler_params=params(6),
        cost_estimate=cost(10 * n // 8, n),
        name="edge",
    )(wi_pl, fi_pl, wi_row, fi_row, pl_a, pl_b, rw_a, rw_b, xa, xb, ya, yb, sums)
    f_edges, w_edges, (wc_pl, wc_row, payload) = out[:4], out[4:8], out[8:]

    fya, fyb = swap("gy", f_edges[2], f_edges[3])
    fxa, fxb = swap("gx", f_edges[0], f_edges[1])
    got = lax.all_to_all(payload, ("gx", "gy"), 0, 0, tiled=True)

    got, w, f, k = lax.optimization_barrier((got, w, f, k))

    w, f, k, cy, cz, g, g_pl, g_row, interp = pl.pallas_call(
        sweep_kernel,
        out_shape=(full,) * 6 + (edges, lines, sds(3, rows, cols)),
        in_specs=[HBM] * 3 + [VM] * 9,
        out_specs=(VM,) * 9,
        scratch_shapes=[
            vm((4, 2) + cells, F32), vm((2,) + cells, F32), vm((2, 2) + cells, F32), dma((3, planes)),
        ],
        compiler_params=params(24),
        cost_estimate=cost(40 * n, 12 * n),
        name="sweep",
    )(k, w, f, got, *w_edges, *f_edges)

    g_edges = pl.pallas_call(
        mid_kernel,
        out_shape=(edge, edge, line, line),
        in_specs=[VM] * 8,
        out_specs=(VM,) * 4,
        scratch_shapes=[vm(edges.shape, F32), vm(lines.shape, F32)],
        compiler_params=params(4),
        cost_estimate=cost(n // 8, n // 2),
        name="mid",
    )(g_pl, g_row, wc_pl, wc_row, fxa, fxb, fya, fyb)

    gya, gyb = swap("gy", g_edges[2], g_edges[3])
    gxa, gxb = swap("gx", g_edges[0], g_edges[1])

    out, body = pl.pallas_call(
        last_kernel,
        out_shape=(full, full),
        in_specs=[VM] * 11,
        out_specs=(HBM, VM),
        scratch_shapes=[vm(full.shape, F32), dma((planes,))],
        compiler_params=params(22),
        cost_estimate=cost(40 * n, 20 * n),
        name="last",
    )(w, f, k, cy, cz, g, interp, *g_edges)

    b_side = (planes - 2, STRIP, cols)
    return pl.pallas_call(
        finish_kernel,
        out_shape=full,
        in_specs=[HBM] + [VM] * 7,
        out_specs=HBM,
        scratch_shapes=[
            vm(edges.shape, F32), vm(b_side, F32), vm(b_side, F32), vm(lines.shape, F32), dma((4,)),
        ],
        input_output_aliases={0: 0},
        compiler_params=params(6),
        cost_estimate=cost(n // 4, 3 * n),
        name="finish",
    )(out, body, wc_pl, wc_row, gxa, gxb, gya, gyb)


def solution(mesh):
    placed = P("gx", "gy", None)
    body = functools.partial(per_device, mesh.shape["gx"], mesh.shape["gy"])
    return jax.shard_map(
        body, mesh=mesh, in_specs=(placed,) * 3, out_specs=placed, check_vma=False
    )
```

```python
import functools
import jax
import jax.numpy as jnp
from jax import lax
from jax.experimental import pallas as pl
from jax.experimental.pallas import tpu as pltpu
from jax.sharding import PartitionSpec as P

F = 16
CSWEEPS = 32
REACTION = 0.2
DAMPING = 0.8
COARSE_FACTOR = 0.25
F32 = jnp.float32
BF16 = jnp.bfloat16
STRIP = 8
LANES = 512

VM = pl.BlockSpec(memory_space=pltpu.VMEM)
ANY = pl.BlockSpec(memory_space=pl.ANY)
HBM = pl.BlockSpec(memory_space=pltpu.HBM)


def params(mib):
    return pltpu.CompilerParams(vmem_limit_bytes=mib * 1024 * 1024)


def cost(flops, nbytes):
    return pl.CostEstimate(flops=int(flops), bytes_accessed=int(nbytes), transcendentals=0)


def sds(*shape):
    return jax.ShapeDtypeStruct(shape, F32)


def left(a):
    return pltpu.roll(a, a.shape[1] - 1, 1)


def right(a):
    return pltpu.roll(a, 1, 1)


def upward(a):
    return pltpu.roll(a, STRIP - 1, 0)


def downward(a):
    return pltpu.roll(a, 1, 0)


def strips(rows):
    return [slice(r * STRIP, (r + 1) * STRIP) for r in range(rows // STRIP)]


def edge_spots(axis, count):
    odd = lax.rem(lax.axis_index(axis), 2)
    return (1 - odd) * (count - 1), odd * (count - 1)


def low_high(axis):
    odd = lax.rem(lax.axis_index(axis), 2)
    return 1 - odd, odd


def planes_kernel(v, k, pl_a, pl_b, sems):
    copies = [
        pltpu.make_async_copy(src.at[x], dst.at[i], sems.at[i, j])
        for i, src in enumerate((v, k))
        for j, (x, dst) in enumerate(zip(edge_spots("gx", v.shape[0]), (pl_a, pl_b)))
    ]
    for c in copies:
        c.start()
    for c in copies:
        c.wait()


def rows_kernel(v, k, rw_a, rw_b, sems):
    copies = [
        pltpu.make_async_copy(src.at[:, y, :], dst.at[i], sems.at[i, j])
        for i, src in enumerate((v, k))
        for j, (y, dst) in enumerate(zip(edge_spots("gy", v.shape[1]), (rw_a, rw_b)))
    ]
    for c in copies:
        c.start()
    for c in copies:
        c.wait()


def inner_kernel(
    v_hbm, s_hbm, k_hbm,
    w_hbm, f_hbm, w_pl, f_pl, w_row, f_row, sums,
    v, s, k, w_ref, f_ref, sems, out_sems,
):
    planes, rows, cols = v.shape
    sl = strips(rows)
    n = len(sl)
    low, high = low_high("gy")

    def copy(i, x):
        src, dst = ((k_hbm, k), (v_hbm, v), (s_hbm, s))[i]
        return pltpu.make_async_copy(src.at[x], dst.at[x], sems.at[i, x])

    def out_copy(i, x):
        src, dst = ((w_ref, w_hbm), (f_ref, f_hbm))[i]
        return pltpu.make_async_copy(src.at[x], dst.at[x], out_sems.at[i, x])

    for x in range(planes):
        for i in range(3):
            copy(i, x).start()
    sums[...] = jnp.zeros_like(sums)
    copy(0, 0).wait()
    copy(1, 0).wait()
    sub = lax.broadcasted_iota(jnp.int32, (STRIP, cols), 0)
    sub0, sub1 = sub == 0, sub == STRIP - 1

    def plane(x, carry):
        @pl.when(x < planes - 1)
        def _():
            copy(0, x + 1).wait()
            copy(1, x + 1).wait()

        copy(2, x).wait()
        xn, xp = jnp.minimum(x + 1, planes - 1), jnp.maximum(x - 1, 0)
        h_prev = jnp.where(x > 0, 0.5, 0.0).astype(F32)
        h_next = jnp.where(x < planes - 1, 0.5, 0.0).astype(F32)
        dc = df = 0.0
        k0, v0 = k[x, sl[0], :], v[x, sl[0], :]
        ku, vu = upward(k0), upward(v0)
        res_sum = k_sum = None
        for r, a in enumerate(sl):
            c_z = 0.5 * (k0 + left(k0))
            f_z = c_z * (v0 - left(v0))
            diag = c_z + right(c_z)
            res = right(f_z) - f_z
            if r + 1 < n:
                k1, v1 = k[x, sl[r + 1], :], v[x, sl[r + 1], :]
                ku1, vu1 = upward(k1), upward(v1)
                c_y = 0.5 * (k0 + jnp.where(sub1, ku1, ku))
                f_y = c_y * (v0 - jnp.where(sub1, vu1, vu))
            else:
                c_y = jnp.where(sub1, 0.0, 0.5 * (k0 + ku))
                f_y = c_y * (v0 - vu)
            nc, nf = downward(c_y), downward(f_y)
            diag = diag + (c_y + jnp.where(sub0, dc, nc))
            res = res + (jnp.where(sub0, df, nf) - f_y)
            dc, df = nc, nf
            c_x = h_next * (k0 + k[xn, a, :])
            f_x = c_x * (v0 - v[xn, a, :])
            c_p = h_prev * (k0 + k[xp, a, :])
            f_p = c_p * (v[xp, a, :] - v0)
            diag = diag + ((c_p + c_x) + REACTION)
            res = res + ((f_p - f_x) + (s[x, a, :] - REACTION * v0))
            w = DAMPING / diag
            w_ref[x, a, :] = w
            f_ref[x, a, :] = w * res
            half = r * STRIP // F
            res_sum = res if r * STRIP % F == 0 else res_sum + res
            k_sum = k0 if r * STRIP % F == 0 else k_sum + k0
            if (r + 1) * STRIP % F == 0:
                sums[half * STRIP : (half + 1) * STRIP, :] += res_sum
                sums[(2 + half) * STRIP : (3 + half) * STRIP, :] += k_sum
            if r + 1 < n:
                k0, v0, ku, vu = k1, v1, ku1, vu1
        out_copy(0, x).start()
        out_copy(1, x).start()
        for place, y in ((low, 0), (high, rows - 1)):
            w_row[place, pl.ds(x, 1), :] = w_ref[x, y : y + 1, :]
            f_row[place, pl.ds(x, 1), :] = f_ref[x, y : y + 1, :]
        return carry

    lax.fori_loop(0, planes, plane, 0)
    for side, x in enumerate(edge_spots("gx", planes)):
        w_pl[side] = w_ref[x]
        f_pl[side] = f_ref[x]
    for x in range(planes):
        for i in range(2):
            out_copy(i, x).wait()


def cross(q_pl, q_row, pls, rws, sign):
    rows, planes = q_pl.shape[1], q_row.shape[1]
    for a in range(2):
        pls[a][...] = pls[a][...] + sign * q_pl[a]
        rws[a][...] = rws[a][...] + sign * q_row[a]
    for a, x in enumerate(edge_spots("gx", planes)):
        for b, y in enumerate(edge_spots("gy", rows)):
            px, py = pl.ds(x, 1), pl.ds(y, 1)
            pls[a][py, :] = pls[a][py, :] + sign * q_row[b, px, :]
            rws[b][px, :] = rws[b][px, :] + sign * q_pl[a, py, :]


def split3(a):
    one = a.astype(BF16)
    rest = a - one.astype(F32)
    two = rest.astype(BF16)
    three = (rest - two.astype(F32)).astype(BF16)
    return jnp.concatenate([one, two, three], 0)


def joined3(a):
    n = a.shape[0] // 3
    return a[:n] + a[n : 2 * n] + a[2 * n :]


def edge_kernel(
    wi_pl, fi_pl, wi_row, fi_row, pl_a, pl_b, rw_a, rw_b, xa, xb, ya, yb, sums,
    f_pl0, f_pl1, f_row0, f_row1, w_pl0, w_pl1, w_row0, w_row1, wc_pl, wc_row, payload,
    q_pl, q_row,
):
    rows, cols = f_pl0.shape
    f_pl, f_row, w_pl, w_row = (f_pl0, f_pl1), (f_row0, f_row1), (w_pl0, w_pl1), (w_row0, w_row1)
    for side, mine, other in ((0, pl_a, xa), (1, pl_b, xb)):
        c = 0.5 * (mine[1] + other[1])
        wc_pl[side] = c
        q_pl[side] = c * (mine[0] - other[0])
    for side, mine, other in ((0, rw_a, ya), (1, rw_b, yb)):
        c = 0.5 * (mine[1] + other[1])
        wc_row[side] = c
        q_row[side] = c * (mine[0] - other[0])
    for w, f, wi, fi in ((w_pl, f_pl, wi_pl, fi_pl), (w_row, f_row, wi_row, fi_row)):
        for side in range(2):
            diag = DAMPING / wi[side]
            w[side][...] = diag
            f[side][...] = fi[side] * (diag * (1.0 / DAMPING))
    cross(wc_pl, wc_row, w_pl, w_row, 1.0)
    cross(q_pl, q_row, f_pl, f_row, -1.0)
    for w, f, wc in ((w_pl, f_pl, wc_pl), (w_row, f_row, wc_row)):
        for side in range(2):
            inv = DAMPING / w[side][...]
            w[side][...] = inv
            f[side][...] = f[side][...] * inv
            wc[side] = wc[side] * inv
    low, high = low_high("gy")
    parts = []
    for half in range(rows // F):
        total = sums[half * STRIP : (half + 1) * STRIP, :]
        for side in range(2):
            for r in range(half * F // STRIP, (half + 1) * F // STRIP):
                total = total - q_pl[side, r * STRIP : (r + 1) * STRIP, :]
        if half == 0:
            for r in range(q_row.shape[1] // STRIP):
                total = total - q_row[low, r * STRIP : (r + 1) * STRIP, :]
        if half == rows // F - 1:
            for r in range(q_row.shape[1] // STRIP):
                total = total - q_row[high, r * STRIP : (r + 1) * STRIP, :]
        parts.append(total)
    parts.append(sums[2 * STRIP :, :])
    col = lax.broadcasted_iota(jnp.int32, (cols, cols // F), 0)
    cell = lax.broadcasted_iota(jnp.int32, (cols, cols // F), 1)
    gather = jnp.where(col // F == cell, 1.0, 0.0).astype(BF16)
    reduced = joined3(
        jnp.dot(split3(jnp.concatenate(parts, 0)), gather, preferred_element_type=F32)
    )
    means = [
        jnp.sum(reduced[i * STRIP : (i + 1) * STRIP], axis=0, keepdims=True) * (1.0 / F**3)
        for i in range(4)
    ]
    tile = jnp.concatenate(means + means, 0)
    for i in range(payload.shape[0] // STRIP):
        payload[i * STRIP : (i + 1) * STRIP, :] = tile


def put_edges(ref, x, e_pl0, e_pl1, e_row0, e_row1):
    planes, rows, _ = ref.shape
    for y, line in zip(edge_spots("gy", rows), (e_row0, e_row1)):
        ref[x, pl.ds(y, 1), :] = line[pl.ds(x, 1), :]
    for spot, plane in zip(edge_spots("gx", planes), (e_pl0, e_pl1)):

        @pl.when(x == spot)
        def _():
            ref[x] = plane[...]


def sweep_kernel(
    k_hbm, w_hbm, f_hbm, w_pl0, w_pl1, w_row0, w_row1, f_pl0, f_pl1, f_row0, f_row1,
    w, f, k, cy, cz, g_ref, g_pl, g_row, sems,
):
    planes, rows, cols = w.shape
    sl = strips(rows)
    low, high = low_high("gy")
    sub = lax.broadcasted_iota(jnp.int32, (STRIP, cols), 0)
    sub0, sub1 = sub == 0, sub == STRIP - 1

    def copy(i, x):
        src, dst = ((k_hbm, k), (f_hbm, f), (w_hbm, w))[i]
        return pltpu.make_async_copy(src.at[x], dst.at[x], sems.at[i, x])

    def arrive(x):
        for i in range(3):
            copy(i, x).wait()
        put_edges(f, x, f_pl0, f_pl1, f_row0, f_row1)
        put_edges(w, x, w_pl0, w_pl1, w_row0, w_row1)

    for x in range(planes):
        for i in range(3):
            copy(i, x).start()
    arrive(0)

    def plane(x, carry):
        @pl.when(x < planes - 1)
        def _():
            arrive(x + 1)

        xn = jnp.minimum(x + 1, planes - 1)
        h_next = jnp.where(x < planes - 1, 0.5, 0.0).astype(F32)
        h_prev = jnp.where(x > 0, 0.5, 0.0).astype(F32)
        xp = jnp.maximum(x - 1, 0)
        dn = 0.0
        k0, u0 = k[x, sl[0], :], f[x, sl[0], :]
        ku, uu = upward(k0), upward(u0)
        for r, a in enumerate(sl):
            c_z = 0.5 * (k0 + left(k0))
            total = c_z * left(u0) + right(c_z * u0)
            if r + 1 < len(sl):
                k1, u1 = k[x, sl[r + 1], :], f[x, sl[r + 1], :]
                ku1, uu1 = upward(k1), upward(u1)
                c_y = 0.5 * (k0 + jnp.where(sub1, ku1, ku))
                above = jnp.where(sub1, uu1, uu)
            else:
                c_y = jnp.where(sub1, 0.0, 0.5 * (k0 + ku))
                above = uu
            nd = downward(c_y * u0)
            total = total + (c_y * above + jnp.where(sub0, dn, nd))
            dn = nd
            c_x = h_next * (k0 + k[xn, a, :])
            c_p = h_prev * (k0 + k[xp, a, :])
            total = total + (c_x * f[xn, a, :] + c_p * f[xp, a, :])
            cy[x, a, :] = c_y
            cz[x, a, :] = c_z
            g_ref[x, a, :] = (2.0 - DAMPING) * u0 + w[x, a, :] * total
            if r + 1 < len(sl):
                k0, u0, ku, uu = k1, u1, ku1, uu1
        for place, y in ((low, 0), (high, rows - 1)):
            g_row[place, pl.ds(x, 1), :] = g_ref[x, y : y + 1, :]
        return carry

    lax.fori_loop(0, planes, plane, 0)
    for side, x in enumerate(edge_spots("gx", planes)):
        g_pl[side] = g_ref[x]


def mid_kernel(
    g_pl, g_row, wc_pl, wc_row, xa, xb, ya, yb, o_pl0, o_pl1, o_row0, o_row1, q_pl, q_row
):
    for side, x, y in ((0, xa, ya), (1, xb, yb)):
        q_pl[side] = wc_pl[side] * x[...]
        q_row[side] = wc_row[side] * y[...]
    for side, p, r in ((0, o_pl0, o_row0), (1, o_pl1, o_row1)):
        p[...] = g_pl[side]
        r[...] = g_row[side]
    cross(q_pl, q_row, (o_pl0, o_pl1), (o_row0, o_row1), 1.0)


def tile_sums(x, u, k, cy, cz):
    planes, rows, cols = u.shape
    sl = strips(rows)
    tl = [slice(j, j + LANES) for j in range(0, cols, LANES)]
    lane = lax.broadcasted_iota(jnp.int32, (STRIP, LANES), 1)
    sub = lax.broadcasted_iota(jnp.int32, (STRIP, LANES), 0)
    xn, xp = jnp.minimum(x + 1, planes - 1), jnp.maximum(x - 1, 0)
    h_next = jnp.where(x < planes - 1, 0.5, 0.0).astype(F32)
    h_prev = jnp.where(x > 0, 0.5, 0.0).astype(F32)
    ru = [left(u[x, a, tl[0]]) for a in sl]
    pm = [right(cz[x, a, tl[-1]] * u[x, a, tl[-1]]) for a in sl]
    for j, t in enumerate(tl):
        us = [u[x, a, t] for a in sl]
        uu = [upward(a) for a in us]
        dn = 0.0
        for r, a in enumerate(sl):
            u0, c_y, c_z = us[r], cy[x, a, t], cz[x, a, t]
            nu = left(u[x, a, tl[(j + 1) % len(tl)]])
            c_x = h_next * (k[x, a, t] + k[xn, a, t])
            c_p = h_prev * (k[x, a, t] + k[xp, a, t])
            total = c_x * u[xn, a, t] + c_p * u[xp, a, t]
            total = total + c_z * jnp.where(lane == LANES - 1, nu, ru[r])
            mu = right(c_z * u0)
            total = total + jnp.where(lane == 0, pm[r], mu)
            ru[r], pm[r] = nu, mu
            above = jnp.where(sub == STRIP - 1, uu[r + 1], uu[r]) if r + 1 < len(sl) else uu[r]
            nd = downward(c_y * u0)
            total = total + (c_y * above + jnp.where(sub == 0, dn, nd))
            dn = nd
            yield a, t, u0, total


def last_kernel(
    w, f, k, cy, cz, g_in, interp, g_pl0, g_pl1, g_row0, g_row1,
    out, body, g, sems,
):
    planes, rows, cols = w.shape

    def copy(x):
        return pltpu.make_async_copy(body.at[x], out.at[x], sems.at[x])

    def arrive(x):
        g[x] = g_in[x]
        put_edges(g, x, g_pl0, g_pl1, g_row0, g_row1)

    arrive(0)

    def plane(x, carry):
        @pl.when(x < planes - 1)
        def _():
            arrive(x + 1)

        offset = ((x % F).astype(F32) + 0.5) / F - 0.5
        weight = jnp.abs(offset)
        side = jnp.where(offset > 0, 2, 0)
        for a, t, u0, total in tile_sums(x, g, k, cy, cz):
            coarse = (1.0 - weight) * interp[1, a, t] + weight * interp[side, a, t]
            new = f[x, a, t] + (1.0 - DAMPING) * u0 + coarse
            body[x, a, t] = new + w[x, a, t] * total

        @pl.when((x > 0) & (x < planes - 1))
        def _():
            copy(x).start()

        return carry

    lax.fori_loop(0, planes, plane, 0)
    for x in range(1, planes - 1):
        copy(x).wait()


def finish_kernel(src, body, wc_pl, wc_row, xa, xb, ya, yb, out, s_pl, s_row, q_row, pl_sems, row_sems):
    del src
    planes, rows, cols = out.shape
    xs, ys = edge_spots("gx", planes), edge_spots("gy", rows)
    q_row[0] = wc_row[0] * ya[...]
    q_row[1] = wc_row[1] * yb[...]
    copies = []
    for i, (place, y) in enumerate(zip(low_high("gy"), (0, rows - 1))):
        mine = jnp.concatenate([body[x, y : y + 1, :] for x in range(planes)], 0)
        s_row[i] = mine + q_row[place]
        for x in range(1, planes - 1):
            copies.append(
                pltpu.make_async_copy(s_row.at[i, x], out.at[x, y, :], row_sems.at[i, x])
            )
            copies[-1].start()
    for side, other in ((0, xa), (1, xb)):
        x = xs[side]
        s_pl[side] = body[x] + wc_pl[side] * other[...]
        for b, y in enumerate(ys):
            py = pl.ds(y, 1)
            s_pl[side, py, :] = s_pl[side, py, :] + q_row[b, pl.ds(x, 1), :]
        copies.append(pltpu.make_async_copy(s_pl.at[side], out.at[x], pl_sems.at[side]))
        copies[-1].start()
    for c in copies:
        c.wait()


def coarse_kernel(got, interp, coef, b_ref, u_ref, *, nx, ny, rows):
    nz = got.shape[1]
    per = 2 * 2

    def field(start):
        return [
            jnp.stack([got[pl.ds(p * ny * per + start + t, ny, stride=per), :] for p in range(nx)], 0)
            for t in range(2)
        ]

    resid, cond = field(0), field(2)

    half = 0.5 * COARSE_FACTOR

    def up(a):
        return pltpu.roll(a, ny - 1, a.ndim - 2)

    def down(a):
        return pltpu.roll(a, 1, a.ndim - 2)

    def after(a):
        return pltpu.roll(a, nz - 1, a.ndim - 1)

    def before(a):
        return pltpu.roll(a, 1, a.ndim - 1)

    inside = half * (cond[0] + cond[1])
    across = half * (cond[1] + up(cond[0]))
    coef[2, 0], coef[2, 1] = inside, across
    for t in range(2):
        c_x = half * (cond[t] + jnp.concatenate([cond[t][1:], cond[t][:1]], 0))
        c_z = half * (cond[t] + after(cond[t]))
        diag = REACTION + (c_x + jnp.concatenate([c_x[-1:], c_x[:-1]], 0))
        diag = diag + (c_z + before(c_z)) + (inside + (across if t else down(across)))
        inv = DAMPING / diag
        coef[0, t], coef[1, t], coef[3, t] = c_x, c_z, inv
        b_ref[t] = inv * resid[t]
        u_ref[0, t] = b_ref[t]

    def sweep(src, dst):
        prv, cur = [[u_ref[src, t, p] for t in range(2)] for p in (nx - 1, 0)]
        c_prv = [coef[0, t, nx - 1] for t in range(2)]
        for p in range(nx):
            nxt = [u_ref[src, t, (p + 1) % nx] for t in range(2)]
            c_x = [coef[0, t, p] for t in range(2)]
            c_in, c_ac = coef[2, 0, p], coef[2, 1, p]
            rows_part = (
                c_in * cur[1] + down(c_ac * cur[1]),
                c_in * cur[0] + c_ac * up(cur[0]),
            )
            for t in range(2):
                c_z = coef[1, t, p]
                total = (c_x[t] * nxt[t] + c_prv[t] * prv[t]) + rows_part[t]
                total = total + (c_z * after(cur[t]) + before(c_z * cur[t]))
                new = (b_ref[t, p] + (1.0 - DAMPING) * cur[t]) + coef[3, t, p] * total
                u_ref[dst, t, p] = new
            prv, cur, c_prv = cur, nxt, c_x

    def pair(i, carry):
        sweep(0, 1)
        sweep(1, 0)
        return carry

    steps = CSWEEPS - 1
    lax.fori_loop(0, steps // 2, pair, 0)
    last = 0
    if steps % 2:
        sweep(0, 1)
        last = 1

    gx, gy = lax.axis_index("gx"), lax.axis_index("gy")
    lines = []
    for d in (-1, 0, 1):
        p = lax.rem(gx + d + nx, nx)
        prev_s, next_s = lax.rem(gy + ny - 1, ny), lax.rem(gy + 1, ny)
        for t, s in ((1, prev_s), (0, gy), (1, gy), (0, next_s)):
            lines.append(u_ref[last, t, p, pl.ds(s, 1), :])
    lines = jnp.concatenate(lines + lines[:4], 0)
    cols = nz * F
    cell = lax.broadcasted_iota(jnp.int32, (nz, cols), 0)
    col = lax.broadcasted_iota(jnp.int32, (nz, cols), 1)
    base = col // F
    offset = ((col % F).astype(F32) + 0.5) / F - 0.5
    side = jnp.where(offset > 0, base + 1, base - 1)
    side = jnp.where(side < 0, side + nz, jnp.where(side >= nz, side - nz, side))
    weight = jnp.abs(offset)
    matrix = jnp.where(cell == base, 1.0 - weight, 0.0) + jnp.where(cell == side, weight, 0.0)
    wide = joined3(jnp.dot(split3(lines), matrix.astype(BF16), preferred_element_type=F32))
    sub = lax.broadcasted_iota(jnp.int32, (STRIP, cols), 0)
    for plane in range(3):
        for r in range(rows // STRIP):
            row = r * STRIP + sub
            off = ((row % F).astype(F32) + 0.5) / F - 0.5
            wt = jnp.abs(off)
            block = r * STRIP // F
            near = block + 1
            far = near + (1 if (r * STRIP) % F >= F // 2 else -1)
            a = wide[plane * 4 + near : plane * 4 + near + 1]
            c = wide[plane * 4 + far : plane * 4 + far + 1]
            interp[plane, r * STRIP : (r + 1) * STRIP, :] = (1.0 - wt) * a + wt * c


def swap(axis, first, second):
    count = lax.axis_size(axis)
    pairs = [(i, i ^ 1) for i in range(count)]
    others = [(i, (i + 1 if i % 2 else i - 1) % count) for i in range(count)]
    return lax.ppermute(first, axis, pairs), lax.ppermute(second, axis, others)


def per_device(nx, ny, v, s, k):
    planes, rows, cols = v.shape
    n = planes * rows * cols
    vm = pltpu.VMEM
    dma = pltpu.SemaphoreType.DMA
    full, edge, line = sds(planes, rows, cols), sds(rows, cols), sds(planes, cols)
    edges, lines = sds(2, rows, cols), sds(2, planes, cols)

    pl_a, pl_b = pl.pallas_call(
        planes_kernel,
        out_shape=(edges, edges),
        in_specs=[HBM] * 2,
        out_specs=(VM,) * 2,
        scratch_shapes=[dma((2, 2))],
        compiler_params=params(50),
        cost_estimate=cost(0, n // 4),
        name="planes",
    )(v, k)
    xa, xb = swap("gx", pl_a, pl_b)
    rw_a, rw_b = pl.pallas_call(
        rows_kernel,
        out_shape=(lines, lines),
        in_specs=[HBM] * 2,
        out_specs=(VM,) * 2,
        scratch_shapes=[dma((2, 2))],
        compiler_params=params(50),
        cost_estimate=cost(0, n // 4),
        name="rows",
    )(v, k)
    ya, yb = swap("gy", rw_a, rw_b)

    w, f, wi_pl, fi_pl, wi_row, fi_row, sums = pl.pallas_call(
        inner_kernel,
        out_shape=(full, full, edges, edges, lines, lines, sds(4 * STRIP, cols)),
        in_specs=[HBM] * 3,
        out_specs=(HBM,) * 2 + (VM,) * 5,
        scratch_shapes=[vm(full.shape, F32)] * 5
        + [dma((3, planes)), dma((2, planes))],
        compiler_params=params(52),
        cost_estimate=cost(50 * n, 20 * n),
        name="inner",
    )(v, s, k)

    devices = nx * ny
    out = pl.pallas_call(
        edge_kernel,
        out_shape=(edge, edge, line, line) * 2 + (edges, lines, sds(devices * 4, cols // F)),
        in_specs=[VM] * 13,
        out_specs=(VM,) * 11,
        scratch_shapes=[vm(edges.shape, F32), vm(lines.shape, F32)],
        compiler_params=params(6),
        cost_estimate=cost(10 * n // 8, n),
        name="edge",
    )(wi_pl, fi_pl, wi_row, fi_row, pl_a, pl_b, rw_a, rw_b, xa, xb, ya, yb, sums)
    f_edges, w_edges, (wc_pl, wc_row, payload) = out[:4], out[4:8], out[8:]

    fya, fyb = swap("gy", f_edges[2], f_edges[3])
    fxa, fxb = swap("gx", f_edges[0], f_edges[1])
    got = lax.all_to_all(payload, ("gx", "gy"), 0, 0, tiled=True)

    got, w, f, k = lax.optimization_barrier((got, w, f, k))

    w, f, k, cy, cz, g, g_pl, g_row = pl.pallas_call(
        sweep_kernel,
        out_shape=(full,) * 6 + (edges, lines),
        in_specs=[HBM] * 3 + [VM] * 8,
        out_specs=(VM,) * 8,
        scratch_shapes=[dma((3, planes))],
        compiler_params=params(26),
        cost_estimate=cost(40 * n, 12 * n),
        name="sweep",
    )(k, w, f, *w_edges, *f_edges)

    g_edges = pl.pallas_call(
        mid_kernel,
        out_shape=(edge, edge, line, line),
        in_specs=[VM] * 8,
        out_specs=(VM,) * 4,
        scratch_shapes=[vm(edges.shape, F32), vm(lines.shape, F32)],
        compiler_params=params(4),
        cost_estimate=cost(n // 8, n // 2),
        name="mid",
    )(g_pl, g_row, wc_pl, wc_row, fxa, fxb, fya, fyb)

    gya, gyb = swap("gy", g_edges[2], g_edges[3])
    gxa, gxb = swap("gx", g_edges[0], g_edges[1])

    cells = (nx, ny, cols // F)
    interp = pl.pallas_call(
        functools.partial(coarse_kernel, nx=nx, ny=ny, rows=rows),
        out_shape=sds(3, rows, cols),
        in_specs=[VM],
        out_specs=VM,
        scratch_shapes=[
            vm((4, 2) + cells, F32),
            vm((2,) + cells, F32),
            vm((2, 2) + cells, F32),
        ],
        compiler_params=params(8),
        cost_estimate=cost(20 * n, n),
        name="coarse",
    )(got)

    b_side = sds(planes - 2, STRIP, cols)
    out, body = pl.pallas_call(
        last_kernel,
        out_shape=(full, full),
        in_specs=[VM] * 11,
        out_specs=(HBM, VM),
        scratch_shapes=[vm(full.shape, F32), dma((planes,))],
        compiler_params=params(22),
        cost_estimate=cost(40 * n, 20 * n),
        name="last",
    )(w, f, k, cy, cz, g, interp, *g_edges)

    return pl.pallas_call(
        finish_kernel,
        out_shape=full,
        in_specs=[HBM] + [VM] * 7,
        out_specs=HBM,
        scratch_shapes=[
            vm(edges.shape, F32), vm(lines.shape, F32), vm(lines.shape, F32),
            dma((2,)), dma((2, planes)),
        ],
        input_output_aliases={0: 0},
        compiler_params=params(6),
        cost_estimate=cost(n // 4, 3 * n),
        name="finish",
    )(out, body, wc_pl, wc_row, gxa, gxb, gya, gyb)


def solution(mesh):
    placed = P("gx", "gy", None)
    body = functools.partial(per_device, mesh.shape["gx"], mesh.shape["gy"])
    return jax.shard_map(
        body, mesh=mesh, in_specs=(placed,) * 3, out_specs=placed, check_vma=False
    )
```

```python
import functools
import jax
import jax.numpy as jnp
from jax import lax
from jax.experimental import pallas as pl
from jax.experimental.pallas import tpu as pltpu
from jax.sharding import PartitionSpec as P

F = 16
CSWEEPS = 32
REACTION = 0.2
DAMPING = 0.8
COARSE_FACTOR = 0.25
F32 = jnp.float32
BF16 = jnp.bfloat16
STRIP = 8
LANES = 512

VM = pl.BlockSpec(memory_space=pltpu.VMEM)
ANY = pl.BlockSpec(memory_space=pl.ANY)
HBM = pl.BlockSpec(memory_space=pltpu.HBM)


def params(mib):
    return pltpu.CompilerParams(vmem_limit_bytes=mib * 1024 * 1024)


def cost(flops, nbytes):
    return pl.CostEstimate(flops=int(flops), bytes_accessed=int(nbytes), transcendentals=0)


def sds(*shape):
    return jax.ShapeDtypeStruct(shape, F32)


def left(a):
    return pltpu.roll(a, a.shape[1] - 1, 1)


def right(a):
    return pltpu.roll(a, 1, 1)


def upward(a):
    return pltpu.roll(a, STRIP - 1, 0)


def downward(a):
    return pltpu.roll(a, 1, 0)


def strips(rows):
    return [slice(r * STRIP, (r + 1) * STRIP) for r in range(rows // STRIP)]


def edge_spots(axis, count):
    odd = lax.rem(lax.axis_index(axis), 2)
    return (1 - odd) * (count - 1), odd * (count - 1)


def low_high(axis):
    odd = lax.rem(lax.axis_index(axis), 2)
    return 1 - odd, odd


def planes_kernel(v, k, pl_a, pl_b, sems):
    copies = [
        pltpu.make_async_copy(src.at[x], dst.at[i], sems.at[i, j])
        for i, src in enumerate((v, k))
        for j, (x, dst) in enumerate(zip(edge_spots("gx", v.shape[0]), (pl_a, pl_b)))
    ]
    for c in copies:
        c.start()
    for c in copies:
        c.wait()


def rows_kernel(v, k, rw_a, rw_b, sems):
    copies = [
        pltpu.make_async_copy(src.at[:, y, :], dst.at[i], sems.at[i, j])
        for i, src in enumerate((v, k))
        for j, (y, dst) in enumerate(zip(edge_spots("gy", v.shape[1]), (rw_a, rw_b)))
    ]
    for c in copies:
        c.start()
    for c in copies:
        c.wait()


def inner_kernel(
    v_hbm, s_hbm, k_hbm,
    w_hbm, f_hbm, w_pl, f_pl, w_row, f_row, sums,
    v, s, k, w_ref, f_ref, sems, out_sems,
):
    planes, rows, cols = v.shape
    sl = strips(rows)
    n = len(sl)
    low, high = low_high("gy")

    def copy(i, x):
        src, dst = ((k_hbm, k), (v_hbm, v), (s_hbm, s))[i]
        return pltpu.make_async_copy(src.at[x], dst.at[x], sems.at[i, x])

    def out_copy(i, x):
        src, dst = ((w_ref, w_hbm), (f_ref, f_hbm))[i]
        return pltpu.make_async_copy(src.at[x], dst.at[x], out_sems.at[i, x])

    for x in range(planes):
        for i in range(3):
            copy(i, x).start()
    sums[...] = jnp.zeros_like(sums)
    copy(0, 0).wait()
    copy(1, 0).wait()
    sub = lax.broadcasted_iota(jnp.int32, (STRIP, cols), 0)
    sub0, sub1 = sub == 0, sub == STRIP - 1

    def plane(x, carry):
        @pl.when(x < planes - 1)
        def _():
            copy(0, x + 1).wait()
            copy(1, x + 1).wait()

        copy(2, x).wait()
        xn, xp = jnp.minimum(x + 1, planes - 1), jnp.maximum(x - 1, 0)
        h_prev = jnp.where(x > 0, 0.5, 0.0).astype(F32)
        h_next = jnp.where(x < planes - 1, 0.5, 0.0).astype(F32)
        dc = df = 0.0
        k0, v0 = k[x, sl[0], :], v[x, sl[0], :]
        ku, vu = upward(k0), upward(v0)
        res_sum = k_sum = None
        for r, a in enumerate(sl):
            c_z = 0.5 * (k0 + left(k0))
            f_z = c_z * (v0 - left(v0))
            diag = c_z + right(c_z)
            res = right(f_z) - f_z
            if r + 1 < n:
                k1, v1 = k[x, sl[r + 1], :], v[x, sl[r + 1], :]
                ku1, vu1 = upward(k1), upward(v1)
                c_y = 0.5 * (k0 + jnp.where(sub1, ku1, ku))
                f_y = c_y * (v0 - jnp.where(sub1, vu1, vu))
            else:
                c_y = jnp.where(sub1, 0.0, 0.5 * (k0 + ku))
                f_y = c_y * (v0 - vu)
            nc, nf = downward(c_y), downward(f_y)
            diag = diag + (c_y + jnp.where(sub0, dc, nc))
            res = res + (jnp.where(sub0, df, nf) - f_y)
            dc, df = nc, nf
            c_x = h_next * (k0 + k[xn, a, :])
            f_x = c_x * (v0 - v[xn, a, :])
            c_p = h_prev * (k0 + k[xp, a, :])
            f_p = c_p * (v[xp, a, :] - v0)
            diag = diag + ((c_p + c_x) + REACTION)
            res = res + ((f_p - f_x) + (s[x, a, :] - REACTION * v0))
            w = DAMPING / diag
            w_ref[x, a, :] = w
            f_ref[x, a, :] = w * res
            half = r * STRIP // F
            res_sum = res if r * STRIP % F == 0 else res_sum + res
            k_sum = k0 if r * STRIP % F == 0 else k_sum + k0
            if (r + 1) * STRIP % F == 0:
                sums[half * STRIP : (half + 1) * STRIP, :] += res_sum
                sums[(2 + half) * STRIP : (3 + half) * STRIP, :] += k_sum
            if r + 1 < n:
                k0, v0, ku, vu = k1, v1, ku1, vu1
        out_copy(0, x).start()
        out_copy(1, x).start()
        for place, y in ((low, 0), (high, rows - 1)):
            w_row[place, pl.ds(x, 1), :] = w_ref[x, y : y + 1, :]
            f_row[place, pl.ds(x, 1), :] = f_ref[x, y : y + 1, :]
        return carry

    lax.fori_loop(0, planes, plane, 0)
    for side, x in enumerate(edge_spots("gx", planes)):
        w_pl[side] = w_ref[x]
        f_pl[side] = f_ref[x]
    for x in range(planes):
        for i in range(2):
            out_copy(i, x).wait()


def cross(q_pl, q_row, pls, rws, sign):
    rows, planes = q_pl.shape[1], q_row.shape[1]
    for a in range(2):
        pls[a][...] = pls[a][...] + sign * q_pl[a]
        rws[a][...] = rws[a][...] + sign * q_row[a]
    for a, x in enumerate(edge_spots("gx", planes)):
        for b, y in enumerate(edge_spots("gy", rows)):
            px, py = pl.ds(x, 1), pl.ds(y, 1)
            pls[a][py, :] = pls[a][py, :] + sign * q_row[b, px, :]
            rws[b][px, :] = rws[b][px, :] + sign * q_pl[a, py, :]


def split3(a):
    one = a.astype(BF16)
    rest = a - one.astype(F32)
    two = rest.astype(BF16)
    three = (rest - two.astype(F32)).astype(BF16)
    return jnp.concatenate([one, two, three], 0)


def joined3(a):
    n = a.shape[0] // 3
    return a[:n] + a[n : 2 * n] + a[2 * n :]


def edge_kernel(
    wi_pl, fi_pl, wi_row, fi_row, pl_a, pl_b, rw_a, rw_b, xa, xb, ya, yb, sums,
    f_pl0, f_pl1, f_row0, f_row1, w_pl0, w_pl1, w_row0, w_row1, wc_pl, wc_row, payload,
    q_pl, q_row,
):
    rows, cols = f_pl0.shape
    f_pl, f_row, w_pl, w_row = (f_pl0, f_pl1), (f_row0, f_row1), (w_pl0, w_pl1), (w_row0, w_row1)
    for side, mine, other in ((0, pl_a, xa), (1, pl_b, xb)):
        c = 0.5 * (mine[1] + other[1])
        wc_pl[side] = c
        q_pl[side] = c * (mine[0] - other[0])
    for side, mine, other in ((0, rw_a, ya), (1, rw_b, yb)):
        c = 0.5 * (mine[1] + other[1])
        wc_row[side] = c
        q_row[side] = c * (mine[0] - other[0])
    for w, f, wi, fi in ((w_pl, f_pl, wi_pl, fi_pl), (w_row, f_row, wi_row, fi_row)):
        for side in range(2):
            diag = DAMPING / wi[side]
            w[side][...] = diag
            f[side][...] = fi[side] * (diag * (1.0 / DAMPING))
    cross(wc_pl, wc_row, w_pl, w_row, 1.0)
    cross(q_pl, q_row, f_pl, f_row, -1.0)
    for w, f, wc in ((w_pl, f_pl, wc_pl), (w_row, f_row, wc_row)):
        for side in range(2):
            inv = DAMPING / w[side][...]
            w[side][...] = inv
            f[side][...] = f[side][...] * inv
            wc[side] = wc[side] * inv
    low, high = low_high("gy")
    parts = []
    for half in range(rows // F):
        total = sums[half * STRIP : (half + 1) * STRIP, :]
        for side in range(2):
            for r in range(half * F // STRIP, (half + 1) * F // STRIP):
                total = total - q_pl[side, r * STRIP : (r + 1) * STRIP, :]
        if half == 0:
            for r in range(q_row.shape[1] // STRIP):
                total = total - q_row[low, r * STRIP : (r + 1) * STRIP, :]
        if half == rows // F - 1:
            for r in range(q_row.shape[1] // STRIP):
                total = total - q_row[high, r * STRIP : (r + 1) * STRIP, :]
        parts.append(total)
    parts.append(sums[2 * STRIP :, :])
    col = lax.broadcasted_iota(jnp.int32, (cols, cols // F), 0)
    cell = lax.broadcasted_iota(jnp.int32, (cols, cols // F), 1)
    gather = jnp.where(col // F == cell, 1.0, 0.0).astype(BF16)
    reduced = joined3(
        jnp.dot(split3(jnp.concatenate(parts, 0)), gather, preferred_element_type=F32)
    )
    means = [
        jnp.sum(reduced[i * STRIP : (i + 1) * STRIP], axis=0, keepdims=True) * (1.0 / F**3)
        for i in range(4)
    ]
    tile = jnp.concatenate(means + means, 0)
    for i in range(payload.shape[0] // STRIP):
        payload[i * STRIP : (i + 1) * STRIP, :] = tile


def put_edges(ref, x, e_pl0, e_pl1, e_row0, e_row1):
    planes, rows, _ = ref.shape
    for y, line in zip(edge_spots("gy", rows), (e_row0, e_row1)):
        ref[x, pl.ds(y, 1), :] = line[pl.ds(x, 1), :]
    for spot, plane in zip(edge_spots("gx", planes), (e_pl0, e_pl1)):

        @pl.when(x == spot)
        def _():
            ref[x] = plane[...]


def moved(r, d):
    return slice(r * STRIP + d, (r + 1) * STRIP + d)


def sweep_kernel(
    k_hbm, w_hbm, f_hbm, w_pl0, w_pl1, w_row0, w_row1, f_pl0, f_pl1, f_row0, f_row1,
    w, f, k, cy, cz, g_ref, g_pl, g_row, sems,
):
    planes, rows, cols = w.shape
    sl = strips(rows)
    low, high = low_high("gy")
    sub = lax.broadcasted_iota(jnp.int32, (STRIP, cols), 0)
    sub0, sub1 = sub == 0, sub == STRIP - 1

    def copy(i, x):
        src, dst = ((k_hbm, k), (f_hbm, f), (w_hbm, w))[i]
        return pltpu.make_async_copy(src.at[x], dst.at[x], sems.at[i, x])

    def arrive(x):
        for i in range(3):
            copy(i, x).wait()
        put_edges(f, x, f_pl0, f_pl1, f_row0, f_row1)
        put_edges(w, x, w_pl0, w_pl1, w_row0, w_row1)

    for x in range(planes):
        for i in range(3):
            copy(i, x).start()
    arrive(0)

    def plane(x, carry):
        @pl.when(x < planes - 1)
        def _():
            arrive(x + 1)

        xn = jnp.minimum(x + 1, planes - 1)
        h_next = jnp.where(x < planes - 1, 0.5, 0.0).astype(F32)
        h_prev = jnp.where(x > 0, 0.5, 0.0).astype(F32)
        xp = jnp.maximum(x - 1, 0)
        n = len(sl)
        for r, a in enumerate(sl):
            k0, u0 = k[x, a, :], f[x, a, :]
            c_z = 0.5 * (k0 + left(k0))
            total = c_z * left(u0) + right(c_z * u0)
            above, below = moved(r, 1), moved(r, -1)
            if r + 1 < n:
                c_y = 0.5 * (k0 + k[x, above, :])
                total = total + c_y * f[x, above, :]
            else:
                c_y = jnp.where(sub1, 0.0, 0.5 * (k0 + upward(k0)))
                total = total + c_y * upward(u0)
            if r > 0:
                total = total + 0.5 * (k0 + k[x, below, :]) * f[x, below, :]
            else:
                total = total + jnp.where(sub0, 0.0, downward(c_y * u0))
            c_x = h_next * (k0 + k[xn, a, :])
            c_p = h_prev * (k0 + k[xp, a, :])
            total = total + (c_x * f[xn, a, :] + c_p * f[xp, a, :])
            cy[x, a, :] = c_y
            cz[x, a, :] = c_z
            g_ref[x, a, :] = (2.0 - DAMPING) * u0 + w[x, a, :] * total
        for place, y in ((low, 0), (high, rows - 1)):
            g_row[place, pl.ds(x, 1), :] = g_ref[x, y : y + 1, :]
        return carry

    lax.fori_loop(0, planes, plane, 0)
    for side, x in enumerate(edge_spots("gx", planes)):
        g_pl[side] = g_ref[x]


def mid_kernel(
    g_pl, g_row, wc_pl, wc_row, xa, xb, ya, yb, o_pl0, o_pl1, o_row0, o_row1, q_pl, q_row
):
    for side, x, y in ((0, xa, ya), (1, xb, yb)):
        q_pl[side] = wc_pl[side] * x[...]
        q_row[side] = wc_row[side] * y[...]
    for side, p, r in ((0, o_pl0, o_row0), (1, o_pl1, o_row1)):
        p[...] = g_pl[side]
        r[...] = g_row[side]
    cross(q_pl, q_row, (o_pl0, o_pl1), (o_row0, o_row1), 1.0)


def tile_sums(x, u, k, cy, cz):
    planes, rows, cols = u.shape
    sl = strips(rows)
    tl = [slice(j, j + LANES) for j in range(0, cols, LANES)]
    lane = lax.broadcasted_iota(jnp.int32, (STRIP, LANES), 1)
    sub = lax.broadcasted_iota(jnp.int32, (STRIP, LANES), 0)
    xn, xp = jnp.minimum(x + 1, planes - 1), jnp.maximum(x - 1, 0)
    h_next = jnp.where(x < planes - 1, 0.5, 0.0).astype(F32)
    h_prev = jnp.where(x > 0, 0.5, 0.0).astype(F32)
    ru = [left(u[x, a, tl[0]]) for a in sl]
    pm = [right(cz[x, a, tl[-1]] * u[x, a, tl[-1]]) for a in sl]
    for j, t in enumerate(tl):
        for r, a in enumerate(sl):
            u0, c_y, c_z = u[x, a, t], cy[x, a, t], cz[x, a, t]
            nu = left(u[x, a, tl[(j + 1) % len(tl)]])
            c_x = h_next * (k[x, a, t] + k[xn, a, t])
            c_p = h_prev * (k[x, a, t] + k[xp, a, t])
            total = c_x * u[xn, a, t] + c_p * u[xp, a, t]
            total = total + c_z * jnp.where(lane == LANES - 1, nu, ru[r])
            mu = right(c_z * u0)
            total = total + jnp.where(lane == 0, pm[r], mu)
            ru[r], pm[r] = nu, mu
            if r + 1 < len(sl):
                total = total + c_y * u[x, moved(r, 1), t]
            else:
                total = total + c_y * upward(u0)
            if r > 0:
                total = total + cy[x, moved(r, -1), t] * u[x, moved(r, -1), t]
            else:
                total = total + jnp.where(sub == 0, 0.0, downward(c_y * u0))
            yield a, t, u0, total


def last_kernel(
    w, f, k, cy, cz, g_in, interp, g_pl0, g_pl1, g_row0, g_row1,
    out, body, g, sems,
):
    planes, rows, cols = w.shape

    def copy(x):
        return pltpu.make_async_copy(body.at[x], out.at[x], sems.at[x])

    def arrive(x):
        g[x] = g_in[x]
        put_edges(g, x, g_pl0, g_pl1, g_row0, g_row1)

    arrive(0)

    def plane(x, carry):
        @pl.when(x < planes - 1)
        def _():
            arrive(x + 1)

        offset = ((x % F).astype(F32) + 0.5) / F - 0.5
        weight = jnp.abs(offset)
        side = jnp.where(offset > 0, 2, 0)
        for a, t, u0, total in tile_sums(x, g, k, cy, cz):
            coarse = (1.0 - weight) * interp[1, a, t] + weight * interp[side, a, t]
            new = f[x, a, t] + (1.0 - DAMPING) * u0 + coarse
            body[x, a, t] = new + w[x, a, t] * total

        @pl.when((x > 0) & (x < planes - 1))
        def _():
            copy(x).start()

        return carry

    lax.fori_loop(0, planes, plane, 0)
    for x in range(1, planes - 1):
        copy(x).wait()


def finish_kernel(src, body, wc_pl, wc_row, xa, xb, ya, yb, out, s_pl, s_row, q_row, pl_sems, row_sems):
    del src
    planes, rows, cols = out.shape
    xs, ys = edge_spots("gx", planes), edge_spots("gy", rows)
    q_row[0] = wc_row[0] * ya[...]
    q_row[1] = wc_row[1] * yb[...]
    copies = []
    for i, (place, y) in enumerate(zip(low_high("gy"), (0, rows - 1))):
        mine = jnp.concatenate([body[x, y : y + 1, :] for x in range(planes)], 0)
        s_row[i] = mine + q_row[place]
        for x in range(1, planes - 1):
            copies.append(
                pltpu.make_async_copy(s_row.at[i, x], out.at[x, y, :], row_sems.at[i, x])
            )
            copies[-1].start()
    for side, other in ((0, xa), (1, xb)):
        x = xs[side]
        s_pl[side] = body[x] + wc_pl[side] * other[...]
        for b, y in enumerate(ys):
            py = pl.ds(y, 1)
            s_pl[side, py, :] = s_pl[side, py, :] + q_row[b, pl.ds(x, 1), :]
        copies.append(pltpu.make_async_copy(s_pl.at[side], out.at[x], pl_sems.at[side]))
        copies[-1].start()
    for c in copies:
        c.wait()


def coarse_kernel(got, interp, coef, b_ref, u_ref, *, nx, ny, rows):
    nz = got.shape[1]
    per = 2 * 2

    def field(start):
        return [
            jnp.stack([got[pl.ds(p * ny * per + start + t, ny, stride=per), :] for p in range(nx)], 0)
            for t in range(2)
        ]

    resid, cond = field(0), field(2)

    half = 0.5 * COARSE_FACTOR

    def up(a):
        return pltpu.roll(a, ny - 1, a.ndim - 2)

    def down(a):
        return pltpu.roll(a, 1, a.ndim - 2)

    def after(a):
        return pltpu.roll(a, nz - 1, a.ndim - 1)

    def before(a):
        return pltpu.roll(a, 1, a.ndim - 1)

    inside = half * (cond[0] + cond[1])
    across = half * (cond[1] + up(cond[0]))
    coef[2, 0], coef[2, 1] = inside, across
    for t in range(2):
        c_x = half * (cond[t] + jnp.concatenate([cond[t][1:], cond[t][:1]], 0))
        c_z = half * (cond[t] + after(cond[t]))
        diag = REACTION + (c_x + jnp.concatenate([c_x[-1:], c_x[:-1]], 0))
        diag = diag + (c_z + before(c_z)) + (inside + (across if t else down(across)))
        inv = DAMPING / diag
        coef[0, t], coef[1, t], coef[3, t] = c_x, c_z, inv
        b_ref[t] = inv * resid[t]
        u_ref[0, t] = b_ref[t]

    def sweep(src, dst):
        prv, cur = [[u_ref[src, t, p] for t in range(2)] for p in (nx - 1, 0)]
        c_prv = [coef[0, t, nx - 1] for t in range(2)]
        for p in range(nx):
            nxt = [u_ref[src, t, (p + 1) % nx] for t in range(2)]
            c_x = [coef[0, t, p] for t in range(2)]
            c_in, c_ac = coef[2, 0, p], coef[2, 1, p]
            rows_part = (
                c_in * cur[1] + down(c_ac * cur[1]),
                c_in * cur[0] + c_ac * up(cur[0]),
            )
            for t in range(2):
                c_z = coef[1, t, p]
                total = (c_x[t] * nxt[t] + c_prv[t] * prv[t]) + rows_part[t]
                total = total + (c_z * after(cur[t]) + before(c_z * cur[t]))
                new = (b_ref[t, p] + (1.0 - DAMPING) * cur[t]) + coef[3, t, p] * total
                u_ref[dst, t, p] = new
            prv, cur, c_prv = cur, nxt, c_x

    def pair(i, carry):
        sweep(0, 1)
        sweep(1, 0)
        return carry

    steps = CSWEEPS - 1
    lax.fori_loop(0, steps // 2, pair, 0)
    last = 0
    if steps % 2:
        sweep(0, 1)
        last = 1

    gx, gy = lax.axis_index("gx"), lax.axis_index("gy")
    lines = []
    for d in (-1, 0, 1):
        p = lax.rem(gx + d + nx, nx)
        prev_s, next_s = lax.rem(gy + ny - 1, ny), lax.rem(gy + 1, ny)
        for t, s in ((1, prev_s), (0, gy), (1, gy), (0, next_s)):
            lines.append(u_ref[last, t, p, pl.ds(s, 1), :])
    lines = jnp.concatenate(lines + lines[:4], 0)
    cols = nz * F
    cell = lax.broadcasted_iota(jnp.int32, (nz, cols), 0)
    col = lax.broadcasted_iota(jnp.int32, (nz, cols), 1)
    base = col // F
    offset = ((col % F).astype(F32) + 0.5) / F - 0.5
    side = jnp.where(offset > 0, base + 1, base - 1)
    side = jnp.where(side < 0, side + nz, jnp.where(side >= nz, side - nz, side))
    weight = jnp.abs(offset)
    matrix = jnp.where(cell == base, 1.0 - weight, 0.0) + jnp.where(cell == side, weight, 0.0)
    wide = joined3(jnp.dot(split3(lines), matrix.astype(BF16), preferred_element_type=F32))
    sub = lax.broadcasted_iota(jnp.int32, (STRIP, cols), 0)
    for plane in range(3):
        for r in range(rows // STRIP):
            row = r * STRIP + sub
            off = ((row % F).astype(F32) + 0.5) / F - 0.5
            wt = jnp.abs(off)
            block = r * STRIP // F
            near = block + 1
            far = near + (1 if (r * STRIP) % F >= F // 2 else -1)
            a = wide[plane * 4 + near : plane * 4 + near + 1]
            c = wide[plane * 4 + far : plane * 4 + far + 1]
            interp[plane, r * STRIP : (r + 1) * STRIP, :] = (1.0 - wt) * a + wt * c


def swap(axis, first, second):
    count = lax.axis_size(axis)
    pairs = [(i, i ^ 1) for i in range(count)]
    others = [(i, (i + 1 if i % 2 else i - 1) % count) for i in range(count)]
    return lax.ppermute(first, axis, pairs), lax.ppermute(second, axis, others)


def per_device(nx, ny, v, s, k):
    planes, rows, cols = v.shape
    n = planes * rows * cols
    vm = pltpu.VMEM
    dma = pltpu.SemaphoreType.DMA
    full, edge, line = sds(planes, rows, cols), sds(rows, cols), sds(planes, cols)
    edges, lines = sds(2, rows, cols), sds(2, planes, cols)

    pl_a, pl_b = pl.pallas_call(
        planes_kernel,
        out_shape=(edges, edges),
        in_specs=[HBM] * 2,
        out_specs=(VM,) * 2,
        scratch_shapes=[dma((2, 2))],
        compiler_params=params(50),
        cost_estimate=cost(0, n // 4),
        name="planes",
    )(v, k)
    xa, xb = swap("gx", pl_a, pl_b)
    rw_a, rw_b = pl.pallas_call(
        rows_kernel,
        out_shape=(lines, lines),
        in_specs=[HBM] * 2,
        out_specs=(VM,) * 2,
        scratch_shapes=[dma((2, 2))],
        compiler_params=params(50),
        cost_estimate=cost(0, n // 4),
        name="rows",
    )(v, k)
    ya, yb = swap("gy", rw_a, rw_b)

    w, f, wi_pl, fi_pl, wi_row, fi_row, sums = pl.pallas_call(
        inner_kernel,
        out_shape=(full, full, edges, edges, lines, lines, sds(4 * STRIP, cols)),
        in_specs=[HBM] * 3,
        out_specs=(HBM,) * 2 + (VM,) * 5,
        scratch_shapes=[vm(full.shape, F32)] * 5
        + [dma((3, planes)), dma((2, planes))],
        compiler_params=params(52),
        cost_estimate=cost(50 * n, 20 * n),
        name="inner",
    )(v, s, k)

    devices = nx * ny
    out = pl.pallas_call(
        edge_kernel,
        out_shape=(edge, edge, line, line) * 2 + (edges, lines, sds(devices * 4, cols // F)),
        in_specs=[VM] * 13,
        out_specs=(VM,) * 11,
        scratch_shapes=[vm(edges.shape, F32), vm(lines.shape, F32)],
        compiler_params=params(6),
        cost_estimate=cost(10 * n // 8, n),
        name="edge",
    )(wi_pl, fi_pl, wi_row, fi_row, pl_a, pl_b, rw_a, rw_b, xa, xb, ya, yb, sums)
    f_edges, w_edges, (wc_pl, wc_row, payload) = out[:4], out[4:8], out[8:]

    fya, fyb = swap("gy", f_edges[2], f_edges[3])
    fxa, fxb = swap("gx", f_edges[0], f_edges[1])
    got = lax.all_to_all(payload, ("gx", "gy"), 0, 0, tiled=True)

    got, w, f, k = lax.optimization_barrier((got, w, f, k))

    w, f, k, cy, cz, g, g_pl, g_row = pl.pallas_call(
        sweep_kernel,
        out_shape=(full,) * 6 + (edges, lines),
        in_specs=[HBM] * 3 + [VM] * 8,
        out_specs=(VM,) * 8,
        scratch_shapes=[dma((3, planes))],
        compiler_params=params(26),
        cost_estimate=cost(40 * n, 12 * n),
        name="sweep",
    )(k, w, f, *w_edges, *f_edges)

    g_edges = pl.pallas_call(
        mid_kernel,
        out_shape=(edge, edge, line, line),
        in_specs=[VM] * 8,
        out_specs=(VM,) * 4,
        scratch_shapes=[vm(edges.shape, F32), vm(lines.shape, F32)],
        compiler_params=params(4),
        cost_estimate=cost(n // 8, n // 2),
        name="mid",
    )(g_pl, g_row, wc_pl, wc_row, fxa, fxb, fya, fyb)

    gya, gyb = swap("gy", g_edges[2], g_edges[3])
    gxa, gxb = swap("gx", g_edges[0], g_edges[1])

    cells = (nx, ny, cols // F)
    interp = pl.pallas_call(
        functools.partial(coarse_kernel, nx=nx, ny=ny, rows=rows),
        out_shape=sds(3, rows, cols),
        in_specs=[VM],
        out_specs=VM,
        scratch_shapes=[
            vm((4, 2) + cells, F32),
            vm((2,) + cells, F32),
            vm((2, 2) + cells, F32),
        ],
        compiler_params=params(8),
        cost_estimate=cost(20 * n, n),
        name="coarse",
    )(got)

    b_side = sds(planes - 2, STRIP, cols)
    out, body = pl.pallas_call(
        last_kernel,
        out_shape=(full, full),
        in_specs=[VM] * 11,
        out_specs=(HBM, VM),
        scratch_shapes=[vm(full.shape, F32), dma((planes,))],
        compiler_params=params(22),
        cost_estimate=cost(40 * n, 20 * n),
        name="last",
    )(w, f, k, cy, cz, g, interp, *g_edges)

    return pl.pallas_call(
        finish_kernel,
        out_shape=full,
        in_specs=[HBM] + [VM] * 7,
        out_specs=HBM,
        scratch_shapes=[
            vm(edges.shape, F32), vm(lines.shape, F32), vm(lines.shape, F32),
            dma((2,)), dma((2, planes)),
        ],
        input_output_aliases={0: 0},
        compiler_params=params(6),
        cost_estimate=cost(n // 4, 3 * n),
        name="finish",
    )(out, body, wc_pl, wc_row, gxa, gxb, gya, gyb)


def solution(mesh):
    placed = P("gx", "gy", None)
    body = functools.partial(per_device, mesh.shape["gx"], mesh.shape["gy"])
    return jax.shard_map(
        body, mesh=mesh, in_specs=(placed,) * 3, out_specs=placed, check_vma=False
    )
```
